256 devices in a mesh: pol: 2 (over y_lo), row: 4 (over x), col: 32 (over z, y_hi, core).
Axes of the slice: x: 4, y: 4 (y_hi: 2, y_lo: 2; y = y_hi * 2 + y_lo), z: 8, core: 2. Of those that a mesh axis runs over, the one named last changes fastest.
Arguments:
- kernel_half: bfloat16 [16384, 16384], P('row', ('pol', 'col')), may hold values from -0.046875 to 0.046875
- dipole: float32 [3, 16384], P(None, 'row'), may hold values from -6 to 6
- band_energy: float32 [8, 512], P('row'), may hold values from 0 to 4
- core_energy: float32 [4], replicated, may hold values from -2 to 2
- core_index: int32 [32], P('row'), may hold values from 0 to 3
Outputs:
- alphas: float32 [3, 2], replicated
- betas: float32 [3, 2], replicated
- last_vector: float32 [3, 16384], P(None, 'row')
The draws below stay inside these ranges and needn't reach their ends.
All inputs are finite; a program needn't handle non-finite values.
Results may differ from the reference program's by a relative error of at most 0.0026.
Values may be sent and summed in bfloat16 or wider, within the bound.
A program may use at most 64 MiB of HBM per device.

```python
import jax
import jax.numpy as jnp
from jax import lax

KP = 8
BANDS = 512
CORES = 4
POLS = 3
ITERS = 2
M = 16384


def set_ends(drawn, own_key, smallest, largest):
    shape = drawn.shape
    place = [jax.random.randint(jax.random.fold_in(own_key, axis), (), 0, shape[axis]) for axis in range(len(shape))]
    drawn = drawn.at[tuple(place)].set(smallest)
    longest = shape.index(max(shape))
    place[longest] = (place[longest] + 1) % shape[longest]
    return drawn.at[tuple(place)].set(largest)


def level_of(rng, extent, shards, smallest, largest):
    gain = 1.0
    for dim, blocks in shards:
        draws = jax.random.uniform(jax.random.fold_in(jax.random.fold_in(rng, 6), dim), (blocks,), jnp.float32, smallest / len(shards), largest / len(shards))
        gain = gain * jnp.repeat(jnp.exp(draws), extent[dim] // blocks).reshape((-1,) + (1,) * (len(extent) - 1 - dim))
    return gain


def centred(own_key, extent, spread, bound, cuts=(), kind=jnp.bfloat16):
    result = jax.random.normal(own_key, extent, jnp.float32) * spread
    if len(cuts) > 0:
        result = level_of(own_key, extent, cuts, -0.22, 0.18) * result
    return jnp.clip(result, min=-bound, max=bound).astype(kind)


def setup_inputs(seed: int = 0) -> dict:
    keys = jax.random.split(jax.random.key(seed), 6)
    return {
        "kernel_half": centred(keys[0], (M, M), M ** -0.5, 0.046875, ((0, 4), (1, 64))),
        "dipole": centred(keys[1], (POLS, M), 1.0, 6.0, ((1, 4),), jnp.float32),
        "band_energy": jnp.clip(4.0 * jax.random.uniform(keys[2], (KP, BANDS), jnp.float32) ** level_of(keys[2], (KP, BANDS), ((0, 4),), -0.2, 0.2), 0.0, 4.0),
        "core_energy": jnp.clip(jax.random.uniform(keys[3], (CORES,), jnp.float32, -2.0, 2.0), -2.0, 2.0),
        "core_index": set_ends(jax.random.randint(keys[4], (KP * CORES,), 0, CORES), jax.random.fold_in(keys[4], 1), 0, CORES - 1).astype(jnp.int32),
    }


def energies(band_energy, core_energy, core_index):
    one_hot = (core_index[:, None] == jnp.arange(CORES, dtype=jnp.int32)[None, :]).astype(jnp.float32)
    offset = lax.optimization_barrier(jnp.sum(one_hot * core_energy[None, :], axis=1))
    levels = band_energy[:, None, :] - offset.reshape(-1, CORES)[:, :, None]
    return levels.reshape(-1)

def reference(kernel_half, dipole, band_energy, core_energy, core_index):
    energy = energies(band_energy, core_energy, core_index)
    vector = dipole / jnp.sqrt(lax.optimization_barrier(jnp.sum(dipole * dipole, axis=1)))[:, None]
    previous = jnp.zeros_like(vector)
    beta_now = jnp.zeros((POLS,), jnp.float32)
    alpha_list = []
    beta_list = []
    for repeat in range(ITERS):
        vector_bf = vector.astype(jnp.bfloat16)
        row_part = jnp.dot(kernel_half, vector_bf.T, preferred_element_type=jnp.float32).T
        col_part = jnp.dot(vector_bf, kernel_half, preferred_element_type=jnp.float32)
        applied = energy[None, :] * vector + row_part + col_part
        alpha_now = lax.optimization_barrier(jnp.sum(vector * applied, axis=1))
        leftover = applied - alpha_now[:, None] * vector - beta_now[:, None] * previous
        beta_next = jnp.sqrt(lax.optimization_barrier(jnp.sum(leftover * leftover, axis=1)))
        previous = vector
        vector = leftover / beta_next[:, None]
        beta_now = beta_next
        alpha_list.append(alpha_now)
        beta_list.append(beta_next)
    return (jnp.stack(alpha_list, axis=1), jnp.stack(beta_list, axis=1), vector)
```

```python
import functools

import jax
import jax.numpy as jnp
from jax import lax
from jax.experimental import pallas as pl
from jax.experimental.pallas import tpu as pltpu
from jax.sharding import PartitionSpec as P

F32 = jnp.float32
BF = jnp.bfloat16
MESH = pl.DeviceIdType.MESH
CORES = 4
LANES = 128
ROWS = 16
QUARTERS = 4
POLS = 3


def iota(width, dim=0):
    return lax.broadcasted_iota(jnp.int32, (ROWS, width), dim)


def spread(parts):
    width = parts[0].shape[1]
    row = iota(width)
    a, b, c = (jnp.broadcast_to(t, (ROWS, width)) for t in parts)
    return jnp.where(row < 4, a, jnp.where(row < 8, b, jnp.where(row < 12, c, 0.0)))


def over_quarters(x):
    return [jnp.sum(x[4 * q : 4 * q + 4], axis=0, keepdims=True) for q in range(POLS)]


def placed(parts, first, rows):
    row = lax.broadcasted_iota(jnp.int32, (rows, LANES), 0)
    out = jnp.zeros((rows, LANES), F32)
    for q in range(POLS):
        out = jnp.where(row == first + q, jnp.broadcast_to(parts[q], (rows, LANES)), out)
    return out


def halves(x):
    high = x.astype(BF)
    return jnp.concatenate([high, (x - high.astype(F32)).astype(BF)], axis=0)


def joined(x):
    return x[:ROWS] + x[ROWS:]


def kernel(
    sizes,
    w_hbm, dip_hbm, band_hbm, core_hbm, index_hbm,
    alpha_ref, beta_ref, last_ref,
    w, dip, band, core, index,
    uc0, u, en, ub,
    send1, recv1, sendc, recvc, send2, recv2, send3, recv3, recvt, sendx, recvx,
    load_sem, core_sem, s0, r0, s1, r1, sc, rc, s2, r2, s3, r3, st, rt, sx, rx,
):
    nx, nz, zl_count = sizes
    zh_count = nz // zl_count
    p = lax.axis_index("pol")
    x = lax.axis_index("row")
    col = lax.axis_index("col")
    z = col // 4
    h = (col // 2) % 2
    k = col % 2
    g_me = h * 4 + k * 2 + p
    zl = z % zl_count
    home = p * zh_count + z // zl_count
    is_home = x == home
    keeper = (z // zl_count) == (x % zh_count)
    p_keep = x // zh_count

    def dev(pp, xx, zz, hh, kk):
        return (pp, xx, zz * 4 + hh * 2 + kk)

    loads = [
        pltpu.make_async_copy(dip_hbm, dip, load_sem.at[0]),
        pltpu.make_async_copy(band_hbm, band, load_sem.at[1]),
        pltpu.make_async_copy(core_hbm, core, core_sem.at[0]),
        pltpu.make_async_copy(index_hbm, index, core_sem.at[1]),
    ]
    for c in loads:
        c.start()
    big = w.shape[0] // 4
    w_loads = [
        pltpu.make_async_copy(
            w_hbm.at[pl.ds(i * big, big)], w.at[pl.ds(i * big, big)], load_sem.at[2 + i]
        )
        for i in range(4)
    ]
    for c in w_loads:
        c.start()

    barrier = pltpu.get_barrier_semaphore()
    greeted = []
    for d in range(1, nz):
        greeted.append(dev(p, x, (z + d) % nz, h, k))
    for dx in range(1, nx):
        for dp in range(2):
            greeted.append(dev((p + dp) % 2, (x + dx) % nx, z, h, k))
    for j in range(1, 8):
        greeted.append(dev((p + j % 2) % 2, x, z, (h + j // 4) % 2, (k + (j // 2) % 2) % 2))
    for d in greeted:
        pl.semaphore_signal(barrier, inc=1, device_id=d, device_id_type=MESH)

    row = iota(LANES)
    row2 = iota(2 * LANES)
    ends = []

    def start(make, condition=None):
        ends.append((make, condition))
        if condition is None:
            make().start()
        else:
            pl.when(condition)(lambda: make().start())

    def finish():
        for make, condition in ends:
            if condition is None:
                make().wait_send()
            else:
                pl.when(condition)(lambda make=make: make().wait_send())


    for c in loads:
        c.wait()
    for g in range(8):
        u[0, g] = jnp.zeros((ROWS, LANES), F32)
        for q in range(POLS):
            for t in range(QUARTERS):
                at = (t * 8 + g) * LANES
                u[0, g, 4 * q + t : 4 * q + t + 1, :] = dip[q : q + 1, at : at + LANES]
    offsets = []
    for i in range(2 * CORES):
        level = index[i]
        off = jnp.float32(0.0)
        for j in range(CORES):
            off = jnp.where(level == j, core[j], off)
        offsets.append(off)
    for g in range(8):
        at = (g % 4) * LANES
        low = jnp.broadcast_to(band[0:1, at : at + LANES], (ROWS, LANES))
        high = jnp.broadcast_to(band[1:2, at : at + LANES], (ROWS, LANES))
        value = jnp.zeros((ROWS, LANES), F32)
        for t in range(QUARTERS):
            level = (low if t < 2 else high) - offsets[(t // 2) * 4 + (t % 2) * 2 + g // 4]
            value = jnp.where(row % 4 == t, level, value)
        en[g] = value

    pl.semaphore_wait(barrier, len(greeted))

    own_at = pl.multiple_of((zl * 4 + h * 2 + k) * 2 * LANES, 2 * LANES)

    def first_copy(dx):
        return pltpu.make_async_remote_copy(
            src_ref=dip.at[:, pl.ds(own_at, 2 * LANES)],
            dst_ref=uc0,
            send_sem=s0.at[dx - 1],
            recv_sem=r0.at[0],
            device_id=dev(p, (x + dx) % nx, z, h, k),
            device_id_type=MESH,
        )

    for dx in range(1, nx):
        start(functools.partial(first_copy, dx), is_home)

    @pl.when(is_home)
    def _():
        uc0[...] = dip[:, pl.ds(own_at, 2 * LANES)]

    for c in w_loads:
        c.wait()

    def tiles_of(hh, kk, t):
        return pl.ds(pl.multiple_of((t * 4 + hh * 2 + kk) * 2 * LANES, 2 * LANES), 2 * LANES)

    coefficients = []
    column = None
    for step in range(2):
        for g in range(8):
            ub[:, g * LANES : (g + 1) * LANES] = halves(u[step, g])
        block = 8 * LANES
        sums = jnp.zeros((ROWS, 2 * LANES), F32)
        for t in range(QUARTERS):
            part = joined(jnp.dot(ub[...], w[t * block : (t + 1) * block, :], preferred_element_type=F32))
            sums = jnp.where(row2 % 4 == t, part, sums)
        col_part = over_quarters(sums)
        col_rows = jnp.where(row2 % 4 == zl, spread(col_part), 0.0)
        for half in range(2):
            sendc[step, half] = col_rows[:, half * LANES : (half + 1) * LANES]

        def col_copy(half, step=step):
            return pltpu.make_async_remote_copy(
                src_ref=sendc.at[step, half],
                dst_ref=recvc.at[step, x],
                send_sem=sc.at[step, half],
                recv_sem=rc.at[step, x],
                device_id=dev(half, home, z, h, k),
                device_id_type=MESH,
            )

        for half in range(2):
            mine = jnp.logical_and(is_home, p == half)

            @pl.when(mine)
            def _(half=half, step=step):
                recvc[step, x] = sendc[step, half]

            start(functools.partial(col_copy, half), jnp.logical_not(mine))

        squares = jnp.zeros((ROWS, LANES), F32)
        weighted = jnp.zeros((ROWS, LANES), F32)
        for g in range(8):
            sq = u[step, g] * u[step, g]
            squares += sq
            weighted += en[g] * sq
        own_sums = placed(over_quarters(squares), 0, 8) + placed(over_quarters(weighted), 4, 8)

        if step == 0:

            @pl.when(jnp.logical_not(is_home))
            def _():
                first_copy(1).wait_recv()

            column = [uc0[q : q + 1, :] for q in range(POLS)]
        else:
            @pl.when(jnp.logical_not(is_home))
            def _():
                for half in range(2):
                    tile_copy(1, half).wait_recv()

            @pl.when(is_home)
            def _():
                for half in range(2):
                    recvt[half] = recv3[0, h * 4 + k * 2 + half]

            both = jnp.concatenate([recvt[0], recvt[1]], axis=1)
            arrived = over_quarters(jnp.where(row2 % 4 == zl, both, 0.0))
            alpha = coefficients[0][0]
            column = [arrived[q] - alpha[q][:, :1] * column[q] for q in range(POLS)]
        twice = []
        for q in range(POLS):
            line = 2.0 * col_part[q] * column[q]
            twice.append(line[:, :LANES] + line[:, LANES:])
        sum_rows = placed(twice, 12, ROWS)
        left = halves(spread(column))

        def row_copy(j, pp, step=step):
            jh, jk = 1 - j // 2, 1 - j % 2
            return pltpu.make_async_remote_copy(
                src_ref=send1.at[step, j, pp],
                dst_ref=recv1.at[step, g_me],
                send_sem=s1.at[step, j, pp],
                recv_sem=r1.at[step, g_me],
                device_id=dev(pp, x, z, (h + jh) % 2, (k + jk) % 2),
                device_id_type=MESH,
            )

        for j in range(4):
            jh, jk = 1 - j // 2, 1 - j % 2
            hh, kk = (h + jh) % 2, (k + jk) % 2
            lines = jnp.zeros((ROWS, 2 * LANES), F32)
            for t in range(QUARTERS):
                part = joined(lax.dot_general(
                    left, w[tiles_of(hh, kk, t), :], (((1,), (1,)), ((), ())),
                    preferred_element_type=F32,
                ))
                lines = jnp.where(row2 % 4 == t, part, lines)
            for pp in range(2):
                send1[step, j, pp] = lines[:, pp * LANES : (pp + 1) * LANES] + sum_rows
            if j < 3:
                for pp in range(2):
                    start(functools.partial(row_copy, j, pp))
            else:
                start(functools.partial(row_copy, j, 1 - p))
                recv1[step, g_me] = send1[step, j, p]

        for j in range(1, 8):
            g = (h + j // 4) % 2 * 4 + (k + (j // 2) % 2) % 2 * 2 + (p + j % 2) % 2
            pltpu.make_async_remote_copy(
                src_ref=send1.at[step, 0, 0], dst_ref=recv1.at[step, g], send_sem=s1.at[step, 0, 0],
                recv_sem=r1.at[step, g], device_id=dev(p, x, z, h, k), device_id_type=MESH,
            ).wait_recv()
        total = recv1[step, 0]
        for g in range(1, 8):
            total += recv1[step, g]
        send2[step] = total

        @pl.when(keeper)
        def _(step=step):
            for xx in range(nx):
                @pl.when(jnp.logical_not(jnp.logical_and(x == xx, p == p_keep)))
                def _(xx=xx):
                    pltpu.make_async_remote_copy(
                        src_ref=sendc.at[step, 0], dst_ref=recvc.at[step, xx], send_sem=sc.at[step, 0],
                        recv_sem=rc.at[step, xx], device_id=dev(p, x, z, h, k), device_id_type=MESH,
                    ).wait_recv()
            cols = recvc[step, 0]
            for xx in range(1, nx):
                cols += recvc[step, xx]
            send2[step] = send2[step] + cols

        def z_copy(d, step=step):
            return pltpu.make_async_remote_copy(
                src_ref=send2.at[step], dst_ref=recv2.at[step, z], send_sem=s2.at[step, d - 1],
                recv_sem=r2.at[step, z], device_id=dev(p, x, (z + d) % nz, h, k), device_id_type=MESH,
            )

        for d in sorted(range(1, nz), key=lambda d: -min(d, nz - d)):
            start(functools.partial(z_copy, d))
        recv2[step, z] = send2[step]
        for d in range(1, nz):
            zz = (z + d) % nz
            pltpu.make_async_remote_copy(
                src_ref=send2.at[step], dst_ref=recv2.at[step, zz], send_sem=s2.at[step, d - 1],
                recv_sem=r2.at[step, zz], device_id=dev(p, x, z, h, k), device_id_type=MESH,
            ).wait_recv()
        total = recv2[step, 0]
        for zz in range(1, nz):
            total += recv2[step, zz]

        low = lax.broadcasted_iota(jnp.int32, (8, LANES), 0)
        sendx[step] = jnp.where(low >= 4, total[8:], 0.0) + own_sums

        def x_copy(dx, at):
            return pltpu.make_async_remote_copy(
                src_ref=sendx.at[at], dst_ref=recvx.at[at, x], send_sem=sx.at[at, dx - 1],
                recv_sem=rx.at[at, x], device_id=dev(p, (x + dx) % nx, z, h, k), device_id_type=MESH,
            )

        def x_wait(dx, at):
            xx = (x + dx) % nx
            pltpu.make_async_remote_copy(
                src_ref=sendx.at[at], dst_ref=recvx.at[at, xx], send_sem=sx.at[at, dx - 1],
                recv_sem=rx.at[at, xx], device_id=dev(p, x, z, h, k), device_id_type=MESH,
            ).wait_recv()

        for dx in range(1, nx):
            start(functools.partial(x_copy, dx, step))
        recvx[step, x] = sendx[step]
        send3[step] = total + en[g_me] * u[step, g_me]

        def tile_copy(dx, half):
            return pltpu.make_async_remote_copy(
                src_ref=send3.at[0], dst_ref=recvt.at[half], send_sem=st.at[dx - 1],
                recv_sem=rt.at[half], device_id=dev(p_keep, (x + dx) % nx, z, h, k), device_id_type=MESH,
            )

        if step == 0:
            for dx in range(1, nx):
                start(functools.partial(tile_copy, dx, p), keeper)

        def chunk_copy(j, step=step):
            return pltpu.make_async_remote_copy(
                src_ref=send3.at[step], dst_ref=recv3.at[step, g_me], send_sem=s3.at[step, j - 1],
                recv_sem=r3.at[step, g_me],
                device_id=dev((p + j % 2) % 2, x, z, (h + j // 4) % 2, (k + (j // 2) % 2) % 2),
                device_id_type=MESH,
            )

        for j in range(7, 0, -1):
            start(functools.partial(chunk_copy, j))
        recv3[step, g_me] = send3[step]

        for dx in range(1, nx):
            x_wait(dx, step)
        sums = recvx[step, 0]
        for xx in range(1, nx):
            sums += recvx[step, xx]
        sums = jnp.broadcast_to(jnp.sum(sums, axis=1, keepdims=True), (8, LANES))
        norms = [sums[q : q + 1] for q in range(POLS)]
        alpha = [sums[4 + q : 5 + q] / norms[q] for q in range(POLS)]
        coefficients.append((alpha, norms))

        for j in range(1, 8):
            g = (h + j // 4) % 2 * 4 + (k + (j // 2) % 2) % 2 * 2 + (p + j % 2) % 2
            pltpu.make_async_remote_copy(
                src_ref=send3.at[step], dst_ref=recv3.at[step, g], send_sem=s3.at[step, j - 1],
                recv_sem=r3.at[step, g], device_id=dev(p, x, z, h, k), device_id_type=MESH,
            ).wait_recv()
        factor = spread(alpha)
        if step == 0:
            for g in range(8):
                u[1, g] = recv3[0, g] - factor * u[0, g]

    (alpha0, norm0), (alpha1, norm1) = coefficients
    ratio = [norm1[q] / norm0[q] for q in range(POLS)]
    back = spread(ratio)
    squares = jnp.zeros((ROWS, LANES), F32)
    last = []
    for g in range(8):
        value = recv3[1, g] - factor * u[1, g] - back * u[0, g]
        squares += value * value
        last.append(value)
    sendx[2] = placed(over_quarters(squares), 0, 8)
    for dx in range(1, nx):
        start(functools.partial(x_copy, dx, 2))
    recvx[2, x] = sendx[2]
    for dx in range(1, nx):
        x_wait(dx, 2)
    sums = recvx[2, 0]
    for xx in range(1, nx):
        sums += recvx[2, xx]
    sums = jnp.broadcast_to(jnp.sum(sums, axis=1, keepdims=True), (8, LANES))
    norm2 = [sums[q : q + 1] for q in range(POLS)]
    inverse = spread([1.0 / jnp.sqrt(t) for t in norm2])
    for g in range(8):
        value = last[g] * inverse
        for q in range(POLS):
            for t in range(QUARTERS):
                at = (t * 8 + g) * LANES
                last_ref[q : q + 1, at : at + LANES] = value[4 * q + t : 4 * q + t + 1, :]
    for q in range(POLS):
        alpha_ref[q : q + 1, 0:1] = alpha0[q][:, :1]
        alpha_ref[q : q + 1, 1:2] = alpha1[q][:, :1]
        beta_ref[q : q + 1, 0:1] = jnp.sqrt(ratio[q])[:, :1]
        beta_ref[q : q + 1, 1:2] = jnp.sqrt(norm2[q] / norm1[q])[:, :1]

    finish()


def lanczos(sizes, kernel_half, dipole, band_energy, core_energy, core_index):
    nx, nz, _ = sizes
    rows, cols = kernel_half.shape
    dma = pltpu.SemaphoreType.DMA
    chunk = (ROWS, LANES)
    return pl.pallas_call(
        functools.partial(kernel, sizes),
        out_shape=(
            jax.ShapeDtypeStruct((POLS, 2), F32),
            jax.ShapeDtypeStruct((POLS, 2), F32),
            jax.ShapeDtypeStruct(dipole.shape, F32),
        ),
        in_specs=[pl.BlockSpec(memory_space=pl.ANY)] * 5,
        out_specs=[pl.BlockSpec(memory_space=pltpu.VMEM)] * 3,
        scratch_shapes=[
            pltpu.VMEM((rows, cols), BF),
            pltpu.VMEM(dipole.shape, F32),
            pltpu.VMEM(band_energy.shape, F32),
            pltpu.SMEM(core_energy.shape, F32),
            pltpu.SMEM(core_index.shape, jnp.int32),
            pltpu.VMEM((POLS, cols), F32),
            pltpu.VMEM((2, 8, *chunk), F32),
            pltpu.VMEM((8, *chunk), F32),
            pltpu.VMEM((2 * ROWS, 8 * LANES), BF),
            pltpu.VMEM((2, 4, 2, *chunk), F32),
            pltpu.VMEM((2, 8, *chunk), F32),
            pltpu.VMEM((2, 2, *chunk), F32),
            pltpu.VMEM((2, nx, *chunk), F32),
            pltpu.VMEM((2, *chunk), F32),
            pltpu.VMEM((2, nz, *chunk), F32),
            pltpu.VMEM((2, *chunk), F32),
            pltpu.VMEM((2, 8, *chunk), F32),
            pltpu.VMEM((2, *chunk), F32),
            pltpu.VMEM((3, 8, LANES), F32),
            pltpu.VMEM((3, nx, 8, LANES), F32),
            dma((6,)), dma((2,)),
            dma((nx - 1,)), dma((1,)),
            dma((2, 4, 2)), dma((2, 8)),
            dma((2, 2)), dma((2, nx)),
            dma((2, nz - 1)), dma((2, nz)),
            dma((2, 7)), dma((2, 8)),
            dma((nx - 1,)), dma((2,)),
            dma((3, nx - 1)), dma((3, nx)),
        ],
        compiler_params=pltpu.CompilerParams(collective_id=0, has_side_effects=True),
    )(kernel_half, dipole, band_energy, core_energy, core_index)


def solution(mesh):
    nx, np_, nz = mesh.shape["row"], mesh.shape["pol"], mesh.shape["col"] // 4
    sizes = (nx, nz, nz * np_ // nx)
    in_specs = (P("row", ("pol", "col")), P(None, "row"), P("row", None), P(), P("row"))
    out_specs = (P(), P(), P(None, "row"))
    return jax.shard_map(
        functools.partial(lanczos, sizes), mesh=mesh, in_specs=in_specs, out_specs=out_specs, check_vma=False
    )
```

```python
import functools

import jax
import jax.numpy as jnp
from jax import lax
from jax.experimental import pallas as pl
from jax.experimental.pallas import tpu as pltpu
from jax.sharding import PartitionSpec as P

F32 = jnp.float32
BF = jnp.bfloat16
MESH = pl.DeviceIdType.MESH
CORES = 4
LANES = 128
POLS = 3
LINES = 8
ROWS = POLS * LINES


def spread(parts):
    return jnp.concatenate([jnp.broadcast_to(t, (LINES, t.shape[1])) for t in parts], axis=0)


def over_lines(x):
    return [jnp.sum(x[LINES * q : LINES * (q + 1)], axis=0, keepdims=True) for q in range(POLS)]


def placed(parts, first=0):
    row = lax.broadcasted_iota(jnp.int32, (8, LANES), 0)
    out = jnp.zeros((8, LANES), F32)
    for q, part in enumerate(parts):
        out = jnp.where(row == first + q, jnp.broadcast_to(part, (8, LANES)), out)
    return out


def two_terms(x):
    high = x.astype(BF).astype(F32)
    return jnp.concatenate([high, x - high], axis=0).astype(BF)


def joined(x):
    return x[:ROWS] + x[ROWS:]


def kernel(
    sizes,
    w_hbm, dip_hbm, band_hbm, core_hbm, index_hbm,
    alpha_ref, beta_ref, last_ref,
    w, dip, band, core, index,
    uc0, u, en,
    send1, recv1, sendc, recvc, send2, recv2, send3, recv3, sendt, recvt, sendx, recvx, sendn, recvn,
    load_sem, core_sem, s0, r0, s1, r1, sc, rc, s2, r2, s3, r3, st, rt, sx, rx, sn, rn,
):
    nx, nz, zl_count = sizes
    zh_count = nz // zl_count
    p = lax.axis_index("pol")
    x = lax.axis_index("row")
    col = lax.axis_index("col")
    z = col // 4
    h = (col // 2) % 2
    k = col % 2
    y = h * 2 + p
    zl = z % zl_count
    home = p * zh_count + z // zl_count
    is_home = x == home
    away = jnp.logical_not(is_home)
    owner = k == 1
    keeper = (z // zl_count) == (x % zh_count)
    p_keep = x // zh_count

    def dev(pp, xx, zz, hh, kk):
        return (pp, xx, zz * 4 + hh * 2 + kk)

    barrier = pltpu.get_barrier_semaphore()

    def greet(d):
        pl.semaphore_signal(barrier, inc=1, device_id=d, device_id_type=MESH)

    beside = [(dx, j) for dx in (2, 1, 3, 0) for j in range(4)]
    for dx, j in beside:
        hh, pp = (h + j // 2) % 2, (p + j % 2) % 2
        if (dx, j) == (0, 0):
            greet(dev(p, x, z, h, 1 - k))
        else:
            greet(dev(pp, (x + dx) % nx, z, hh, 1))

    @pl.when(owner)
    def _():
        for d in sorted(range(1, nz), key=lambda d: -min(d, nz - d)):
            greet(dev(p, x, (z + d) % nz, h, 1))
        for dx, j in beside:
            if (dx, j) != (0, 0):
                greet(dev((p + j % 2) % 2, (x + dx) % nx, z, (h + j // 2) % 2, 0))

    loads = [
        pltpu.make_async_copy(dip_hbm, dip, load_sem.at[0]),
        pltpu.make_async_copy(band_hbm, band, load_sem.at[1]),
        pltpu.make_async_copy(core_hbm, core, core_sem.at[0]),
        pltpu.make_async_copy(index_hbm, index, core_sem.at[1]),
    ]
    for c in loads:
        c.start()
    big = w.shape[0] // 4
    w_loads = [
        pltpu.make_async_copy(
            w_hbm.at[pl.ds(i * big, big)], w.at[pl.ds(i * big, big)], load_sem.at[2 + i]
        )
        for i in range(4)
    ]
    for c in w_loads:
        c.start()

    ends = []

    def start(make, condition=None, within=None):
        if condition is None:
            make().start()
        else:
            pl.when(condition)(lambda: make().start())
        ends.append((make, condition, within))

    def finish():
        for make, condition, within in ends:
            if condition is None and within is None:
                make().wait_send()
            elif condition is None or within is None:
                pl.when(within if condition is None else condition)(lambda make=make: make().wait_send())
            else:
                pl.when(jnp.logical_and(condition, within))(lambda make=make: make().wait_send())

    def send(src, dst, send_sem, recv_sem, device):
        return pltpu.make_async_remote_copy(
            src_ref=src, dst_ref=dst, send_sem=send_sem, recv_sem=recv_sem, device_id=device,
            device_id_type=MESH,
        )

    me = dev(p, x, z, h, k)

    def arrived(dst, recv_sem, spare_sem):
        send(dst, dst, spare_sem, recv_sem, me).wait_recv()

    for c in loads:
        c.wait()
    for c in range(4):
        for q in range(POLS):
            for t in range(LINES):
                at = ((t // 2) * 8 + (c // 2) * 4 + (t % 2) * 2 + c % 2) * LANES
                u[0, c, LINES * q + t : LINES * q + t + 1, :] = dip[q : q + 1, at : at + LANES]
    offsets = []
    for i in range(2 * CORES):
        level = index[i]
        off = jnp.float32(0.0)
        for j in range(CORES):
            off = jnp.where(level == j, core[j], off)
        offsets.append(off)
    row8 = lax.broadcasted_iota(jnp.int32, (8, LANES), 0)
    for c in range(4):
        value = jnp.zeros((8, LANES), F32)
        for t in range(LINES):
            line = (t // 2) * 8 + (c // 2) * 4 + (t % 2) * 2 + c % 2
            at = (line % 4) * LANES
            level = band[line // 16 : line // 16 + 1, at : at + LANES] - offsets[line // 4]
            value = jnp.where(row8 == t, jnp.broadcast_to(level, (8, LANES)), value)
        en[c] = value

    pl.semaphore_wait(barrier, jnp.where(owner, 2 * len(beside) - 1 + nz - 1, len(beside)))

    def own_lines(kk):
        return pl.ds(pl.multiple_of((zl * 4 + h * 2 + kk) * 2 * LANES, 2 * LANES), 2 * LANES)

    def first_copy(dx, kk):
        return send(
            dip.at[:, own_lines(kk)], uc0, s0.at[dx - 1, kk], r0.at[0], dev(p, (x + dx) % nx, z, h, kk)
        )

    for dx in (2, 1, 3):
        for kk in range(2):
            start(functools.partial(first_copy, dx, kk), jnp.logical_and(is_home, owner))

    @pl.when(is_home)
    def _():
        uc0[...] = dip[:, own_lines(k)]

    for c in w_loads:
        c.wait()

    row_mod = lax.broadcasted_iota(jnp.int32, (ROWS, 2 * LANES), 0) % LINES

    def line_rows(hh, pp, t):
        line = (t // 2) * 8 + hh * 4 + (t % 2) * 2 + pp
        return pl.ds(pl.multiple_of(line * LANES, LANES), LANES)

    def columns_of(value, hh, pp):
        left = two_terms(value)
        out = jnp.zeros((ROWS, 2 * LANES), F32)
        for t in range(LINES):
            part = joined(jnp.dot(left, w[line_rows(hh, pp, t), :], preferred_element_type=F32))
            out = jnp.where(row_mod == t, part, out)
        return out

    near = [(0, 0), (0, 1), (1, 1), (1, 0)]

    alpha = ratio = column = col_first = norms = None
    for step in range(2):
        rows = ROWS + 8 if step == 0 else ROWS
        sums = jnp.zeros((ROWS, 2 * LANES), F32)
        if step == 0:
            for c in range(4):
                sums += columns_of(u[0, c], c // 2, c % 2)
            col_part = over_lines(sums)
            col_first = col_part
        else:
            for jh, jp in near:
                hh, pp = (h + jh) % 2, (p + jp) % 2
                c = hh * 2 + pp
                hear = functools.partial(arrived, recv3.at[0, c], r3.at[0, c], s3.at[0, 0])
                if (jh, jp) == (0, 0):
                    pl.when(jnp.logical_not(owner))(hear)
                else:
                    hear()
                sums += columns_of(recv3[0, c], hh, pp)
            for xx in range(nx):
                pl.when(jnp.logical_not(jnp.logical_and(owner, x == xx)))(
                    functools.partial(arrived, recvx.at[0, xx], rx.at[0, xx], sx.at[0, 0])
                )
            whole = recvx[0, 0]
            for xx in range(1, nx):
                whole += recvx[0, xx]
            whole = jnp.broadcast_to(jnp.sum(whole, axis=1, keepdims=True), (8, LANES))
            norms = [whole[q : q + 1] for q in range(POLS)]
            alpha = [whole[4 + q : 5 + q] / norms[q] for q in range(POLS)]
            col_part = over_lines(sums)
            col_part = [col_part[q] - alpha[q][:, :1] * col_first[q] for q in range(POLS)]
        for half in range(2):
            sendc[step, half] = placed([t[:, half * LANES : (half + 1) * LANES] for t in col_part])

        def col_copy(half, step=step):
            return send(
                sendc.at[step, half], recvc.at[step, x, k], sc.at[step, half], rc.at[step, x, k],
                dev(half, home, z, h, 1),
            )

        for half in range(2):
            mine = jnp.logical_and(owner, jnp.logical_and(is_home, p == half))

            @pl.when(mine)
            def _(half=half, step=step):
                recvc[step, x, k] = sendc[step, half]

            start(functools.partial(col_copy, half), jnp.logical_not(mine))

        if step == 0:
            pl.when(away)(functools.partial(arrived, uc0, r0.at[0], s0.at[0, 0]))
            column = [uc0[q : q + 1, :] for q in range(POLS)]
        else:

            @pl.when(is_home)
            def _():
                for half in range(2):
                    value = recv3[0, h * 2 + half]
                    mask = lax.broadcasted_iota(jnp.int32, (ROWS, LANES), 0) % LINES == zl * 2 + k
                    recvt[half] = placed(over_lines(jnp.where(mask, value, 0.0)))

            for half in range(2):
                pl.when(away)(functools.partial(arrived, recvt.at[half], rt.at[half], st.at[0, 0]))
            got = jnp.concatenate([recvt[0], recvt[1]], axis=1)
            got = jnp.where(away, jnp.where(k == 1, pltpu.roll(got, 4, 0), got), got)
            column = [got[q : q + 1] - alpha[q][:, :1] * column[q] for q in range(POLS)]
        if step == 0:
            twice = []
            for q in range(POLS):
                line = 2.0 * col_part[q] * column[q]
                twice.append(line[:, :LANES] + line[:, LANES:])
            sum_rows = placed(twice)
        left = two_terms(spread(column))

        def row_copy(j, step=step, rows=rows):
            jh, jp = near[j]
            return send(
                send1.at[step, j, pl.ds(0, rows)], recv1.at[step, y * 2 + k, pl.ds(0, rows)],
                s1.at[step, j], r1.at[step, y * 2 + k], dev((p + jp) % 2, x, z, (h + jh) % 2, 1),
            )

        for j in (3, 2, 1, 0):
            jh, jp = near[j]
            hh, pp = (h + jh) % 2, (p + jp) % 2
            lines = jnp.zeros((ROWS, LANES), F32)
            for t in range(LINES):
                part = joined(
                    lax.dot_general(
                        left, w[line_rows(hh, pp, t), :], (((1,), (1,)), ((), ())),
                        preferred_element_type=F32,
                    )
                )
                lines = jnp.where(row_mod[:, :LANES] == t, part, lines)
            send1[step, j, :ROWS] = lines
            if step == 0:
                send1[step, j, ROWS:] = sum_rows
            start(functools.partial(row_copy, j), None if j else jnp.logical_not(owner))

        if step == 1:
            factor = spread(alpha)
            for c in range(4):
                u[1, c] = recv3[0, c] - factor * u[0, c]
        squares = jnp.zeros((ROWS, LANES), F32)
        weighted = jnp.zeros((ROWS, LANES), F32)
        for c in range(4):
            sq = u[step, c] * u[step, c]
            squares += sq
            weighted += jnp.concatenate([en[c]] * POLS, axis=0) * sq
        own_sums = placed(over_lines(squares))

        def x_copy(dx, kk, at):
            return send(
                sendx.at[at], recvx.at[at, x], sx.at[at, (dx - 1) * 2 + kk if dx else 6], rx.at[at, x],
                dev(p, (x + dx) % nx, z, h, kk),
            )

        def share(at):
            for dx in (2, 1, 3):
                for kk in range(2):
                    start(functools.partial(x_copy, dx, kk, at), None, owner)
            start(functools.partial(x_copy, 0, 0, at), None, owner)
            recvx[at, x] = sendx[at]

        if step == 0:
            own_sums += placed(over_lines(weighted), 4)

        @pl.when(owner)
        def _(step=step, rows=rows, own_sums=own_sums):
            if step == 1:
                sendx[1] = own_sums
                share(1)
            recv1[step, y * 2 + k, pl.ds(0, rows)] = send1[step, 0, pl.ds(0, rows)]
            for jh, jp in near:
                hh, pp = (h + jh) % 2, (p + jp) % 2
                for kk in range(2):
                    if (jh, jp, kk) != (0, 0, 1):
                        g = (hh * 2 + pp) * 2 + kk
                        arrived(recv1.at[step, g, pl.ds(0, rows)], r1.at[step, g], s1.at[step, 0])
            total = recv1[step, 0, pl.ds(0, rows)]
            for g in range(1, 8):
                total += recv1[step, g, pl.ds(0, rows)]
            send2[step, pl.ds(0, rows)] = total

            @pl.when(keeper)
            def _():
                for kk in range(2):
                    for xx in range(nx):
                        hear = functools.partial(
                            arrived, recvc.at[step, xx, kk], rc.at[step, xx, kk], sc.at[step, 0]
                        )
                        if kk == 0:
                            hear()
                        else:
                            pl.when(jnp.logical_not(jnp.logical_and(x == xx, p == p_keep)))(hear)
                    cols = recvc[step, 0, kk]
                    for xx in range(1, nx):
                        cols += recvc[step, xx, kk]
                    for q in range(POLS):
                        at = pl.ds(LINES * q, LINES)
                        line = jnp.broadcast_to(cols[q : q + 1], (8, LANES))
                        send2[step, at] = send2[step, at] + jnp.where(row8 == zl * 2 + kk, line, 0.0)

            def z_copy(d):
                return send(
                    send2.at[step, pl.ds(0, rows)], recv2.at[step, z, pl.ds(0, rows)], s2.at[step, d - 1],
                    r2.at[step, z], dev(p, x, (z + d) % nz, h, 1),
                )

            for d in sorted(range(1, nz), key=lambda d: -min(d, nz - d)):
                start(functools.partial(z_copy, d), None, owner)
            recv2[step, z, pl.ds(0, rows)] = send2[step, pl.ds(0, rows)]
            if step == 1:
                for dx in range(1, nx):
                    xx = (x + dx) % nx
                    arrived(recvx.at[1, xx], rx.at[1, xx], sx.at[1, 0])
            for d in range(1, nz):
                zz = (z + d) % nz
                arrived(recv2.at[step, zz, pl.ds(0, rows)], r2.at[step, zz], s2.at[step, 0])
            total = recv2[step, 0, pl.ds(0, rows)]
            for zz in range(1, nz):
                total += recv2[step, zz, pl.ds(0, rows)]
            value = total[:ROWS] + jnp.concatenate([en[y]] * POLS, axis=0) * u[step, y]

            if step == 0:
                sendx[0] = jnp.concatenate([total[ROWS + 4 :], total[ROWS : ROWS + 4]], axis=0) + own_sums
                share(0)
                send3[0] = value
                mod = lax.broadcasted_iota(jnp.int32, (ROWS, LANES), 0) % LINES
                tile = jnp.zeros((8, LANES), F32)
                for kk in range(2):
                    tile += placed(over_lines(jnp.where(mod == zl * 2 + kk, value, 0.0)), 4 * kk)
                sendt[...] = tile

                def tile_copy(dx, kk):
                    return send(
                        sendt, recvt.at[p], st.at[dx - 1, kk], rt.at[p],
                        dev(p_keep, (x + dx) % nx, z, h, kk),
                    )

                for dx in (2, 1, 3):
                    for kk in range(2):
                        start(functools.partial(tile_copy, dx, kk), keeper, owner)
            else:
                w1 = value - spread(alpha) * u[1, y] - spread(ratio_of(1)) * u[0, y]
                sendn[...] = placed(over_lines(w1 * w1)) + placed(over_lines(w1 * u[1, y]), 4)

                def sums_copy(dx, j, kk):
                    jh, jp = near[j]
                    return send(
                        sendn, recvn.at[x, y], sn.at[dx, j, kk], rn.at[x, y],
                        dev((p + jp) % 2, (x + dx) % nx, z, (h + jh) % 2, kk),
                    )

                for dx in (2, 1, 3, 0):
                    for j in (3, 2, 1, 0):
                        for kk in range(2):
                            if (dx, j, kk) != (0, 0, 1):
                                start(functools.partial(sums_copy, dx, j, kk), None, owner)
                recvn[x, y] = sendn[...]
                send3[1] = w1

            def chunk_copy(j, kk):
                jh, jp = near[j]
                return send(
                    send3.at[step], recv3.at[step, y], s3.at[step, j * 2 + kk], r3.at[step, y],
                    dev((p + jp) % 2, x, z, (h + jh) % 2, kk),
                )

            for j in (3, 2, 1, 0):
                for kk in range(2):
                    if (j, kk) != (0, 1):
                        start(functools.partial(chunk_copy, j, kk), None, owner)
            recv3[step, y] = send3[step]

        def ratio_of(at):
            whole = recvx[at, 0]
            for xx in range(1, nx):
                whole += recvx[at, xx]
            whole = jnp.broadcast_to(jnp.sum(whole, axis=1, keepdims=True), (8, LANES))
            return [whole[q : q + 1] / norms[q] for q in range(POLS)]

    @pl.when(jnp.logical_not(owner))
    def _():
        for xx in range(nx):
            arrived(recvx.at[1, xx], rx.at[1, xx], sx.at[1, 0])

    ratio = ratio_of(1)
    norm1 = [ratio[q] * norms[q] for q in range(POLS)]
    for xx in range(nx):
        for c in range(4):
            pl.when(jnp.logical_not(jnp.logical_and(owner, jnp.logical_and(x == xx, y == c))))(
                functools.partial(arrived, recvn.at[xx, c], rn.at[xx, c], sn.at[0, 0, 0])
            )
    whole = jnp.zeros((8, LANES), F32)
    for xx in range(nx):
        for c in range(4):
            whole += recvn[xx, c]
    whole = jnp.broadcast_to(jnp.sum(whole, axis=1, keepdims=True), (8, LANES))
    shift = [whole[4 + q : 5 + q] / norm1[q] for q in range(POLS)]
    norm2 = [whole[q : q + 1] - shift[q] * whole[4 + q : 5 + q] for q in range(POLS)]
    inverse = spread([1.0 / jnp.sqrt(t) for t in norm2])
    back = spread(shift)
    for jh, jp in near:
        c = (h + jh) % 2 * 2 + (p + jp) % 2
        hear = functools.partial(arrived, recv3.at[1, c], r3.at[1, c], s3.at[1, 0])
        if (jh, jp) == (0, 0):
            pl.when(jnp.logical_not(owner))(hear)
        else:
            hear()
    for c in range(4):
        value = (recv3[1, c] - back * u[1, c]) * inverse
        for q in range(POLS):
            for t in range(LINES):
                at = ((t // 2) * 8 + (c // 2) * 4 + (t % 2) * 2 + c % 2) * LANES
                last_ref[q : q + 1, at : at + LANES] = value[LINES * q + t : LINES * q + t + 1, :]
    for q in range(POLS):
        alpha_ref[q : q + 1, 0:1] = alpha[q][:, :1]
        alpha_ref[q : q + 1, 1:2] = (alpha[q] + shift[q])[:, :1]
        beta_ref[q : q + 1, 0:1] = jnp.sqrt(ratio[q])[:, :1]
        beta_ref[q : q + 1, 1:2] = jnp.sqrt(norm2[q] / norm1[q])[:, :1]
    finish()


def lanczos(sizes, kernel_half, dipole, band_energy, core_energy, core_index):
    nx, nz, _ = sizes
    rows, cols = kernel_half.shape
    dma = pltpu.SemaphoreType.DMA
    chunk = (ROWS, LANES)
    longer = (ROWS + 8, LANES)
    tile = (8, LANES)
    return pl.pallas_call(
        functools.partial(kernel, sizes),
        out_shape=(
            jax.ShapeDtypeStruct((POLS, 2), F32),
            jax.ShapeDtypeStruct((POLS, 2), F32),
            jax.ShapeDtypeStruct(dipole.shape, F32),
        ),
        in_specs=[pl.BlockSpec(memory_space=pl.ANY)] * 5,
        out_specs=[pl.BlockSpec(memory_space=pltpu.VMEM)] * 3,
        scratch_shapes=[
            pltpu.VMEM((rows, cols), BF),
            pltpu.VMEM(dipole.shape, F32),
            pltpu.VMEM(band_energy.shape, F32),
            pltpu.SMEM(core_energy.shape, F32),
            pltpu.SMEM(core_index.shape, jnp.int32),
            pltpu.VMEM((POLS, cols), F32),
            pltpu.VMEM((2, 4, *chunk), F32),
            pltpu.VMEM((4, *tile), F32),
            pltpu.VMEM((2, 4, *longer), F32),
            pltpu.VMEM((2, 8, *longer), F32),
            pltpu.VMEM((2, 2, *tile), F32),
            pltpu.VMEM((2, nx, 2, *tile), F32),
            pltpu.VMEM((2, *longer), F32),
            pltpu.VMEM((2, nz, *longer), F32),
            pltpu.VMEM((2, *chunk), F32),
            pltpu.VMEM((2, 4, *chunk), F32),
            pltpu.VMEM(tile, F32),
            pltpu.VMEM((2, *tile), F32),
            pltpu.VMEM((2, *tile), F32),
            pltpu.VMEM((2, nx, *tile), F32),
            pltpu.VMEM(tile, F32),
            pltpu.VMEM((nx, 4, *tile), F32),
            dma((6,)), dma((2,)),
            dma((nx - 1, 2)), dma((1,)),
            dma((2, 4)), dma((2, 8)),
            dma((2, 2)), dma((2, nx, 2)),
            dma((2, nz - 1)), dma((2, nz)),
            dma((2, 8)), dma((2, 4)),
            dma((nx - 1, 2)), dma((2,)),
            dma((2, 7)), dma((2, nx)),
            dma((nx, 4, 2)), dma((nx, 4)),
        ],
        compiler_params=pltpu.CompilerParams(collective_id=0, has_side_effects=True),
    )(kernel_half, dipole, band_energy, core_energy, core_index)


def solution(mesh):
    nx, np_, nz = mesh.shape["row"], mesh.shape["pol"], mesh.shape["col"] // 4
    sizes = (nx, nz, nz * np_ // nx)
    in_specs = (P("row", ("pol", "col")), P(None, "row"), P("row", None), P(), P("row"))
    out_specs = (P(), P(), P(None, "row"))
    return jax.shard_map(
        functools.partial(lanczos, sizes), mesh=mesh, in_specs=in_specs, out_specs=out_specs, check_vma=False
    )
```

```python
import functools

import jax
import jax.numpy as jnp
from jax import lax
from jax.experimental import pallas as pl
from jax.experimental.pallas import tpu as pltpu
from jax.sharding import PartitionSpec as P

F32 = jnp.float32
BF = jnp.bfloat16
MESH = pl.DeviceIdType.MESH
CORES = 4
LANES = 128
POLS = 3
LINES = 8
ROWS = POLS * LINES


def spread(parts):
    return jnp.concatenate([jnp.broadcast_to(t, (LINES, t.shape[1])) for t in parts], axis=0)


def over_lines(x):
    return [jnp.sum(x[LINES * q : LINES * (q + 1)], axis=0, keepdims=True) for q in range(POLS)]


def placed(parts, first=0):
    row = lax.broadcasted_iota(jnp.int32, (8, LANES), 0)
    out = jnp.zeros((8, LANES), F32)
    for q, part in enumerate(parts):
        out = jnp.where(row == first + q, jnp.broadcast_to(part, (8, LANES)), out)
    return out


def two_terms(x):
    high = x.astype(BF).astype(F32)
    return jnp.concatenate([high, x - high], axis=0).astype(BF)


def joined(x):
    return x[:ROWS] + x[ROWS:]


def kernel(
    sizes,
    w_hbm, dip_hbm, band_hbm, core_hbm, index_hbm,
    alpha_ref, beta_ref, last_ref,
    w, dip, band, core, index,
    uc0, u, en,
    send1, recv1, sendc, recvc, send2, recv2, send3, recv3, sendt, recvt, sendx, recvx, sendn, recvn,
    load_sem, core_sem, s0, r0, s1, r1, sc, rc, s2, r2, s3, r3, st, rt, sx, rx, sn, rn,
):
    nx, nz, zl_count = sizes
    zh_count = nz // zl_count
    p = lax.axis_index("pol")
    x = lax.axis_index("row")
    col = lax.axis_index("col")
    z = col // 4
    h = (col // 2) % 2
    k = col % 2
    y = h * 2 + p
    zl = z % zl_count
    home = p * zh_count + z // zl_count
    is_home = x == home
    away = jnp.logical_not(is_home)
    owner = k == 1
    keeper = (z // zl_count) == (x % zh_count)
    p_keep = x // zh_count

    def dev(pp, xx, zz, hh, kk):
        return (pp, xx, zz * 4 + hh * 2 + kk)

    barrier = pltpu.get_barrier_semaphore()

    def greet(d):
        pl.semaphore_signal(barrier, inc=1, device_id=d, device_id_type=MESH)

    beside = [(dx, j) for dx in (2, 1, 3, 0) for j in range(4)]
    for dx, j in beside:
        hh, pp = (h + j // 2) % 2, (p + j % 2) % 2
        if (dx, j) == (0, 0):
            greet(dev(p, x, z, h, 1 - k))
        else:
            greet(dev(pp, (x + dx) % nx, z, hh, 1))

    @pl.when(owner)
    def _():
        for d in sorted(range(1, nz), key=lambda d: -min(d, nz - d)):
            greet(dev(p, x, (z + d) % nz, h, 1))
        for dx, j in beside:
            if (dx, j) != (0, 0):
                greet(dev((p + j % 2) % 2, (x + dx) % nx, z, (h + j // 2) % 2, 0))

    loads = [
        pltpu.make_async_copy(dip_hbm, dip, load_sem.at[0]),
        pltpu.make_async_copy(band_hbm, band, load_sem.at[1]),
        pltpu.make_async_copy(core_hbm, core, core_sem.at[0]),
        pltpu.make_async_copy(index_hbm, index, core_sem.at[1]),
    ]
    for c in loads:
        c.start()
    big = w.shape[0] // 4
    w_loads = [
        pltpu.make_async_copy(
            w_hbm.at[pl.ds(i * big, big)], w.at[pl.ds(i * big, big)], load_sem.at[2 + i]
        )
        for i in range(4)
    ]
    for c in w_loads:
        c.start()

    ends = []

    def start(make, condition=None, within=None):
        if condition is None:
            make().start()
        else:
            pl.when(condition)(lambda: make().start())
        ends.append((make, condition, within))

    def finish():
        for make, condition, within in ends:
            if condition is None and within is None:
                make().wait_send()
            elif condition is None or within is None:
                pl.when(within if condition is None else condition)(lambda make=make: make().wait_send())
            else:
                pl.when(jnp.logical_and(condition, within))(lambda make=make: make().wait_send())

    def send(src, dst, send_sem, recv_sem, device):
        return pltpu.make_async_remote_copy(
            src_ref=src, dst_ref=dst, send_sem=send_sem, recv_sem=recv_sem, device_id=device,
            device_id_type=MESH,
        )

    me = dev(p, x, z, h, k)

    def arrived(dst, recv_sem, spare_sem):
        send(dst, dst, spare_sem, recv_sem, me).wait_recv()

    for c in loads:
        c.wait()
    for c in range(4):
        for q in range(POLS):
            for t in range(LINES):
                at = ((t // 2) * 8 + (c // 2) * 4 + (t % 2) * 2 + c % 2) * LANES
                u[0, c, LINES * q + t : LINES * q + t + 1, :] = dip[q : q + 1, at : at + LANES]
    offsets = []
    for i in range(2 * CORES):
        level = index[i]
        off = jnp.float32(0.0)
        for j in range(CORES):
            off = jnp.where(level == j, core[j], off)
        offsets.append(off)
    row8 = lax.broadcasted_iota(jnp.int32, (8, LANES), 0)
    for c in range(4):
        value = jnp.zeros((8, LANES), F32)
        for t in range(LINES):
            line = (t // 2) * 8 + (c // 2) * 4 + (t % 2) * 2 + c % 2
            at = (line % 4) * LANES
            level = band[line // 16 : line // 16 + 1, at : at + LANES] - offsets[line // 4]
            value = jnp.where(row8 == t, jnp.broadcast_to(level, (8, LANES)), value)
        en[c] = value

    pl.semaphore_wait(barrier, jnp.where(owner, 2 * len(beside) - 1 + nz - 1, len(beside)))

    def own_lines(kk):
        return pl.ds(pl.multiple_of((zl * 4 + h * 2 + kk) * 2 * LANES, 2 * LANES), 2 * LANES)

    def first_copy(dx, kk):
        return send(
            dip.at[:, own_lines(kk)], uc0, s0.at[dx - 1, kk], r0.at[0], dev(p, (x + dx) % nx, z, h, kk)
        )

    for dx in (2, 1, 3):
        for kk in range(2):
            start(functools.partial(first_copy, dx, kk), jnp.logical_and(is_home, owner))

    @pl.when(is_home)
    def _():
        uc0[...] = dip[:, own_lines(k)]

    for c in w_loads:
        c.wait()

    row_mod = lax.broadcasted_iota(jnp.int32, (ROWS, 2 * LANES), 0) % LINES

    def line_rows(hh, pp, t):
        line = (t // 2) * 8 + hh * 4 + (t % 2) * 2 + pp
        return pl.ds(pl.multiple_of(line * LANES, LANES), LANES)

    def columns_of(value, hh, pp):
        left = two_terms(value)
        out = jnp.zeros((ROWS, 2 * LANES), F32)
        for t in range(LINES):
            part = joined(jnp.dot(left, w[line_rows(hh, pp, t), :], preferred_element_type=F32))
            out = jnp.where(row_mod == t, part, out)
        return out

    near = [(0, 0), (0, 1), (1, 1), (1, 0)]

    alpha = ratio = column = col_first = norms = None
    for step in range(2):
        rows = ROWS + 8 if step == 0 else ROWS
        sums = jnp.zeros((ROWS, 2 * LANES), F32)
        if step == 0:
            for c in range(4):
                sums += columns_of(u[0, c], c // 2, c % 2)
            col_part = over_lines(sums)
            col_first = col_part
        else:
            for jh, jp in near:
                hh, pp = (h + jh) % 2, (p + jp) % 2
                c = hh * 2 + pp
                hear = functools.partial(arrived, recv3.at[0, c], r3.at[0, c], s3.at[0, 0])
                if (jh, jp) == (0, 0):
                    pl.when(jnp.logical_not(owner))(hear)
                else:
                    hear()
                sums += columns_of(recv3[0, c], hh, pp)
            for xx in range(nx):
                pl.when(jnp.logical_not(jnp.logical_and(owner, x == xx)))(
                    functools.partial(arrived, recvx.at[0, xx], rx.at[0, xx], sx.at[0, 0])
                )
            whole = recvx[0, 0]
            for xx in range(1, nx):
                whole += recvx[0, xx]
            whole = jnp.broadcast_to(jnp.sum(whole, axis=1, keepdims=True), (8, LANES))
            norms = [whole[q : q + 1] for q in range(POLS)]
            alpha = [whole[4 + q : 5 + q] / norms[q] for q in range(POLS)]
            col_part = over_lines(sums)
            col_part = [col_part[q] - alpha[q][:, :1] * col_first[q] for q in range(POLS)]
        for half in range(2):
            sendc[step, half] = placed([t[:, half * LANES : (half + 1) * LANES] for t in col_part])

        def col_copy(half, step=step):
            return send(
                sendc.at[step, half], recvc.at[step, x, k], sc.at[step, half], rc.at[step, x, k],
                dev(half, home, z, h, 1),
            )

        for half in range(2):
            mine = jnp.logical_and(owner, jnp.logical_and(is_home, p == half))

            @pl.when(mine)
            def _(half=half, step=step):
                recvc[step, x, k] = sendc[step, half]

            start(functools.partial(col_copy, half), jnp.logical_not(mine))

        if step == 0:
            pl.when(away)(functools.partial(arrived, uc0, r0.at[0], s0.at[0, 0]))
            column = [uc0[q : q + 1, :] for q in range(POLS)]
        else:

            @pl.when(is_home)
            def _():
                for half in range(2):
                    value = recv3[0, h * 2 + half]
                    mask = lax.broadcasted_iota(jnp.int32, (ROWS, LANES), 0) % LINES == zl * 2 + k
                    recvt[half] = placed(over_lines(jnp.where(mask, value, 0.0)))

            for half in range(2):
                pl.when(away)(functools.partial(arrived, recvt.at[half], rt.at[half], st.at[0, 0]))
            got = jnp.concatenate([recvt[0], recvt[1]], axis=1)
            got = jnp.where(away, jnp.where(k == 1, pltpu.roll(got, 4, 0), got), got)
            column = [got[q : q + 1] - alpha[q][:, :1] * column[q] for q in range(POLS)]
        if step == 0:
            twice = []
            for q in range(POLS):
                line = 2.0 * col_part[q] * column[q]
                twice.append(line[:, :LANES] + line[:, LANES:])
            sum_rows = placed(twice)
        left = two_terms(spread(column))

        def row_copy(j, step=step, rows=rows):
            jh, jp = near[j]
            return send(
                send1.at[step, j, pl.ds(0, rows)], recv1.at[step, y * 2 + k, pl.ds(0, rows)],
                s1.at[step, j], r1.at[step, y * 2 + k], dev((p + jp) % 2, x, z, (h + jh) % 2, 1),
            )

        for j in (3, 2, 1, 0):
            jh, jp = near[j]
            hh, pp = (h + jh) % 2, (p + jp) % 2
            lines = jnp.zeros((ROWS, LANES), F32)
            for t in range(LINES):
                part = joined(
                    lax.dot_general(
                        left, w[line_rows(hh, pp, t), :], (((1,), (1,)), ((), ())),
                        preferred_element_type=F32,
                    )
                )
                lines = jnp.where(row_mod[:, :LANES] == t, part, lines)
            send1[step, j, :ROWS] = lines
            if step == 0:
                send1[step, j, ROWS:] = sum_rows
            start(functools.partial(row_copy, j), None if j else jnp.logical_not(owner))

        if step == 1:
            factor = spread(alpha)
            for c in range(4):
                u[1, c] = recv3[0, c] - factor * u[0, c]
        squares = jnp.zeros((ROWS, LANES), F32)
        weighted = jnp.zeros((ROWS, LANES), F32)
        for c in range(4):
            sq = u[step, c] * u[step, c]
            squares += sq
            weighted += jnp.concatenate([en[c]] * POLS, axis=0) * sq
        own_sums = placed(over_lines(squares))

        def x_copy(dx, kk, at):
            return send(
                sendx.at[at], recvx.at[at, x], sx.at[at, (dx - 1) * 2 + kk if dx else 6], rx.at[at, x],
                dev(p, (x + dx) % nx, z, h, kk),
            )

        def share(at):
            for dx in (2, 1, 3):
                for kk in range(2):
                    start(functools.partial(x_copy, dx, kk, at), None, owner)
            start(functools.partial(x_copy, 0, 0, at), None, owner)
            recvx[at, x] = sendx[at]

        if step == 0:
            own_sums += placed(over_lines(weighted), 4)

        @pl.when(owner)
        def _(step=step, rows=rows, own_sums=own_sums):
            if step == 1:
                sendx[1] = own_sums
                share(1)
            recv1[step, y * 2 + k, pl.ds(0, rows)] = send1[step, 0, pl.ds(0, rows)]
            for jh, jp in near:
                hh, pp = (h + jh) % 2, (p + jp) % 2
                for kk in range(2):
                    if (jh, jp, kk) != (0, 0, 1):
                        g = (hh * 2 + pp) * 2 + kk
                        arrived(recv1.at[step, g, pl.ds(0, rows)], r1.at[step, g], s1.at[step, 0])
            total = recv1[step, 0, pl.ds(0, rows)]
            for g in range(1, 8):
                total += recv1[step, g, pl.ds(0, rows)]
            send2[step, pl.ds(0, rows)] = total

            @pl.when(keeper)
            def _():
                for kk in range(2):
                    for xx in range(nx):
                        hear = functools.partial(
                            arrived, recvc.at[step, xx, kk], rc.at[step, xx, kk], sc.at[step, 0]
                        )
                        if kk == 0:
                            hear()
                        else:
                            pl.when(jnp.logical_not(jnp.logical_and(x == xx, p == p_keep)))(hear)
                    cols = recvc[step, 0, kk]
                    for xx in range(1, nx):
                        cols += recvc[step, xx, kk]
                    for q in range(POLS):
                        at = pl.ds(LINES * q, LINES)
                        line = jnp.broadcast_to(cols[q : q + 1], (8, LANES))
                        send2[step, at] = send2[step, at] + jnp.where(row8 == zl * 2 + kk, line, 0.0)

            def z_copy(d):
                return send(
                    send2.at[step, pl.ds(0, rows)], recv2.at[step, z, pl.ds(0, rows)], s2.at[step, d - 1],
                    r2.at[step, z], dev(p, x, (z + d) % nz, h, 1),
                )

            for d in sorted(range(1, nz), key=lambda d: -min(d, nz - d)):
                start(functools.partial(z_copy, d), None, owner)
            recv2[step, z, pl.ds(0, rows)] = send2[step, pl.ds(0, rows)]
            if step == 1:
                for dx in range(1, nx):
                    xx = (x + dx) % nx
                    arrived(recvx.at[1, xx], rx.at[1, xx], sx.at[1, 0])
            for d in range(1, nz):
                zz = (z + d) % nz
                arrived(recv2.at[step, zz, pl.ds(0, rows)], r2.at[step, zz], s2.at[step, 0])
            total = recv2[step, 0, pl.ds(0, rows)]
            for zz in range(1, nz):
                total += recv2[step, zz, pl.ds(0, rows)]
            value = total[:ROWS] + jnp.concatenate([en[y]] * POLS, axis=0) * u[step, y]

            if step == 0:
                sendx[0] = jnp.concatenate([total[ROWS + 4 :], total[ROWS : ROWS + 4]], axis=0) + own_sums
                share(0)
                send3[0] = value
                mod = lax.broadcasted_iota(jnp.int32, (ROWS, LANES), 0) % LINES
                tile = jnp.zeros((8, LANES), F32)
                for kk in range(2):
                    tile += placed(over_lines(jnp.where(mod == zl * 2 + kk, value, 0.0)), 4 * kk)
                sendt[...] = tile

                def tile_copy(dx, kk):
                    return send(
                        sendt, recvt.at[p], st.at[dx - 1, kk], rt.at[p],
                        dev(p_keep, (x + dx) % nx, z, h, kk),
                    )

                for dx in (2, 1, 3):
                    for kk in range(2):
                        start(functools.partial(tile_copy, dx, kk), keeper, owner)
            else:
                w1 = value - spread(alpha) * u[1, y] - spread(ratio_of(1)) * u[0, y]
                sendn[...] = placed(over_lines(w1 * w1)) + placed(over_lines(w1 * u[1, y]), 4)

                def sums_copy(dx, j, kk):
                    jh, jp = near[j]
                    return send(
                        sendn, recvn.at[x, y], sn.at[dx, j, kk], rn.at[x, y],
                        dev((p + jp) % 2, (x + dx) % nx, z, (h + jh) % 2, kk),
                    )

                for dx in (2, 1, 3, 0):
                    for j in (3, 2, 1, 0):
                        for kk in range(2):
                            if (dx, j, kk) != (0, 0, 1):
                                start(functools.partial(sums_copy, dx, j, kk), None, owner)
                recvn[x, y] = sendn[...]
                send3[1] = w1

            def chunk_copy(j, kk):
                jh, jp = near[j]
                return send(
                    send3.at[step], recv3.at[step, y], s3.at[step, j * 2 + kk], r3.at[step, y],
                    dev((p + jp) % 2, x, z, (h + jh) % 2, kk),
                )

            for j in (3, 2, 1, 0):
                for kk in range(2):
                    if (j, kk) != (0, 1):
                        start(functools.partial(chunk_copy, j, kk), None, owner)
            recv3[step, y] = send3[step]

        def ratio_of(at):
            whole = recvx[at, 0]
            for xx in range(1, nx):
                whole += recvx[at, xx]
            whole = jnp.broadcast_to(jnp.sum(whole, axis=1, keepdims=True), (8, LANES))
            return [whole[q : q + 1] / norms[q] for q in range(POLS)]

    @pl.when(jnp.logical_not(owner))
    def _():
        for xx in range(nx):
            arrived(recvx.at[1, xx], rx.at[1, xx], sx.at[1, 0])

    ratio = ratio_of(1)
    norm1 = [ratio[q] * norms[q] for q in range(POLS)]
    for xx in range(nx):
        for c in range(4):
            pl.when(jnp.logical_not(jnp.logical_and(owner, jnp.logical_and(x == xx, y == c))))(
                functools.partial(arrived, recvn.at[xx, c], rn.at[xx, c], sn.at[0, 0, 0])
            )
    whole = jnp.zeros((8, LANES), F32)
    for xx in range(nx):
        for c in range(4):
            whole += recvn[xx, c]
    whole = jnp.broadcast_to(jnp.sum(whole, axis=1, keepdims=True), (8, LANES))
    shift = [whole[4 + q : 5 + q] / norm1[q] for q in range(POLS)]
    norm2 = [whole[q : q + 1] - shift[q] * whole[4 + q : 5 + q] for q in range(POLS)]
    inverse = spread([1.0 / jnp.sqrt(t) for t in norm2])
    back = spread(shift)
    for jh, jp in near:
        c = (h + jh) % 2 * 2 + (p + jp) % 2
        hear = functools.partial(arrived, recv3.at[1, c], r3.at[1, c], s3.at[1, 0])
        if (jh, jp) == (0, 0):
            pl.when(jnp.logical_not(owner))(hear)
        else:
            hear()
    for c in range(4):
        value = (recv3[1, c] - back * u[1, c]) * inverse
        for q in range(POLS):
            for t in range(LINES):
                at = ((t // 2) * 8 + (c // 2) * 4 + (t % 2) * 2 + c % 2) * LANES
                last_ref[q : q + 1, at : at + LANES] = value[LINES * q + t : LINES * q + t + 1, :]
    for q in range(POLS):
        alpha_ref[0:1, q : q + 1] = alpha[q][:, :1]
        alpha_ref[1:2, q : q + 1] = (alpha[q] + shift[q])[:, :1]
        beta_ref[0:1, q : q + 1] = jnp.sqrt(ratio[q])[:, :1]
        beta_ref[1:2, q : q + 1] = jnp.sqrt(norm2[q] / norm1[q])[:, :1]
    finish()


def write_out(*refs):
    sources, targets, sems = refs[:3], refs[3:6], refs[6]
    copies = [pltpu.make_async_copy(a, b, sems.at[i]) for i, (a, b) in enumerate(zip(sources, targets, strict=True))]
    for c in copies:
        c.start()
    for c in copies:
        c.wait()


def lanczos(sizes, kernel_half, dipole, band_energy, core_energy, core_index):
    nx, nz, _ = sizes
    rows, cols = kernel_half.shape
    dma = pltpu.SemaphoreType.DMA
    chunk = (ROWS, LANES)
    longer = (ROWS + 8, LANES)
    tile = (8, LANES)
    results = pl.pallas_call(
        functools.partial(kernel, sizes),
        out_shape=(pltpu.VMEM((2, POLS), F32), pltpu.VMEM((2, POLS), F32), pltpu.VMEM(dipole.shape, F32)),
        in_specs=[pl.BlockSpec(memory_space=pl.ANY)] * 5,
        out_specs=[pl.BlockSpec(memory_space=pltpu.VMEM)] * 3,
        scratch_shapes=[
            pltpu.VMEM((rows, cols), BF),
            pltpu.VMEM(dipole.shape, F32),
            pltpu.VMEM(band_energy.shape, F32),
            pltpu.SMEM(core_energy.shape, F32),
            pltpu.SMEM(core_index.shape, jnp.int32),
            pltpu.VMEM((POLS, cols), F32),
            pltpu.VMEM((2, 4, *chunk), F32),
            pltpu.VMEM((4, *tile), F32),
            pltpu.VMEM((2, 4, *longer), F32),
            pltpu.VMEM((2, 8, *longer), F32),
            pltpu.VMEM((2, 2, *tile), F32),
            pltpu.VMEM((2, nx, 2, *tile), F32),
            pltpu.VMEM((2, *longer), F32),
            pltpu.VMEM((2, nz, *longer), F32),
            pltpu.VMEM((2, *chunk), F32),
            pltpu.VMEM((2, 4, *chunk), F32),
            pltpu.VMEM(tile, F32),
            pltpu.VMEM((2, *tile), F32),
            pltpu.VMEM((2, *tile), F32),
            pltpu.VMEM((2, nx, *tile), F32),
            pltpu.VMEM(tile, F32),
            pltpu.VMEM((nx, 4, *tile), F32),
            dma((6,)), dma((2,)),
            dma((nx - 1, 2)), dma((1,)),
            dma((2, 4)), dma((2, 8)),
            dma((2, 2)), dma((2, nx, 2)),
            dma((2, nz - 1)), dma((2, nz)),
            dma((2, 8)), dma((2, 4)),
            dma((nx - 1, 2)), dma((2,)),
            dma((2, 7)), dma((2, nx)),
            dma((nx, 4, 2)), dma((nx, 4)),
        ],
        compiler_params=pltpu.CompilerParams(collective_id=0, has_side_effects=True),
    )(kernel_half, dipole, band_energy, core_energy, core_index)
    alphas, betas, last = pl.pallas_call(
        write_out,
        out_shape=(
            jax.ShapeDtypeStruct((2, POLS), F32),
            jax.ShapeDtypeStruct((2, POLS), F32),
            jax.ShapeDtypeStruct(dipole.shape, F32),
        ),
        in_specs=[pl.BlockSpec(memory_space=pltpu.VMEM)] * 3,
        out_specs=[pl.BlockSpec(memory_space=pl.ANY)] * 3,
        scratch_shapes=[dma((3,))],
    )(*[pltpu.with_memory_space_constraint(r, pltpu.VMEM) for r in results])
    return alphas.T, betas.T, last


def solution(mesh):
    nx, np_, nz = mesh.shape["row"], mesh.shape["pol"], mesh.shape["col"] // 4
    sizes = (nx, nz, nz * np_ // nx)
    in_specs = (P("row", ("pol", "col")), P(None, "row"), P("row", None), P(), P("row"))
    out_specs = (P(), P(), P(None, "row"))
    return jax.shard_map(
        functools.partial(lanczos, sizes), mesh=mesh, in_specs=in_specs, out_specs=out_specs, check_vma=False
    )
```

```python
import functools

import jax
import jax.numpy as jnp
from jax import lax
from jax.experimental import pallas as pl
from jax.experimental.pallas import tpu as pltpu
from jax.sharding import PartitionSpec as P

F32 = jnp.float32
BF = jnp.bfloat16
MESH = pl.DeviceIdType.MESH
CORES = 4
LANES = 128
POLS = 3
LINES = 8
ROWS = POLS * LINES


def spread(parts):
    return jnp.concatenate([jnp.broadcast_to(t, (LINES, t.shape[1])) for t in parts], axis=0)


def over_lines(x):
    return [jnp.sum(x[LINES * q : LINES * (q + 1)], axis=0, keepdims=True) for q in range(POLS)]


def placed(parts, first=0):
    row = lax.broadcasted_iota(jnp.int32, (8, LANES), 0)
    out = jnp.zeros((8, LANES), F32)
    for q, part in enumerate(parts):
        out = jnp.where(row == first + q, jnp.broadcast_to(part, (8, LANES)), out)
    return out


def two_terms(x):
    high = x.astype(BF).astype(F32)
    return jnp.concatenate([high, x - high], axis=0).astype(BF)


def joined(x):
    return x[:ROWS] + x[ROWS:]


def kernel(
    sizes,
    w_hbm, dip_hbm, band_hbm, core_hbm, index_hbm,
    alpha_ref, beta_ref, last_ref,
    w, dip, band, core, index,
    uc0, u, en,
    send1, recv1, sendc, recvc, send2, recv2, send3, recv3, sendt, recvt, sendx, recvx, sendn, recvn,
    load_sem, core_sem, s0, r0, s1, r1, sc, rc, s2, r2, s3, r3, st, rt, sx, rx, sn, rn,
):
    nx, nz, zl_count = sizes
    zh_count = nz // zl_count
    p = lax.axis_index("pol")
    x = lax.axis_index("row")
    col = lax.axis_index("col")
    z = col // 4
    h = (col // 2) % 2
    k = col % 2
    y = h * 2 + p
    zl = z % zl_count
    home = p * zh_count + z // zl_count
    is_home = x == home
    away = jnp.logical_not(is_home)
    owner = k == 1
    keeper = (z // zl_count) == (x % zh_count)
    p_keep = x // zh_count

    def dev(pp, xx, zz, hh, kk):
        return (pp, xx, zz * 4 + hh * 2 + kk)

    barrier = pltpu.get_barrier_semaphore()

    def greet(d):
        pl.semaphore_signal(barrier, inc=1, device_id=d, device_id_type=MESH)

    far_first = sorted(range(1, nz), key=lambda d: -min(d, nz - d))

    @pl.when(owner)
    def _():
        for d in far_first:
            greet(dev(p, x, (z + d) % nz, h, 1))

    beside = [(dx, j) for dx in (2, 1, 3, 0) for j in (2, 3, 1, 0)]
    for dx, j in beside:
        hh, pp = (h + j // 2) % 2, (p + j % 2) % 2
        if (dx, j) == (0, 0):
            greet(dev(p, x, z, h, 1 - k))
        else:
            greet(dev(pp, (x + dx) % nx, z, hh, 1))

    @pl.when(owner)
    def _():
        for dx, j in beside:
            if (dx, j) != (0, 0):
                greet(dev((p + j % 2) % 2, (x + dx) % nx, z, (h + j // 2) % 2, 0))

    loads = [
        pltpu.make_async_copy(dip_hbm, dip, load_sem.at[0]),
        pltpu.make_async_copy(band_hbm, band, load_sem.at[1]),
        pltpu.make_async_copy(core_hbm, core, core_sem.at[0]),
        pltpu.make_async_copy(index_hbm, index, core_sem.at[1]),
    ]
    for c in loads:
        c.start()
    big = w.shape[0] // 4
    w_loads = [
        pltpu.make_async_copy(
            w_hbm.at[pl.ds(i * big, big)], w.at[pl.ds(i * big, big)], load_sem.at[2]
        )
        for i in range(4)
    ]
    for c in w_loads:
        c.start()

    def start(copy, condition=None):
        if condition is None:
            copy().start()
        else:
            pl.when(condition)(lambda: copy().start())

    def send(src, dst, send_sem, recv_sem, device):
        return pltpu.make_async_remote_copy(
            src_ref=src, dst_ref=dst, send_sem=send_sem, recv_sem=recv_sem, device_id=device,
            device_id_type=MESH,
        )

    me = dev(p, x, z, h, k)

    def arrived(dst, recv_sem):
        send(dst, dst, s1.at[0], recv_sem, me).wait_recv()

    def left_here(src, send_sem):
        send(src, src, send_sem, r1.at[0], me).wait_send()

    def either(condition, then, other):
        pl.when(condition)(then)
        pl.when(jnp.logical_not(condition))(other)

    def finish():
        @pl.when(owner)
        def _():
            @pl.when(is_home)
            def _():
                left_here(dip.at[:, pl.ds(0, 6 * 2 * LANES)], s0.at[0])

            @pl.when(keeper)
            def _():
                left_here(recvc.at[pl.ds(0, 6)], st.at[0])

            left_here(recv2.at[pl.ds(0, 2 * (nz - 1))], s2.at[0])
            for step in range(2):
                left_here(recv3.at[pl.ds(0, 7)], s3.at[step])
                left_here(recvn.at[pl.ds(0, 16 - step)], sn.at[step])
            left_here(recvc.at[pl.ds(0, 14)], sx.at[0])

        either(
            owner,
            lambda: left_here(recv1.at[pl.ds(0, 6)], s1.at[0]),
            lambda: left_here(recv1.at[pl.ds(0, 8)], s1.at[0]),
        )
        either(
            jnp.logical_and(owner, is_home),
            lambda: left_here(recvc.at[pl.ds(0, 2)], sc.at[0]),
            lambda: left_here(recvc.at[pl.ds(0, 4)], sc.at[0]),
        )

    for c in loads:
        c.wait()
    for c in range(4):
        for q in range(POLS):
            for t in range(LINES):
                at = ((t // 2) * 8 + (c // 2) * 4 + (t % 2) * 2 + c % 2) * LANES
                u[0, c, LINES * q + t : LINES * q + t + 1, :] = dip[q : q + 1, at : at + LANES]
    offsets = []
    for i in range(2 * CORES):
        level = index[i]
        off = jnp.float32(0.0)
        for j in range(CORES):
            off = jnp.where(level == j, core[j], off)
        offsets.append(off)
    row8 = lax.broadcasted_iota(jnp.int32, (8, LANES), 0)
    for c in range(4):
        value = jnp.zeros((8, LANES), F32)
        for t in range(LINES):
            line = (t // 2) * 8 + (c // 2) * 4 + (t % 2) * 2 + c % 2
            at = (line % 4) * LANES
            level = band[line // 16 : line // 16 + 1, at : at + LANES] - offsets[line // 4]
            value = jnp.where(row8 == t, jnp.broadcast_to(level, (8, LANES)), value)
        en[c] = value

    pl.semaphore_wait(barrier, jnp.where(owner, 2 * len(beside) - 1 + nz - 1, len(beside)))

    def own_lines(kk):
        return pl.ds(pl.multiple_of((zl * 4 + h * 2 + kk) * 2 * LANES, 2 * LANES), 2 * LANES)

    def first_copy(dx, kk):
        return send(
            dip.at[:, own_lines(kk)], uc0, s0.at[0], r0.at[0], dev(p, (x + dx) % nx, z, h, kk)
        )

    for dx in (2, 1, 3):
        for kk in range(2):
            start(functools.partial(first_copy, dx, kk), jnp.logical_and(is_home, owner))

    @pl.when(is_home)
    def _():
        uc0[...] = dip[:, own_lines(k)]

    pltpu.make_async_copy(w_hbm, w, load_sem.at[2]).wait()

    row_mod = lax.broadcasted_iota(jnp.int32, (ROWS, 2 * LANES), 0) % LINES

    def line_rows(hh, pp, t):
        line = (t // 2) * 8 + hh * 4 + (t % 2) * 2 + pp
        return pl.ds(pl.multiple_of(line * LANES, LANES), LANES)

    def columns_of(value, hh, pp):
        left = two_terms(value)
        out = jnp.zeros((ROWS, 2 * LANES), F32)
        for t in range(LINES):
            part = joined(jnp.dot(left, w[line_rows(hh, pp, t), :], preferred_element_type=F32))
            out = jnp.where(row_mod == t, part, out)
        return out

    near = [(0, 0), (0, 1), (1, 1), (1, 0)]

    alpha = ratio = column = col_first = norms = None
    for step in range(2):
        sums = jnp.zeros((ROWS, 2 * LANES), F32)
        if step == 0:
            for c in range(4):
                sums += columns_of(u[0, c], c // 2, c % 2)
            col_part = over_lines(sums)
            col_first = col_part
        else:
            def chunk_share(jh, jp):
                hh, pp = (h + jh) % 2, (p + jp) % 2
                c = hh * 2 + pp
                hear = functools.partial(arrived, recv3.at[c], r3.at[c])
                if (jh, jp) == (0, 0):
                    pl.when(jnp.logical_not(owner))(hear)
                else:
                    hear()
                return columns_of(recv3[c], hh, pp)

            for jh, jp in near[:3]:
                sums += chunk_share(jh, jp)
            either(
                owner,
                lambda: arrived(recvx.at[pl.ds(0, nx - 1)], rx.at[0]),
                lambda: arrived(recvx.at[pl.ds(0, nx)], rx.at[0]),
            )
            whole = recvx[0]
            for xx in range(1, nx):
                whole += recvx[xx]
            whole = jnp.broadcast_to(jnp.sum(whole, axis=1, keepdims=True), (8, LANES))
            norms = [whole[q : q + 1] for q in range(POLS)]
            alpha = [whole[4 + q : 5 + q] / norms[q] for q in range(POLS)]
            sums += chunk_share(*near[3])
            col_part = over_lines(sums)
            col_part = [col_part[q] - alpha[q][:, :1] * col_first[q] for q in range(POLS)]
        for half in range(2):
            sendc[step, half] = placed([t[:, half * LANES : (half + 1) * LANES] for t in col_part])

        def col_copy(half, step=step):
            return send(
                sendc.at[step, half], recvc.at[(step * nx + x) * 2 + k], sc.at[0], rc.at[step],
                dev(half, home, z, h, 1),
            )

        for half in range(2):
            mine = jnp.logical_and(owner, jnp.logical_and(is_home, p == half))

            @pl.when(mine)
            def _(half=half, step=step):
                recvc[(step * nx + x) * 2 + k] = sendc[step, half]

            start(functools.partial(col_copy, half), jnp.logical_not(mine))

        if step == 0:
            pl.when(away)(functools.partial(arrived, uc0, r0.at[0]))
            column = [uc0[q : q + 1, :] for q in range(POLS)]
        else:

            @pl.when(is_home)
            def _():
                for half in range(2):
                    value = recv3[h * 2 + half]
                    mask = lax.broadcasted_iota(jnp.int32, (ROWS, LANES), 0) % LINES == zl * 2 + k
                    recvt[half] = placed(over_lines(jnp.where(mask, value, 0.0)))

            pl.when(away)(functools.partial(arrived, recvt, rt.at[0]))
            got = jnp.concatenate([recvt[0], recvt[1]], axis=1)
            got = jnp.where(away, jnp.where(k == 1, pltpu.roll(got, 4, 0), got), got)
            column = [got[q : q + 1] - alpha[q][:, :1] * column[q] for q in range(POLS)]
        if step == 0:
            twice = []
            for q in range(POLS):
                line = 2.0 * col_part[q] * column[q]
                twice.append(line[:, :LANES] + line[:, LANES:])
            sum_rows = placed(twice)
        left = two_terms(spread(column))

        def row_copy(j, step=step):
            jh, jp = near[j]
            return send(
                send1.at[step, j], recv1.at[step * 8 + y * 2 + k], s1.at[0], r1.at[step], dev((p + jp) % 2, x, z, (h + jh) % 2, 1),
            )

        for j in (3, 2, 1, 0):
            jh, jp = near[j]
            hh, pp = (h + jh) % 2, (p + jp) % 2
            lines = jnp.zeros((ROWS, LANES), F32)
            for t in range(LINES):
                part = joined(
                    lax.dot_general(
                        left, w[line_rows(hh, pp, t), :], (((1,), (1,)), ((), ())),
                        preferred_element_type=F32,
                    )
                )
                lines = jnp.where(row_mod[:, :LANES] == t, part, lines)
            send1[step, j, :ROWS] = lines
            send1[step, j, ROWS:] = sum_rows if step == 0 else jnp.zeros((8, LANES), F32)
            start(functools.partial(row_copy, j), None if j else jnp.logical_not(owner))

        if step == 1:
            factor = spread(alpha)
            for c in range(4):
                u[1, c] = recv3[c] - factor * u[0, c]
        squares = jnp.zeros((ROWS, LANES), F32)
        weighted = jnp.zeros((ROWS, LANES), F32)
        for c in range(4):
            sq = u[step, c] * u[step, c]
            squares += sq
            weighted += jnp.concatenate([en[c]] * POLS, axis=0) * sq
        own_sums = placed(over_lines(squares))

        def x_copy(dx, kk, at):
            return send(
                sendx.at[at], recvx.at[at * nx + x], sx.at[0], rx.at[at],
                dev(p, (x + dx) % nx, z, h, kk),
            )

        def share(at):
            for dx in (2, 1, 3):
                for kk in range(2):
                    start(functools.partial(x_copy, dx, kk, at))
            start(functools.partial(x_copy, 0, 0, at))
            recvx[at * nx + x] = sendx[at]

        if step == 0:
            own_sums += placed(over_lines(weighted), 4)

        @pl.when(owner)
        def _(step=step, own_sums=own_sums):
            if step == 1:
                sendx[1] = own_sums
                share(1)
            recv1[step * 8 + y * 2 + k] = send1[step, 0]
            arrived(recv1.at[pl.ds(step * 8, 7)], r1.at[step])
            total = recv1[step * 8]
            for g in range(1, 8):
                total += recv1[step * 8 + g]
            send2[step] = total

            @pl.when(keeper)
            def _():
                either(
                    p == p_keep,
                    lambda: arrived(recvc.at[pl.ds(step * 2 * nx, 2 * nx - 1)], rc.at[step]),
                    lambda: arrived(recvc.at[pl.ds(step * 2 * nx, 2 * nx)], rc.at[step]),
                )
                for kk in range(2):
                    cols = recvc[step * 2 * nx + kk]
                    for xx in range(1, nx):
                        cols += recvc[(step * nx + xx) * 2 + kk]
                    for q in range(POLS):
                        at = pl.ds(LINES * q, LINES)
                        line = jnp.broadcast_to(cols[q : q + 1], (8, LANES))
                        send2[step, at] = send2[step, at] + jnp.where(row8 == zl * 2 + kk, line, 0.0)

            def z_copy(d):
                return send(
                    send2.at[step], recv2.at[step * nz + z], s2.at[0], r2.at[step],
                    dev(p, x, (z + d) % nz, h, 1),
                )

            for d in far_first:
                start(functools.partial(z_copy, d))
            recv2[step * nz + z] = send2[step]
            if step == 1:
                arrived(recvx.at[pl.ds(nx, nx - 1)], rx.at[1])
            arrived(recv2.at[pl.ds(step * nz, nz - 1)], r2.at[step])
            total = recv2[step * nz]
            for zz in range(1, nz):
                total += recv2[step * nz + zz]
            value = total[:ROWS] + jnp.concatenate([en[y]] * POLS, axis=0) * u[step, y]

            if step == 0:
                sendx[0] = jnp.concatenate([total[ROWS + 4 :], total[ROWS : ROWS + 4]], axis=0) + own_sums
                share(0)
                send3[0] = value
                mod = lax.broadcasted_iota(jnp.int32, (ROWS, LANES), 0) % LINES
                tile = jnp.zeros((8, LANES), F32)
                for kk in range(2):
                    tile += placed(over_lines(jnp.where(mod == zl * 2 + kk, value, 0.0)), 4 * kk)
                sendt[...] = tile

                def tile_copy(dx, kk):
                    return send(
                        sendt, recvt.at[p], st.at[0], rt.at[0],
                        dev(p_keep, (x + dx) % nx, z, h, kk),
                    )

                for dx in (2, 1, 3):
                    for kk in range(2):
                        start(functools.partial(tile_copy, dx, kk), keeper)
            else:
                w1 = value - spread(alpha) * u[1, y] - spread(ratio_of(1)) * u[0, y]
                sendn[...] = placed(over_lines(w1 * w1)) + placed(over_lines(w1 * u[1, y]), 4)

                def sums_copy(dx, j, kk):
                    jh, jp = near[j]
                    return send(
                        sendn, recvn.at[x * 4 + y], sn.at[kk], rn.at[0],
                        dev((p + jp) % 2, (x + dx) % nx, z, (h + jh) % 2, kk),
                    )

                for dx in (2, 1, 3, 0):
                    for j in (3, 2, 1, 0):
                        for kk in range(2):
                            if (dx, j, kk) != (0, 0, 1):
                                start(functools.partial(sums_copy, dx, j, kk))
                recvn[x * 4 + y] = sendn[...]
                send3[1] = w1

            def chunk_copy(j, kk):
                jh, jp = near[j]
                return send(
                    send3.at[step], recv3.at[step * 4 + y], s3.at[step], r3.at[step * 4 + y],
                    dev((p + jp) % 2, x, z, (h + jh) % 2, kk),
                )

            for j in (3, 2, 1, 0):
                for kk in range(2):
                    if (j, kk) != (0, 1):
                        start(functools.partial(chunk_copy, j, kk))
            recv3[step * 4 + y] = send3[step]

        def ratio_of(at):
            whole = recvx[at * nx]
            for xx in range(1, nx):
                whole += recvx[at * nx + xx]
            whole = jnp.broadcast_to(jnp.sum(whole, axis=1, keepdims=True), (8, LANES))
            return [whole[q : q + 1] / norms[q] for q in range(POLS)]

    @pl.when(jnp.logical_not(owner))
    def _():
        arrived(recvx.at[pl.ds(nx, nx)], rx.at[1])

    ratio = ratio_of(1)
    norm1 = [ratio[q] * norms[q] for q in range(POLS)]
    either(
        owner,
        lambda: arrived(recvn.at[pl.ds(0, 4 * nx - 1)], rn.at[0]),
        lambda: arrived(recvn.at[pl.ds(0, 4 * nx)], rn.at[0]),
    )
    whole = recvn[0]
    for c in range(1, 4 * nx):
        whole += recvn[c]
    whole = jnp.broadcast_to(jnp.sum(whole, axis=1, keepdims=True), (8, LANES))
    shift = [whole[4 + q : 5 + q] / norm1[q] for q in range(POLS)]
    norm2 = [whole[q : q + 1] - shift[q] * whole[4 + q : 5 + q] for q in range(POLS)]
    inverse = spread([1.0 / jnp.sqrt(t) for t in norm2])
    back = spread(shift)
    for jh, jp in near:
        c = (h + jh) % 2 * 2 + (p + jp) % 2
        hear = functools.partial(arrived, recv3.at[4 + c], r3.at[4 + c])
        if (jh, jp) == (0, 0):
            pl.when(jnp.logical_not(owner))(hear)
        else:
            hear()
    for c in range(4):
        value = (recv3[4 + c] - back * u[1, c]) * inverse
        for q in range(POLS):
            for t in range(LINES):
                at = ((t // 2) * 8 + (c // 2) * 4 + (t % 2) * 2 + c % 2) * LANES
                last_ref[q : q + 1, at : at + LANES] = value[LINES * q + t : LINES * q + t + 1, :]
    for q in range(POLS):
        alpha_ref[0:1, q : q + 1] = alpha[q][:, :1]
        alpha_ref[1:2, q : q + 1] = (alpha[q] + shift[q])[:, :1]
        beta_ref[0:1, q : q + 1] = jnp.sqrt(ratio[q])[:, :1]
        beta_ref[1:2, q : q + 1] = jnp.sqrt(norm2[q] / norm1[q])[:, :1]
    finish()


def write_out(*refs):
    sources, targets, sems = refs[:3], refs[3:6], refs[6]
    copies = [pltpu.make_async_copy(a, b, sems.at[i]) for i, (a, b) in enumerate(zip(sources, targets, strict=True))]
    for c in copies:
        c.start()
    for c in copies:
        c.wait()


def lanczos(sizes, kernel_half, dipole, band_energy, core_energy, core_index):
    nx, nz, _ = sizes
    rows, cols = kernel_half.shape
    dma = pltpu.SemaphoreType.DMA
    chunk = (ROWS, LANES)
    longer = (ROWS + 8, LANES)
    tile = (8, LANES)
    results = pl.pallas_call(
        functools.partial(kernel, sizes),
        out_shape=(pltpu.VMEM((2, POLS), F32), pltpu.VMEM((2, POLS), F32), pltpu.VMEM(dipole.shape, F32)),
        in_specs=[pl.BlockSpec(memory_space=pl.ANY)] * 5,
        out_specs=[pl.BlockSpec(memory_space=pltpu.VMEM)] * 3,
        scratch_shapes=[
            pltpu.VMEM((rows, cols), BF),
            pltpu.VMEM(dipole.shape, F32),
            pltpu.VMEM(band_energy.shape, F32),
            pltpu.SMEM(core_energy.shape, F32),
            pltpu.SMEM(core_index.shape, jnp.int32),
            pltpu.VMEM((POLS, cols), F32),
            pltpu.VMEM((2, 4, *chunk), F32),
            pltpu.VMEM((4, *tile), F32),
            pltpu.VMEM((2, 4, *longer), F32),
            pltpu.VMEM((2 * 8, *longer), F32),
            pltpu.VMEM((2, 2, *tile), F32),
            pltpu.VMEM((2 * nx * 2, *tile), F32),
            pltpu.VMEM((2, *longer), F32),
            pltpu.VMEM((2 * nz, *longer), F32),
            pltpu.VMEM((2, *chunk), F32),
            pltpu.VMEM((2 * 4, *chunk), F32),
            pltpu.VMEM(tile, F32),
            pltpu.VMEM((2, *tile), F32),
            pltpu.VMEM((2, *tile), F32),
            pltpu.VMEM((2 * nx, *tile), F32),
            pltpu.VMEM(tile, F32),
            pltpu.VMEM((nx * 4, *tile), F32),
            dma((3,)), dma((2,)),
            dma((1,)), dma((1,)),
            dma((1,)), dma((2,)),
            dma((1,)), dma((2,)),
            dma((1,)), dma((2,)),
            dma((2,)), dma((8,)),
            dma((1,)), dma((1,)),
            dma((1,)), dma((2,)),
            dma((2,)), dma((1,)),
        ],
        compiler_params=pltpu.CompilerParams(collective_id=0, has_side_effects=True),
    )(kernel_half, dipole, band_energy, core_energy, core_index)
    alphas, betas, last = pl.pallas_call(
        write_out,
        out_shape=(
            jax.ShapeDtypeStruct((2, POLS), F32),
            jax.ShapeDtypeStruct((2, POLS), F32),
            jax.ShapeDtypeStruct(dipole.shape, F32),
        ),
        in_specs=[pl.BlockSpec(memory_space=pltpu.VMEM)] * 3,
        out_specs=[pl.BlockSpec(memory_space=pl.ANY)] * 3,
        scratch_shapes=[dma((3,))],
    )(*[pltpu.with_memory_space_constraint(r, pltpu.VMEM) for r in results])
    return alphas.T, betas.T, last


def solution(mesh):
    nx, np_, nz = mesh.shape["row"], mesh.shape["pol"], mesh.shape["col"] // 4
    sizes = (nx, nz, nz * np_ // nx)
    in_specs = (P("row", ("pol", "col")), P(None, "row"), P("row", None), P(), P("row"))
    out_specs = (P(), P(), P(None, "row"))
    return jax.shard_map(
        functools.partial(lanczos, sizes), mesh=mesh, in_specs=in_specs, out_specs=out_specs, check_vma=False
    )
```

```python
import functools

import jax
import jax.numpy as jnp
from jax import lax
from jax.experimental import pallas as pl
from jax.experimental.pallas import tpu as pltpu
from jax.sharding import PartitionSpec as P

F32 = jnp.float32
BF = jnp.bfloat16
MESH = pl.DeviceIdType.MESH
CORES = 4
LANES = 128
POLS = 3
LINES = 8
ROWS = POLS * LINES


def spread(parts):
    return jnp.concatenate([jnp.broadcast_to(t, (LINES, t.shape[1])) for t in parts], axis=0)


def over_lines(x):
    return [jnp.sum(x[LINES * q : LINES * (q + 1)], axis=0, keepdims=True) for q in range(POLS)]


def placed(parts, first=0):
    row = lax.broadcasted_iota(jnp.int32, (8, LANES), 0)
    out = jnp.zeros((8, LANES), F32)
    for q, part in enumerate(parts):
        out = jnp.where(row == first + q, jnp.broadcast_to(part, (8, LANES)), out)
    return out


def two_terms(x):
    high = x.astype(BF).astype(F32)
    return jnp.concatenate([high, x - high], axis=0).astype(BF)


def joined(x):
    return x[:ROWS] + x[ROWS:]


def kernel(
    sizes,
    w_hbm, dip_hbm, band_hbm, core_hbm, index_hbm,
    alpha_ref, beta_ref, last_ref,
    w, wt, dip, band, core, index,
    uc0, u, en,
    send1, recv1, sendc, recvc, send2, recv2, send3, recv3, sendt, recvt, sendx, recvx, sendn, recvn,
    load_sem, core_sem, s0, r0, s1, r1, sc, rc, s2, r2, s3, r3, st, rt, sx, rx, sn, rn, known, rounds,
):
    nx, nz, zl_count = sizes
    zh_count = nz // zl_count
    p = lax.axis_index("pol")
    x = lax.axis_index("row")
    col = lax.axis_index("col")
    z = col // 4
    h = (col // 2) % 2
    k = col % 2
    y = h * 2 + p
    zl = z % zl_count
    home = p * zh_count + z // zl_count
    is_home = x == home
    away = jnp.logical_not(is_home)
    owner = k == 1
    keeper = (z // zl_count) == (x % zh_count)
    p_keep = x // zh_count

    def dev(pp, xx, zz, hh, kk):
        return (pp, xx, zz * 4 + hh * 2 + kk)

    barrier = pltpu.get_barrier_semaphore()
    far_first = sorted(range(1, nz), key=lambda d: -min(d, nz - d))
    near = [(0, 0), (0, 1), (1, 1), (1, 0)]

    def signal(sem, d):
        pl.semaphore_signal(sem, inc=1, device_id=d, device_id_type=MESH)

    def member(jh, jp, kk):
        return dev((p + jp) % 2, x, z, (h + jh) % 2, kk)

    def above_and_below(sem):
        for d in (1, nz - 1):
            signal(sem, dev(p, x, (z + d) % nz, h, 1))

    for dx in (2, 1, 3):
        signal(barrier, dev(p, (x + dx) % nx, z, h, 1))
    for jh, jp in near[:0:-1]:
        signal(barrier, member(jh, jp, 1))
    signal(barrier, dev(p, x, z, h, 1 - k))

    @pl.when(owner)
    def _():
        for dx in (2, 1, 3):
            signal(barrier, dev(p, (x + dx) % nx, z, h, 0))
        for jh, jp in near[:0:-1]:
            signal(barrier, member(jh, jp, 0))
        above_and_below(barrier)

    loads = [
        pltpu.make_async_copy(dip_hbm, dip, load_sem.at[0]),
        pltpu.make_async_copy(band_hbm, band, load_sem.at[1]),
        pltpu.make_async_copy(core_hbm, core, core_sem.at[0]),
        pltpu.make_async_copy(index_hbm, index, core_sem.at[1]),
    ]
    for c in loads:
        c.start()
    big = w.shape[0] // 4
    w_loads = [
        pltpu.make_async_copy(
            w_hbm.at[pl.ds(i * big, big)], w.at[pl.ds(i * big, big)], load_sem.at[2]
        )
        for i in range(4)
    ]
    for c in w_loads:
        c.start()

    def start(copy, condition=None):
        if condition is None:
            copy().start()
        else:
            pl.when(condition)(lambda: copy().start())

    def send(src, dst, send_sem, recv_sem, device):
        return pltpu.make_async_remote_copy(
            src_ref=src, dst_ref=dst, send_sem=send_sem, recv_sem=recv_sem, device_id=device,
            device_id_type=MESH,
        )

    me = dev(p, x, z, h, k)

    def arrived(dst, recv_sem):
        send(dst, dst, s1.at[0], recv_sem, me).wait_recv()

    def left_here(src, send_sem):
        send(src, src, send_sem, r1.at[0], me).wait_send()

    def either(condition, then, other):
        pl.when(condition)(then)
        pl.when(jnp.logical_not(condition))(other)

    def finish():
        @pl.when(owner)
        def _():
            @pl.when(is_home)
            def _():
                left_here(dip.at[:, pl.ds(0, 6 * 2 * LANES)], s0.at[0])

            @pl.when(keeper)
            def _():
                left_here(recvc.at[pl.ds(0, 6)], st.at[0])

            left_here(recv2.at[pl.ds(0, 2 * (nz - 1))], s2.at[0])
            for step in range(2):
                left_here(recv3.at[pl.ds(0, 7)], s3.at[step])
                left_here(recvn.at[pl.ds(0, 16 - step)], sn.at[step])
            left_here(recvc.at[pl.ds(0, 14)], sx.at[0])

        either(
            owner,
            lambda: left_here(recv1.at[pl.ds(0, 6)], s1.at[0]),
            lambda: left_here(recv1.at[pl.ds(0, 8)], s1.at[0]),
        )
        either(
            jnp.logical_and(owner, is_home),
            lambda: left_here(recvc.at[pl.ds(0, 2)], sc.at[0]),
            lambda: left_here(recvc.at[pl.ds(0, 4)], sc.at[0]),
        )

    loads[0].wait()
    pl.semaphore_wait(barrier, jnp.where(owner, 7 + 2 * (nx - 1) + 2, 4 + nx - 1))

    @pl.when(owner)
    def _():
        for jh, jp in near[:0:-1]:
            for kk in range(2):
                signal(known, member(jh, jp, kk))
        signal(known, dev(p, x, z, h, 0))
        above_and_below(rounds.at[0])

    def own_lines(kk):
        return pl.ds(pl.multiple_of((zl * 4 + h * 2 + kk) * 2 * LANES, 2 * LANES), 2 * LANES)

    def first_copy(dx, kk):
        return send(
            dip.at[:, own_lines(kk)], uc0, s0.at[0], r0.at[0], dev(p, (x + dx) % nx, z, h, kk)
        )

    for dx in (2, 1, 3):
        for kk in range(2):
            start(functools.partial(first_copy, dx, kk), jnp.logical_and(is_home, owner))

    @pl.when(is_home)
    def _():
        uc0[...] = dip[:, own_lines(k)]

    for c in loads[1:]:
        c.wait()
    for c in range(4):
        for q in range(POLS):
            for t in range(LINES):
                at = ((t // 2) * 8 + (c // 2) * 4 + (t % 2) * 2 + c % 2) * LANES
                u[0, c, LINES * q + t : LINES * q + t + 1, :] = dip[q : q + 1, at : at + LANES]
    offsets = []
    for i in range(2 * CORES):
        level = index[i]
        off = jnp.float32(0.0)
        for j in range(CORES):
            off = jnp.where(level == j, core[j], off)
        offsets.append(off)
    row8 = lax.broadcasted_iota(jnp.int32, (8, LANES), 0)
    for c in range(4):
        value = jnp.zeros((8, LANES), F32)
        for t in range(LINES):
            line = (t // 2) * 8 + (c // 2) * 4 + (t % 2) * 2 + c % 2
            at = (line % 4) * LANES
            level = band[line // 16 : line // 16 + 1, at : at + LANES] - offsets[line // 4]
            value = jnp.where(row8 == t, jnp.broadcast_to(level, (8, LANES)), value)
        en[c] = value

    pltpu.make_async_copy(w_hbm, w, load_sem.at[2]).wait()

    row_mod = lax.broadcasted_iota(jnp.int32, (ROWS, 2 * LANES), 0) % LINES

    def line_rows(hh, pp, t):
        line = (t // 2) * 8 + hh * 4 + (t % 2) * 2 + pp
        return pl.ds(pl.multiple_of(line * LANES, LANES), LANES)

    def columns_of(value, hh, pp):
        left = two_terms(value)
        out = jnp.zeros((ROWS, 2 * LANES), F32)
        for t in range(LINES):
            part = joined(jnp.dot(left, w[line_rows(hh, pp, t), :], preferred_element_type=F32))
            out = jnp.where(row_mod == t, part, out)
        return out

    def send_columns(step, col_part):
        for half in range(2):
            sendc[step, half] = placed([t[:, half * LANES : (half + 1) * LANES] for t in col_part])

        def col_copy(half):
            return send(
                sendc.at[step, half], recvc.at[(step * nx + x) * 2 + k], sc.at[0], rc.at[step],
                dev(half, home, z, h, 1),
            )

        for half in range(2):
            mine = jnp.logical_and(owner, jnp.logical_and(is_home, p == half))

            @pl.when(mine)
            def _(half=half):
                recvc[(step * nx + x) * 2 + k] = sendc[step, half]

            start(functools.partial(col_copy, half), jnp.logical_not(mine))

    def transpose():
        side = w.shape[1]

        @pl.loop(0, w.shape[0] // side)
        def _(i):
            at = pl.ds(pl.multiple_of(i * side, side), side)
            wt[:, at] = w[at, :].T

    alpha = ratio = column = col_first = norms = None
    for step in range(2):
        sums = jnp.zeros((ROWS, 2 * LANES), F32)
        if step == 0:
            for c in range(4):
                sums += columns_of(u[0, c], c // 2, c % 2)
            col_part = over_lines(sums)
            col_first = col_part
        else:
            def chunk_share(jh, jp):
                hh, pp = (h + jh) % 2, (p + jp) % 2
                c = hh * 2 + pp
                hear = functools.partial(arrived, recv3.at[c], r3.at[c])
                if (jh, jp) == (0, 0):
                    pl.when(jnp.logical_not(owner))(hear)
                else:
                    hear()
                return columns_of(recv3[c], hh, pp)

            for jh, jp in near[:3]:
                sums += chunk_share(jh, jp)
            either(
                owner,
                lambda: arrived(recvx.at[pl.ds(0, nx - 1)], rx.at[0]),
                lambda: arrived(recvx.at[pl.ds(0, nx)], rx.at[0]),
            )
            whole = recvx[0]
            for xx in range(1, nx):
                whole += recvx[xx]
            whole = jnp.broadcast_to(jnp.sum(whole, axis=1, keepdims=True), (8, LANES))
            norms = [whole[q : q + 1] for q in range(POLS)]
            alpha = [whole[4 + q : 5 + q] / norms[q] for q in range(POLS)]
            sums += chunk_share(*near[3])
            col_part = over_lines(sums)
            col_part = [col_part[q] - alpha[q][:, :1] * col_first[q] for q in range(POLS)]
        if step == 1:
            send_columns(1, col_part)

        if step == 0:
            pl.when(away)(functools.partial(arrived, uc0, r0.at[0]))
            column = [uc0[q : q + 1, :] for q in range(POLS)]
            pl.semaphore_wait(known, jnp.where(owner, 3, 4))
            send_columns(0, col_part)

            @pl.when(owner)
            def _():
                pl.semaphore_wait(rounds.at[0], 2)
                above_and_below(rounds.at[1])

        else:

            @pl.when(is_home)
            def _():
                for half in range(2):
                    value = recv3[h * 2 + half]
                    mask = lax.broadcasted_iota(jnp.int32, (ROWS, LANES), 0) % LINES == zl * 2 + k
                    recvt[half] = placed(over_lines(jnp.where(mask, value, 0.0)))

            pl.when(away)(functools.partial(arrived, recvt, rt.at[0]))
            got = jnp.concatenate([recvt[0], recvt[1]], axis=1)
            got = jnp.where(away, jnp.where(k == 1, pltpu.roll(got, 4, 0), got), got)
            column = [got[q : q + 1] - alpha[q][:, :1] * column[q] for q in range(POLS)]
        if step == 0:
            twice = []
            for q in range(POLS):
                line = 2.0 * col_part[q] * column[q]
                twice.append(line[:, :LANES] + line[:, LANES:])
            sum_rows = placed(twice)
        left = two_terms(spread(column))

        def row_copy(j, step=step):
            jh, jp = near[j]
            return send(
                send1.at[step, j], recv1.at[step * 8 + y * 2 + k], s1.at[0], r1.at[step], dev((p + jp) % 2, x, z, (h + jh) % 2, 1),
            )

        for j in (3, 2, 1, 0):
            jh, jp = near[j]
            hh, pp = (h + jh) % 2, (p + jp) % 2
            lines = jnp.zeros((ROWS, LANES), F32)
            for t in range(LINES):
                if step == 0:
                    part = lax.dot_general(
                        left, w[line_rows(hh, pp, t), :], (((1,), (1,)), ((), ())),
                        preferred_element_type=F32,
                    )
                else:
                    part = jnp.dot(left, wt[:, line_rows(hh, pp, t)], preferred_element_type=F32)
                part = joined(part)
                lines = jnp.where(row_mod[:, :LANES] == t, part, lines)
            send1[step, j, :ROWS] = lines
            send1[step, j, ROWS:] = sum_rows if step == 0 else jnp.zeros((8, LANES), F32)
            start(functools.partial(row_copy, j), None if j else jnp.logical_not(owner))

        if step == 1:
            factor = spread(alpha)
            for c in range(4):
                u[1, c] = recv3[c] - factor * u[0, c]
        squares = jnp.zeros((ROWS, LANES), F32)
        weighted = jnp.zeros((ROWS, LANES), F32)
        for c in range(4):
            sq = u[step, c] * u[step, c]
            squares += sq
            weighted += jnp.concatenate([en[c]] * POLS, axis=0) * sq
        own_sums = placed(over_lines(squares))

        def x_copy(dx, kk, at):
            return send(
                sendx.at[at], recvx.at[at * nx + x], sx.at[0], rx.at[at],
                dev(p, (x + dx) % nx, z, h, kk),
            )

        def share(at):
            for dx in (2, 1, 3):
                for kk in range(2):
                    start(functools.partial(x_copy, dx, kk, at))
            start(functools.partial(x_copy, 0, 0, at))
            recvx[at * nx + x] = sendx[at]

        if step == 0:
            own_sums += placed(over_lines(weighted), 4)

        if step == 0:
            pl.when(jnp.logical_not(owner))(transpose)

        @pl.when(owner)
        def _(step=step, own_sums=own_sums):
            if step == 0:
                pl.semaphore_wait(rounds.at[1], 2)
                above_and_below(rounds.at[2])
            if step == 1:
                sendx[1] = own_sums
                share(1)
            recv1[step * 8 + y * 2 + k] = send1[step, 0]
            arrived(recv1.at[pl.ds(step * 8, 7)], r1.at[step])
            total = recv1[step * 8]
            for g in range(1, 8):
                total += recv1[step * 8 + g]
            send2[step] = total

            @pl.when(keeper)
            def _():
                either(
                    p == p_keep,
                    lambda: arrived(recvc.at[pl.ds(step * 2 * nx, 2 * nx - 1)], rc.at[step]),
                    lambda: arrived(recvc.at[pl.ds(step * 2 * nx, 2 * nx)], rc.at[step]),
                )
                for kk in range(2):
                    cols = recvc[step * 2 * nx + kk]
                    for xx in range(1, nx):
                        cols += recvc[(step * nx + xx) * 2 + kk]
                    for q in range(POLS):
                        at = pl.ds(LINES * q, LINES)
                        line = jnp.broadcast_to(cols[q : q + 1], (8, LANES))
                        send2[step, at] = send2[step, at] + jnp.where(row8 == zl * 2 + kk, line, 0.0)

            if step == 0:
                pl.semaphore_wait(rounds.at[2], 2)
            def z_copy(d):
                return send(
                    send2.at[step], recv2.at[step * nz + z], s2.at[0], r2.at[step],
                    dev(p, x, (z + d) % nz, h, 1),
                )

            for d in far_first:
                start(functools.partial(z_copy, d))
            recv2[step * nz + z] = send2[step]
            rest = jnp.concatenate([en[y]] * POLS, axis=0) * u[step, y]
            if step == 0:
                transpose()
            else:
                arrived(recvx.at[pl.ds(nx, nx - 1)], rx.at[1])
                rest = rest - spread(alpha) * u[1, y] - spread(ratio_of(1)) * u[0, y]
            arrived(recv2.at[pl.ds(step * nz, nz - 1)], r2.at[step])
            total = recv2[step * nz]
            for zz in range(1, nz):
                total += recv2[step * nz + zz]
            value = total[:ROWS] + rest

            if step == 0:
                sendx[0] = jnp.concatenate([total[ROWS + 4 :], total[ROWS : ROWS + 4]], axis=0) + own_sums
                share(0)
                send3[0] = value
                mod = lax.broadcasted_iota(jnp.int32, (ROWS, LANES), 0) % LINES
                tile = jnp.zeros((8, LANES), F32)
                for kk in range(2):
                    tile += placed(over_lines(jnp.where(mod == zl * 2 + kk, value, 0.0)), 4 * kk)
                sendt[...] = tile

                def tile_copy(dx, kk):
                    return send(
                        sendt, recvt.at[p], st.at[0], rt.at[0],
                        dev(p_keep, (x + dx) % nx, z, h, kk),
                    )

                for dx in (2, 1, 3):
                    for kk in range(2):
                        start(functools.partial(tile_copy, dx, kk), keeper)
            else:
                sendn[...] = placed(over_lines(value * value)) + placed(over_lines(value * u[1, y]), 4)

                def sums_copy(dx, j, kk):
                    jh, jp = near[j]
                    return send(
                        sendn, recvn.at[x * 4 + y], sn.at[kk], rn.at[0],
                        dev((p + jp) % 2, (x + dx) % nx, z, (h + jh) % 2, kk),
                    )

                for dx in (2, 1, 3, 0):
                    for j in (3, 2, 1, 0):
                        for kk in range(2):
                            if (dx, j, kk) != (0, 0, 1):
                                start(functools.partial(sums_copy, dx, j, kk))
                recvn[x * 4 + y] = sendn[...]
                send3[1] = value

            def chunk_copy(j, kk):
                jh, jp = near[j]
                return send(
                    send3.at[step], recv3.at[step * 4 + y], s3.at[step], r3.at[step * 4 + y],
                    dev((p + jp) % 2, x, z, (h + jh) % 2, kk),
                )

            for j in (3, 2, 1, 0):
                for kk in range(2):
                    if (j, kk) != (0, 1):
                        start(functools.partial(chunk_copy, j, kk))
            recv3[step * 4 + y] = send3[step]

        def ratio_of(at):
            whole = recvx[at * nx]
            for xx in range(1, nx):
                whole += recvx[at * nx + xx]
            whole = jnp.broadcast_to(jnp.sum(whole, axis=1, keepdims=True), (8, LANES))
            return [whole[q : q + 1] / norms[q] for q in range(POLS)]

    @pl.when(jnp.logical_not(owner))
    def _():
        arrived(recvx.at[pl.ds(nx, nx)], rx.at[1])

    ratio = ratio_of(1)
    norm1 = [ratio[q] * norms[q] for q in range(POLS)]
    either(
        owner,
        lambda: arrived(recvn.at[pl.ds(0, 4 * nx - 1)], rn.at[0]),
        lambda: arrived(recvn.at[pl.ds(0, 4 * nx)], rn.at[0]),
    )
    whole = recvn[0]
    for c in range(1, 4 * nx):
        whole += recvn[c]
    whole = jnp.broadcast_to(jnp.sum(whole, axis=1, keepdims=True), (8, LANES))
    shift = [whole[4 + q : 5 + q] / norm1[q] for q in range(POLS)]
    norm2 = [whole[q : q + 1] - shift[q] * whole[4 + q : 5 + q] for q in range(POLS)]
    inverse = spread([1.0 / jnp.sqrt(t) for t in norm2])
    back = spread(shift)
    for jh, jp in near:
        c = (h + jh) % 2 * 2 + (p + jp) % 2
        hear = functools.partial(arrived, recv3.at[4 + c], r3.at[4 + c])
        if (jh, jp) == (0, 0):
            pl.when(jnp.logical_not(owner))(hear)
        else:
            hear()
    for c in range(4):
        value = (recv3[4 + c] - back * u[1, c]) * inverse
        for q in range(POLS):
            for t in range(LINES):
                at = ((t // 2) * 8 + (c // 2) * 4 + (t % 2) * 2 + c % 2) * LANES
                last_ref[q : q + 1, at : at + LANES] = value[LINES * q + t : LINES * q + t + 1, :]
    for q in range(POLS):
        alpha_ref[0:1, q : q + 1] = alpha[q][:, :1]
        alpha_ref[1:2, q : q + 1] = (alpha[q] + shift[q])[:, :1]
        beta_ref[0:1, q : q + 1] = jnp.sqrt(ratio[q])[:, :1]
        beta_ref[1:2, q : q + 1] = jnp.sqrt(norm2[q] / norm1[q])[:, :1]
    finish()


def write_out(*refs):
    sources, targets, sems = refs[:3], refs[3:6], refs[6]
    copies = [pltpu.make_async_copy(a, b, sems.at[i]) for i, (a, b) in enumerate(zip(sources, targets, strict=True))]
    for c in copies:
        c.start()
    for c in copies:
        c.wait()


def lanczos(sizes, kernel_half, dipole, band_energy, core_energy, core_index):
    nx, nz, _ = sizes
    rows, cols = kernel_half.shape
    dma = pltpu.SemaphoreType.DMA
    chunk = (ROWS, LANES)
    longer = (ROWS + 8, LANES)
    tile = (8, LANES)
    results = pl.pallas_call(
        functools.partial(kernel, sizes),
        out_shape=(pltpu.VMEM((2, POLS), F32), pltpu.VMEM((2, POLS), F32), pltpu.VMEM(dipole.shape, F32)),
        in_specs=[pl.BlockSpec(memory_space=pl.ANY)] * 5,
        out_specs=[pl.BlockSpec(memory_space=pltpu.VMEM)] * 3,
        scratch_shapes=[
            pltpu.VMEM((rows, cols), BF),
            pltpu.VMEM((cols, rows), BF),
            pltpu.VMEM(dipole.shape, F32),
            pltpu.VMEM(band_energy.shape, F32),
            pltpu.SMEM(core_energy.shape, F32),
            pltpu.SMEM(core_index.shape, jnp.int32),
            pltpu.VMEM((POLS, cols), F32),
            pltpu.VMEM((2, 4, *chunk), F32),
            pltpu.VMEM((4, *tile), F32),
            pltpu.VMEM((2, 4, *longer), F32),
            pltpu.VMEM((2 * 8, *longer), F32),
            pltpu.VMEM((2, 2, *tile), F32),
            pltpu.VMEM((2 * nx * 2, *tile), F32),
            pltpu.VMEM((2, *longer), F32),
            pltpu.VMEM((2 * nz, *longer), F32),
            pltpu.VMEM((2, *chunk), F32),
            pltpu.VMEM((2 * 4, *chunk), F32),
            pltpu.VMEM(tile, F32),
            pltpu.VMEM((2, *tile), F32),
            pltpu.VMEM((2, *tile), F32),
            pltpu.VMEM((2 * nx, *tile), F32),
            pltpu.VMEM(tile, F32),
            pltpu.VMEM((nx * 4, *tile), F32),
            dma((3,)), dma((2,)),
            dma((1,)), dma((1,)),
            dma((1,)), dma((2,)),
            dma((1,)), dma((2,)),
            dma((1,)), dma((2,)),
            dma((2,)), dma((8,)),
            dma((1,)), dma((1,)),
            dma((1,)), dma((2,)),
            dma((2,)), dma((1,)),
            pltpu.SemaphoreType.REGULAR, pltpu.SemaphoreType.REGULAR((3,)),
        ],
        compiler_params=pltpu.CompilerParams(collective_id=0, has_side_effects=True),
    )(kernel_half, dipole, band_energy, core_energy, core_index)
    alphas, betas, last = pl.pallas_call(
        write_out,
        out_shape=(
            jax.ShapeDtypeStruct((2, POLS), F32),
            jax.ShapeDtypeStruct((2, POLS), F32),
            jax.ShapeDtypeStruct(dipole.shape, F32),
        ),
        in_specs=[pl.BlockSpec(memory_space=pltpu.VMEM)] * 3,
        out_specs=[pl.BlockSpec(memory_space=pl.ANY)] * 3,
        scratch_shapes=[dma((3,))],
    )(*[pltpu.with_memory_space_constraint(r, pltpu.VMEM) for r in results])
    return alphas.T, betas.T, last


def solution(mesh):
    nx, np_, nz = mesh.shape["row"], mesh.shape["pol"], mesh.shape["col"] // 4
    sizes = (nx, nz, nz * np_ // nx)
    in_specs = (P("row", ("pol", "col")), P(None, "row"), P("row", None), P(), P("row"))
    out_specs = (P(), P(), P(None, "row"))
    return jax.shard_map(
        functools.partial(lanczos, sizes), mesh=mesh, in_specs=in_specs, out_specs=out_specs, check_vma=False
    )
```

```python
import functools

import jax
import jax.numpy as jnp
from jax import lax
from jax.experimental import pallas as pl
from jax.experimental.pallas import tpu as pltpu
from jax.sharding import PartitionSpec as P

F32 = jnp.float32
BF = jnp.bfloat16
MESH = pl.DeviceIdType.MESH
CORES = 4
LANES = 128
POLS = 3
LINES = 8
ROWS = POLS * LINES


def spread(parts):
    return jnp.concatenate([jnp.broadcast_to(t, (LINES, t.shape[1])) for t in parts], axis=0)


def over_lines(x):
    return [jnp.sum(x[LINES * q : LINES * (q + 1)], axis=0, keepdims=True) for q in range(POLS)]


def placed(parts, first=0):
    row = lax.broadcasted_iota(jnp.int32, (8, LANES), 0)
    out = jnp.zeros((8, LANES), F32)
    for q, part in enumerate(parts):
        out = jnp.where(row == first + q, jnp.broadcast_to(part, (8, LANES)), out)
    return out


def two_terms(x):
    high = x.astype(BF).astype(F32)
    return jnp.concatenate([high, x - high], axis=0).astype(BF)


def joined(x):
    return x[:ROWS] + x[ROWS:]


def kernel(
    sizes,
    w_hbm, dip_hbm, band_hbm, core_hbm, index_hbm,
    alpha_ref, beta_ref, last_ref,
    w, wt, wb, wtb, colb, dip, band, core, index,
    uc0, u, en,
    send1, recv1, sendc, recvc, send2, recv2, send3, recv3, sendt, recvt, sendx, recvx, sendn, recvn,
    load_sem, core_sem, s0, r0, s1, r1, sc, rc, s2, r2, s3, r3, st, rt, sx, rx, sn, rn, known, rounds, sb, rb,
):
    nx, nz, zl_count = sizes
    zh_count = nz // zl_count
    p = lax.axis_index("pol")
    x = lax.axis_index("row")
    col = lax.axis_index("col")
    z = col // 4
    h = (col // 2) % 2
    k = col % 2
    y = h * 2 + p
    zl = z % zl_count
    home = p * zh_count + z // zl_count
    is_home = x == home
    away = jnp.logical_not(is_home)
    owner = k == 1
    keeper = (z // zl_count) == (x % zh_count)
    p_keep = x // zh_count

    def dev(pp, xx, zz, hh, kk):
        return (pp, xx, zz * 4 + hh * 2 + kk)

    barrier = pltpu.get_barrier_semaphore()
    far_first = sorted(range(1, nz), key=lambda d: -min(d, nz - d))
    near = [(0, 0), (0, 1), (1, 1), (1, 0)]

    def signal(sem, d):
        pl.semaphore_signal(sem, inc=1, device_id=d, device_id_type=MESH)

    def member(jh, jp, kk):
        return dev((p + jp) % 2, x, z, (h + jh) % 2, kk)

    def above_and_below(sem):
        for d in (1, nz - 1):
            signal(sem, dev(p, x, (z + d) % nz, h, 1))

    for dx in (2, 1, 3):
        signal(barrier, dev(p, (x + dx) % nx, z, h, 1))
    for jh, jp in near[:0:-1]:
        signal(barrier, member(jh, jp, 1))
    signal(barrier, dev(p, x, z, h, 1 - k))

    @pl.when(owner)
    def _():
        for dx in (2, 1, 3):
            signal(barrier, dev(p, (x + dx) % nx, z, h, 0))
        for jh, jp in near[:0:-1]:
            signal(barrier, member(jh, jp, 0))
        above_and_below(barrier)

    loads = [
        pltpu.make_async_copy(dip_hbm, dip, load_sem.at[0]),
        pltpu.make_async_copy(band_hbm, band, load_sem.at[1]),
        pltpu.make_async_copy(core_hbm, core, core_sem.at[0]),
        pltpu.make_async_copy(index_hbm, index, core_sem.at[1]),
    ]
    for c in loads:
        c.start()
    big = w.shape[0] // 4
    w_loads = [
        pltpu.make_async_copy(
            w_hbm.at[pl.ds(i * big, big)], w.at[pl.ds(i * big, big)], load_sem.at[2]
        )
        for i in range(4)
    ]
    for c in w_loads:
        c.start()

    def start(copy, condition=None):
        if condition is None:
            copy().start()
        else:
            pl.when(condition)(lambda: copy().start())

    def send(src, dst, send_sem, recv_sem, device):
        return pltpu.make_async_remote_copy(
            src_ref=src, dst_ref=dst, send_sem=send_sem, recv_sem=recv_sem, device_id=device,
            device_id_type=MESH,
        )

    me = dev(p, x, z, h, k)

    def arrived(dst, recv_sem):
        send(dst, dst, s1.at[0], recv_sem, me).wait_recv()

    def left_here(src, send_sem):
        send(src, src, send_sem, r1.at[0], me).wait_send()

    def either(condition, then, other):
        pl.when(condition)(then)
        pl.when(jnp.logical_not(condition))(other)

    def finish():
        @pl.when(owner)
        def _():
            @pl.when(is_home)
            def _():
                left_here(dip.at[:, pl.ds(0, 6 * 4 * LANES)], s0.at[0])

            @pl.when(keeper)
            def _():
                left_here(recvc.at[pl.ds(0, 3)], st.at[0])

            left_here(recv2.at[pl.ds(0, 2 * (nz - 1))], s2.at[0])
            for step in range(2):
                left_here(recv3.at[pl.ds(0, 7)], s3.at[step])
                left_here(recvn.at[pl.ds(0, 16 - step)], sn.at[step])
            left_here(recvc.at[pl.ds(0, 14)], sx.at[0])

        either(
            owner,
            lambda: left_here(recv1.at[pl.ds(0, 6)], s1.at[0]),
            lambda: left_here(recv1.at[pl.ds(0, 4)], s1.at[0]),
        )

        @pl.when(jnp.logical_not(owner))
        def _():
            left_here(w, sb.at[0])
            left_here(wt, sb.at[1])
            left_here(sendc.at[0], sb.at[2])

        either(
            jnp.logical_or(jnp.logical_not(owner), is_home),
            lambda: left_here(recvc.at[pl.ds(0, 2)], sc.at[0]),
            lambda: left_here(recvc.at[pl.ds(0, 4)], sc.at[0]),
        )

    loads[0].wait()
    pl.semaphore_wait(barrier, jnp.where(owner, 7 + 2 * (nx - 1) + 2, 4 + nx - 1))

    @pl.when(owner)
    def _():
        for jh, jp in near[:0:-1]:
            for kk in range(2):
                signal(known, member(jh, jp, kk))
        signal(known, dev(p, x, z, h, 0))
        above_and_below(rounds.at[0])

    chip_lines = pl.ds(pl.multiple_of((zl * 2 + h) * 4 * LANES, 4 * LANES), 4 * LANES)

    def first_copy(dx, kk):
        return send(
            dip.at[:, chip_lines], uc0, s0.at[0], r0.at[0], dev(p, (x + dx) % nx, z, h, kk)
        )

    for dx in (2, 1, 3):
        for kk in range(2):
            start(functools.partial(first_copy, dx, kk), jnp.logical_and(is_home, owner))

    @pl.when(is_home)
    def _():
        uc0[...] = dip[:, chip_lines]

    for c in loads[1:]:
        c.wait()
    for c in range(4):
        for q in range(POLS):
            for t in range(LINES):
                at = ((t // 2) * 8 + (c // 2) * 4 + (t % 2) * 2 + c % 2) * LANES
                u[0, c, LINES * q + t : LINES * q + t + 1, :] = dip[q : q + 1, at : at + LANES]
    offsets = []
    for i in range(2 * CORES):
        level = index[i]
        off = jnp.float32(0.0)
        for j in range(CORES):
            off = jnp.where(level == j, core[j], off)
        offsets.append(off)
    row8 = lax.broadcasted_iota(jnp.int32, (8, LANES), 0)
    for c in range(4):
        value = jnp.zeros((8, LANES), F32)
        for t in range(LINES):
            line = (t // 2) * 8 + (c // 2) * 4 + (t % 2) * 2 + c % 2
            at = (line % 4) * LANES
            level = band[line // 16 : line // 16 + 1, at : at + LANES] - offsets[line // 4]
            value = jnp.where(row8 == t, jnp.broadcast_to(level, (8, LANES)), value)
        en[c] = value

    pltpu.make_async_copy(w_hbm, w, load_sem.at[2]).wait()

    row_mod = lax.broadcasted_iota(jnp.int32, (ROWS, 2 * LANES), 0) % LINES

    def line_rows(hh, pp, t):
        line = (t // 2) * 8 + hh * 4 + (t % 2) * 2 + pp
        return pl.ds(pl.multiple_of(line * LANES, LANES), LANES)

    def columns_of(left, block, hh, pp):
        out = jnp.zeros((ROWS, 2 * LANES), F32)
        for t in range(LINES):
            part = joined(jnp.dot(left, block[line_rows(hh, pp, t), :], preferred_element_type=F32))
            out = jnp.where(row_mod == t, part, out)
        return out

    def send_columns(step, tiles):
        slot = x * 2 + k if step == 0 else 2 * nx + x
        for half in range(2):
            sendc[step, half] = tiles[half]

        def col_copy(half):
            return send(
                sendc.at[step, half], recvc.at[slot], sc.at[0], rc.at[step], dev(half, home, z, h, 1)
            )

        for half in range(2):
            mine = jnp.logical_and(owner, jnp.logical_and(is_home, p == half))

            @pl.when(mine)
            def _(half=half):
                recvc[slot] = sendc[step, half]

            start(functools.partial(col_copy, half), jnp.logical_not(mine))

    def half_of(lines, half):
        return [t[:, half * LANES : (half + 1) * LANES] for t in lines]

    def transpose():
        @pl.loop(0, w.shape[0] // LANES)
        def _(i):
            source = pl.ds(pl.multiple_of(i * LANES, LANES), LANES)
            target = pl.ds(pl.multiple_of((i // 8 * 2 + i // 2 % 2) * LANES, LANES), LANES)
            wt[i // 4 % 2 * 2 + i % 2, :, target] = w[source, :].T

    def first_sums():
        whole = recvx[0]
        for xx in range(1, nx):
            whole += recvx[xx]
        whole = jnp.broadcast_to(jnp.sum(whole, axis=1, keepdims=True), (8, LANES))
        norms = [whole[q : q + 1] for q in range(POLS)]
        return norms, [whole[4 + q : 5 + q] / norms[q] for q in range(POLS)]

    def line_tile(value):
        mod = lax.broadcasted_iota(jnp.int32, (ROWS, LANES), 0) % LINES
        tile = jnp.zeros((8, LANES), F32)
        for kk in range(2):
            tile += placed(over_lines(jnp.where(mod == zl * 2 + kk, value, 0.0)), 4 * kk)
        return tile

    alpha = col_first = norms = None
    for step in range(2):
        def row_copy(j, step=step):
            jh, jp = near[j]
            return send(
                send1.at[step, j], recv1.at[y * 2 + k if step == 0 else 8 + y], s1.at[0], r1.at[step],
                member(jh, jp, 1),
            )

        def first_products():
            sums = jnp.zeros((ROWS, 2 * LANES), F32)
            for c in range(4):
                sums += columns_of(two_terms(u[0, c]), w, c // 2, c % 2)
            col_part = over_lines(sums)

            pl.when(away)(functools.partial(arrived, uc0, r0.at[0]))
            mine = pl.ds(pl.multiple_of(k * 2 * LANES, 2 * LANES), 2 * LANES)
            column = [uc0[q : q + 1, mine] for q in range(POLS)]
            pl.semaphore_wait(known, jnp.where(owner, 3, 4))
            send_columns(0, [placed(half_of(col_part, half)) for half in range(2)])

            @pl.when(owner)
            def _():
                pl.semaphore_wait(rounds.at[0], 2)
                above_and_below(rounds.at[1])

            twice = []
            for q in range(POLS):
                line = 2.0 * col_part[q] * column[q]
                twice.append(line[:, :LANES] + line[:, LANES:])
            sum_rows = placed(twice)
            left = two_terms(spread(column))

            for j in (3, 2, 1, 0):
                jh, jp = near[j]
                hh, pp = (h + jh) % 2, (p + jp) % 2
                lines = jnp.zeros((ROWS, LANES), F32)
                for t in range(LINES):
                    part = joined(
                        lax.dot_general(
                            left, w[line_rows(hh, pp, t), :], (((1,), (1,)), ((), ())),
                            preferred_element_type=F32,
                        )
                    )
                    lines = jnp.where(row_mod[:, :LANES] == t, part, lines)
                send1[0, j, :ROWS] = lines
                send1[0, j, ROWS:] = sum_rows
                start(functools.partial(row_copy, j), None if j else jnp.logical_not(owner))
            return col_part

        def chip_copy(i):
            src, dst = ((w, wb), (wt, wtb), (sendc.at[0], colb))[i]
            return send(src, dst, sb.at[i], rb.at[i], dev(p, x, z, h, 1))

        def second_products(col_first):
            for i, dst in enumerate((wb, wtb, colb)):
                arrived(dst, rb.at[i])
            sums = [jnp.zeros((ROWS, 2 * LANES), F32)] * 2

            def add_chunk(jh, jp):
                hh, pp = (h + jh) % 2, (p + jp) % 2
                if (jh, jp) != (0, 0):
                    arrived(recv3.at[hh * 2 + pp], r3.at[hh * 2 + pp])
                left = two_terms(recv3[hh * 2 + pp])
                for b, block in enumerate((wb, w)):
                    sums[b] = sums[b] + columns_of(left, block, hh, pp)

            for jh, jp in near[:3]:
                add_chunk(jh, jp)
            arrived(recvx.at[pl.ds(0, nx - 1)], rx.at[0])
            _, alpha = first_sums()
            add_chunk(*near[3])
            before = [
                [jnp.concatenate([colb[0, q : q + 1], colb[1, q : q + 1]], axis=1) for q in range(POLS)],
                col_first,
            ]
            parts = []
            for b in range(2):
                part = over_lines(sums[b])
                parts.append([part[q] - alpha[q][:, :1] * before[b][q] for q in range(POLS)])
            send_columns(
                1, [placed(half_of(parts[0], half)) + placed(half_of(parts[1], half), 4) for half in range(2)]
            )

            @pl.when(is_home)
            def _():
                for half in range(2):
                    recvt[half] = line_tile(recv3[h * 2 + half])

            pl.when(away)(functools.partial(arrived, recvt, rt.at[0]))
            lefts = []
            for b in range(2):
                mine = slice(b * 2 * LANES, (b + 1) * 2 * LANES)
                column = []
                for q in range(POLS):
                    at = slice(4 * b + q, 4 * b + q + 1)
                    got = jnp.concatenate([recvt[0, at], recvt[1, at]], axis=1)
                    column.append(got - alpha[q][:, :1] * uc0[q : q + 1, mine])
                lefts.append(two_terms(spread(column)))
            for j in (3, 2, 1, 0):
                jh, jp = near[j]
                c = (h + jh) % 2 * 2 + (p + jp) % 2
                wide = joined(
                    jnp.dot(lefts[0], wtb[c], preferred_element_type=F32)
                    + jnp.dot(lefts[1], wt[c], preferred_element_type=F32)
                )
                lines = jnp.zeros((ROWS, LANES), F32)
                for t in range(LINES):
                    lines = jnp.where(row_mod[:, :LANES] == t, wide[:, t * LANES : (t + 1) * LANES], lines)
                send1[1, j, :ROWS] = lines
                send1[1, j, ROWS:] = jnp.zeros((8, LANES), F32)
                if j:
                    start(functools.partial(row_copy, j))

        if step == 0:
            col_first = first_products()
        else:

            def only_wait():
                for c in range(4):
                    arrived(recv3.at[c], r3.at[c])
                arrived(recvx.at[pl.ds(0, nx)], rx.at[0])

            either(owner, lambda: second_products(col_first), only_wait)
            norms, alpha = first_sums()

        if step == 1:
            factor = spread(alpha)
            for c in range(4):
                u[1, c] = recv3[c] - factor * u[0, c]
        squares = jnp.zeros((ROWS, LANES), F32)
        weighted = jnp.zeros((ROWS, LANES), F32)
        for c in range(4):
            sq = u[step, c] * u[step, c]
            squares += sq
            weighted += jnp.concatenate([en[c]] * POLS, axis=0) * sq
        own_sums = placed(over_lines(squares))

        def x_copy(dx, kk, at):
            return send(
                sendx.at[at], recvx.at[at * nx + x], sx.at[0], rx.at[at],
                dev(p, (x + dx) % nx, z, h, kk),
            )

        def share(at):
            for dx in (2, 1, 3):
                for kk in range(2):
                    start(functools.partial(x_copy, dx, kk, at))
            start(functools.partial(x_copy, 0, 0, at))
            recvx[at * nx + x] = sendx[at]

        if step == 0:
            own_sums += placed(over_lines(weighted), 4)

        if step == 0:

            @pl.when(jnp.logical_not(owner))
            def _():
                chip_copy(2).start()
                chip_copy(0).start()
                transpose()
                chip_copy(1).start()

        @pl.when(owner)
        def _(step=step, own_sums=own_sums):
            if step == 0:
                pl.semaphore_wait(rounds.at[1], 2)
                above_and_below(rounds.at[2])
            if step == 1:
                sendx[1] = own_sums
                share(1)
            recv1[y * 2 + k if step == 0 else 8 + y] = send1[step, 0]
            members = 4 if step else 8
            arrived(recv1.at[pl.ds(step * 8, members - 1)], r1.at[step])
            total = recv1[step * 8]
            for g in range(1, members):
                total += recv1[step * 8 + g]
            send2[step] = total

            @pl.when(keeper)
            def _():
                base, many = (0, 2 * nx) if step == 0 else (2 * nx, nx)
                either(
                    p == p_keep,
                    lambda: arrived(recvc.at[pl.ds(base, many - 1)], rc.at[step]),
                    lambda: arrived(recvc.at[pl.ds(base, many)], rc.at[step]),
                )
                for kk in range(2):
                    slots = [base + 2 * xx + kk if step == 0 else base + xx for xx in range(nx)]
                    cols = recvc[slots[0]]
                    for slot in slots[1:]:
                        cols += recvc[slot]
                    first = 0 if step == 0 else 4 * kk
                    for q in range(POLS):
                        at = pl.ds(LINES * q, LINES)
                        line = jnp.broadcast_to(cols[first + q : first + q + 1], (8, LANES))
                        send2[step, at] = send2[step, at] + jnp.where(row8 == zl * 2 + kk, line, 0.0)

            if step == 0:
                pl.semaphore_wait(rounds.at[2], 2)
            def z_copy(d):
                return send(
                    send2.at[step], recv2.at[step * nz + z], s2.at[0], r2.at[step],
                    dev(p, x, (z + d) % nz, h, 1),
                )

            for d in far_first:
                start(functools.partial(z_copy, d))
            recv2[step * nz + z] = send2[step]
            rest = jnp.concatenate([en[y]] * POLS, axis=0) * u[step, y]
            if step == 0:
                transpose()
            else:
                arrived(recvx.at[pl.ds(nx, nx - 1)], rx.at[1])
                rest = rest - spread(alpha) * u[1, y] - spread(ratio_of(1)) * u[0, y]
            arrived(recv2.at[pl.ds(step * nz, nz - 1)], r2.at[step])
            total = recv2[step * nz]
            for zz in range(1, nz):
                total += recv2[step * nz + zz]
            value = total[:ROWS] + rest

            if step == 0:
                sendx[0] = jnp.concatenate([total[ROWS + 4 :], total[ROWS : ROWS + 4]], axis=0) + own_sums
                share(0)
                send3[0] = value
                sendt[...] = line_tile(value)

                def tile_copy(dx):
                    return send(
                        sendt, recvt.at[p], st.at[0], rt.at[0], dev(p_keep, (x + dx) % nx, z, h, 1)
                    )

                for dx in (2, 1, 3):
                    start(functools.partial(tile_copy, dx), keeper)
            else:
                sendn[...] = placed(over_lines(value * value)) + placed(over_lines(value * u[1, y]), 4)

                def sums_copy(dx, j, kk):
                    jh, jp = near[j]
                    return send(
                        sendn, recvn.at[x * 4 + y], sn.at[kk], rn.at[0],
                        dev((p + jp) % 2, (x + dx) % nx, z, (h + jh) % 2, kk),
                    )

                for dx in (2, 1, 3, 0):
                    for j in (3, 2, 1, 0):
                        for kk in range(2):
                            if (dx, j, kk) != (0, 0, 1):
                                start(functools.partial(sums_copy, dx, j, kk))
                recvn[x * 4 + y] = sendn[...]
                send3[1] = value

            def chunk_copy(j, kk):
                jh, jp = near[j]
                return send(
                    send3.at[step], recv3.at[step * 4 + y], s3.at[step], r3.at[step * 4 + y],
                    dev((p + jp) % 2, x, z, (h + jh) % 2, kk),
                )

            for j in (3, 2, 1, 0):
                for kk in range(2):
                    if (j, kk) != (0, 1):
                        start(functools.partial(chunk_copy, j, kk))
            recv3[step * 4 + y] = send3[step]

        def ratio_of(at):
            whole = recvx[at * nx]
            for xx in range(1, nx):
                whole += recvx[at * nx + xx]
            whole = jnp.broadcast_to(jnp.sum(whole, axis=1, keepdims=True), (8, LANES))
            return [whole[q : q + 1] / norms[q] for q in range(POLS)]

    @pl.when(jnp.logical_not(owner))
    def _():
        arrived(recvx.at[pl.ds(nx, nx)], rx.at[1])

    ratio = ratio_of(1)
    norm1 = [ratio[q] * norms[q] for q in range(POLS)]
    either(
        owner,
        lambda: arrived(recvn.at[pl.ds(0, 4 * nx - 1)], rn.at[0]),
        lambda: arrived(recvn.at[pl.ds(0, 4 * nx)], rn.at[0]),
    )
    whole = recvn[0]
    for c in range(1, 4 * nx):
        whole += recvn[c]
    whole = jnp.broadcast_to(jnp.sum(whole, axis=1, keepdims=True), (8, LANES))
    shift = [whole[4 + q : 5 + q] / norm1[q] for q in range(POLS)]
    norm2 = [whole[q : q + 1] - shift[q] * whole[4 + q : 5 + q] for q in range(POLS)]
    inverse = spread([1.0 / jnp.sqrt(t) for t in norm2])
    back = spread(shift)
    for jh, jp in near:
        c = (h + jh) % 2 * 2 + (p + jp) % 2
        hear = functools.partial(arrived, recv3.at[4 + c], r3.at[4 + c])
        if (jh, jp) == (0, 0):
            pl.when(jnp.logical_not(owner))(hear)
        else:
            hear()
    for c in range(4):
        value = (recv3[4 + c] - back * u[1, c]) * inverse
        for q in range(POLS):
            for t in range(LINES):
                at = ((t // 2) * 8 + (c // 2) * 4 + (t % 2) * 2 + c % 2) * LANES
                last_ref[q : q + 1, at : at + LANES] = value[LINES * q + t : LINES * q + t + 1, :]
    for q in range(POLS):
        alpha_ref[0:1, q : q + 1] = alpha[q][:, :1]
        alpha_ref[1:2, q : q + 1] = (alpha[q] + shift[q])[:, :1]
        beta_ref[0:1, q : q + 1] = jnp.sqrt(ratio[q])[:, :1]
        beta_ref[1:2, q : q + 1] = jnp.sqrt(norm2[q] / norm1[q])[:, :1]
    finish()


def write_out(*refs):
    sources, targets, sems = refs[:3], refs[3:6], refs[6]
    copies = [pltpu.make_async_copy(a, b, sems.at[i]) for i, (a, b) in enumerate(zip(sources, targets, strict=True))]
    for c in copies:
        c.start()
    for c in copies:
        c.wait()


def lanczos(sizes, kernel_half, dipole, band_energy, core_energy, core_index):
    nx, nz, _ = sizes
    rows, cols = kernel_half.shape
    dma = pltpu.SemaphoreType.DMA
    chunk = (ROWS, LANES)
    longer = (ROWS + 8, LANES)
    tile = (8, LANES)
    results = pl.pallas_call(
        functools.partial(kernel, sizes),
        out_shape=(pltpu.VMEM((2, POLS), F32), pltpu.VMEM((2, POLS), F32), pltpu.VMEM(dipole.shape, F32)),
        in_specs=[pl.BlockSpec(memory_space=pl.ANY)] * 5,
        out_specs=[pl.BlockSpec(memory_space=pltpu.VMEM)] * 3,
        scratch_shapes=[
            pltpu.VMEM((rows, cols), BF),
            pltpu.VMEM((4, cols, LINES * LANES), BF),
            pltpu.VMEM((rows, cols), BF),
            pltpu.VMEM((4, cols, LINES * LANES), BF),
            pltpu.VMEM((2, *tile), F32),
            pltpu.VMEM(dipole.shape, F32),
            pltpu.VMEM(band_energy.shape, F32),
            pltpu.SMEM(core_energy.shape, F32),
            pltpu.SMEM(core_index.shape, jnp.int32),
            pltpu.VMEM((POLS, 2 * cols), F32),
            pltpu.VMEM((2, 4, *chunk), F32),
            pltpu.VMEM((4, *tile), F32),
            pltpu.VMEM((2, 4, *longer), F32),
            pltpu.VMEM((2 * 8, *longer), F32),
            pltpu.VMEM((2, 2, *tile), F32),
            pltpu.VMEM((2 * nx * 2, *tile), F32),
            pltpu.VMEM((2, *longer), F32),
            pltpu.VMEM((2 * nz, *longer), F32),
            pltpu.VMEM((2, *chunk), F32),
            pltpu.VMEM((2 * 4, *chunk), F32),
            pltpu.VMEM(tile, F32),
            pltpu.VMEM((2, *tile), F32),
            pltpu.VMEM((2, *tile), F32),
            pltpu.VMEM((2 * nx, *tile), F32),
            pltpu.VMEM(tile, F32),
            pltpu.VMEM((nx * 4, *tile), F32),
            dma((3,)), dma((2,)),
            dma((1,)), dma((1,)),
            dma((1,)), dma((2,)),
            dma((1,)), dma((2,)),
            dma((1,)), dma((2,)),
            dma((2,)), dma((8,)),
            dma((1,)), dma((1,)),
            dma((1,)), dma((2,)),
            dma((2,)), dma((1,)),
            pltpu.SemaphoreType.REGULAR, pltpu.SemaphoreType.REGULAR((3,)),
            dma((3,)), dma((3,)),
        ],
        compiler_params=pltpu.CompilerParams(collective_id=0, has_side_effects=True),
    )(kernel_half, dipole, band_energy, core_energy, core_index)
    alphas, betas, last = pl.pallas_call(
        write_out,
        out_shape=(
            jax.ShapeDtypeStruct((2, POLS), F32),
            jax.ShapeDtypeStruct((2, POLS), F32),
            jax.ShapeDtypeStruct(dipole.shape, F32),
        ),
        in_specs=[pl.BlockSpec(memory_space=pltpu.VMEM)] * 3,
        out_specs=[pl.BlockSpec(memory_space=pl.ANY)] * 3,
        scratch_shapes=[dma((3,))],
    )(*[pltpu.with_memory_space_constraint(r, pltpu.VMEM) for r in results])
    return alphas.T, betas.T, last


def solution(mesh):
    nx, np_, nz = mesh.shape["row"], mesh.shape["pol"], mesh.shape["col"] // 4
    sizes = (nx, nz, nz * np_ // nx)
    in_specs = (P("row", ("pol", "col")), P(None, "row"), P("row", None), P(), P("row"))
    out_specs = (P(), P(), P(None, "row"))
    return jax.shard_map(
        functools.partial(lanczos, sizes), mesh=mesh, in_specs=in_specs, out_specs=out_specs, check_vma=False
    )
```

```python
import functools

import jax
import jax.numpy as jnp
from jax import lax
from jax.experimental import pallas as pl
from jax.experimental.pallas import tpu as pltpu
from jax.sharding import PartitionSpec as P

F32 = jnp.float32
BF = jnp.bfloat16
MESH = pl.DeviceIdType.MESH
CORES = 4
LANES = 128
POLS = 3
LINES = 8
ROWS = POLS * LINES


def spread(parts):
    return jnp.concatenate([jnp.broadcast_to(t, (LINES, t.shape[1])) for t in parts], axis=0)


def over_lines(x):
    return [jnp.sum(x[LINES * q : LINES * (q + 1)], axis=0, keepdims=True) for q in range(POLS)]


def placed(parts, first=0):
    row = lax.broadcasted_iota(jnp.int32, (8, LANES), 0)
    out = jnp.zeros((8, LANES), F32)
    for q, part in enumerate(parts):
        out = jnp.where(row == first + q, jnp.broadcast_to(part, (8, LANES)), out)
    return out


def stacked(parts):
    width = parts[0].shape[1]
    row = lax.broadcasted_iota(jnp.int32, (8, width), 0)
    a, b, c = (jnp.broadcast_to(t, (8, width)) for t in parts)
    return jnp.where(row == 0, a, jnp.where(row == 1, b, c))


def other_rows(x):
    return jnp.concatenate([x[4:], x[:4]], axis=0)


def two_terms(x):
    high = x.astype(BF).astype(F32)
    return jnp.concatenate([high, x - high], axis=0).astype(BF)


def joined(x):
    half = x.shape[0] // 2
    return x[:half] + x[half:]


def kernel(
    sizes,
    w_hbm, dip_hbm, band_hbm, core_hbm, index_hbm,
    alpha_ref, beta_ref, last_ref,
    w, wt, wb, wtb, turn, dip, band, core, index,
    uc0, u, en,
    send1, recv1, sendc, recvc, send2, recv2, send3, recv3, sendt, recvt, sendx, recvx, sendn, recvn,
    load_sem, core_sem, s0, r0, s1, r1, sc, rc, s2, r2, s3, r3, st, rt, sx, rx, sn, rn, known, rounds, sb, rb,
):
    nx, nz, zl_count = sizes
    zh_count = nz // zl_count
    p = lax.axis_index("pol")
    x = lax.axis_index("row")
    col = lax.axis_index("col")
    z = col // 4
    h = (col // 2) % 2
    k = col % 2
    y = h * 2 + p
    zl = z % zl_count
    home = p * zh_count + z // zl_count
    is_home = x == home
    away = jnp.logical_not(is_home)
    owner = k == 1
    keeper = (z // zl_count) == (x % zh_count)
    p_keep = x // zh_count

    def dev(pp, xx, zz, hh, kk):
        return (pp, xx, zz * 4 + hh * 2 + kk)

    barrier = pltpu.get_barrier_semaphore()
    far_first = sorted(range(1, nz), key=lambda d: -min(d, nz - d))
    near = [(0, 0), (0, 1), (1, 1), (1, 0)]

    def signal(sem, d):
        pl.semaphore_signal(sem, inc=1, device_id=d, device_id_type=MESH)

    def member(jh, jp, kk):
        return dev((p + jp) % 2, x, z, (h + jh) % 2, kk)

    def above_and_below(sem):
        for d in (1, nz - 1):
            signal(sem, dev(p, x, (z + d) % nz, h, 1))

    for dx in (2, 1, 3):
        signal(barrier, dev(p, (x + dx) % nx, z, h, 1))
    for jh, jp in near[:0:-1]:
        signal(barrier, member(jh, jp, 1))
    signal(barrier, dev(p, x, z, h, 1 - k))

    @pl.when(owner)
    def _():
        for dx in (2, 1, 3):
            signal(barrier, dev(p, (x + dx) % nx, z, h, 0))
        for jh, jp in near[:0:-1]:
            signal(barrier, member(jh, jp, 0))
        above_and_below(barrier)

    loads = [
        pltpu.make_async_copy(dip_hbm, dip, load_sem.at[0]),
        pltpu.make_async_copy(band_hbm, band, load_sem.at[1]),
        pltpu.make_async_copy(core_hbm, core, core_sem.at[0]),
        pltpu.make_async_copy(index_hbm, index, core_sem.at[1]),
    ]
    for c in loads:
        c.start()
    big = w.shape[0] // 4
    w_loads = [
        pltpu.make_async_copy(
            w_hbm.at[pl.ds(i * big, big)], w.at[pl.ds(i * big, big)], load_sem.at[2]
        )
        for i in range(4)
    ]
    for c in w_loads:
        c.start()

    def start(copy, condition=None):
        if condition is None:
            copy().start()
        else:
            pl.when(condition)(lambda: copy().start())

    def send(src, dst, send_sem, recv_sem, device):
        return pltpu.make_async_remote_copy(
            src_ref=src, dst_ref=dst, send_sem=send_sem, recv_sem=recv_sem, device_id=device,
            device_id_type=MESH,
        )

    me = dev(p, x, z, h, k)

    def arrived(dst, recv_sem):
        send(dst, dst, s1.at[0], recv_sem, me).wait_recv()

    def left_here(src, send_sem):
        send(src, src, send_sem, r1.at[0], me).wait_send()

    def either(condition, then, other):
        pl.when(condition)(then)
        pl.when(jnp.logical_not(condition))(other)

    def finish():
        @pl.when(owner)
        def _():
            @pl.when(is_home)
            def _():
                left_here(dip.at[:, pl.ds(0, 6 * 4 * LANES)], s0.at[0])

            @pl.when(keeper)
            def _():
                left_here(recvc.at[pl.ds(0, 3)], st.at[0])

            left_here(recv2.at[pl.ds(0, 2 * (nz - 1))], s2.at[0])
            for step in range(2):
                left_here(recv3.at[pl.ds(0, 7)], s3.at[step])
                left_here(recvn.at[pl.ds(0, 16 - step)], sn.at[step])
            left_here(recvc.at[pl.ds(0, 14)], sx.at[0])

        either(
            owner,
            lambda: left_here(recv1.at[pl.ds(0, 6)], s1.at[0]),
            lambda: left_here(recv1.at[pl.ds(0, 4)], s1.at[0]),
        )

        @pl.when(jnp.logical_not(owner))
        def _():
            left_here(w, sb.at[0])
            left_here(wt, sb.at[1])

        either(
            jnp.logical_or(jnp.logical_not(owner), is_home),
            lambda: left_here(recvc.at[pl.ds(0, 2)], sc.at[0]),
            lambda: left_here(recvc.at[pl.ds(0, 4)], sc.at[0]),
        )

    loads[0].wait()
    pl.semaphore_wait(barrier, jnp.where(owner, 7 + 2 * (nx - 1) + 2, 4 + nx - 1))

    @pl.when(owner)
    def _():
        for jh, jp in near[:0:-1]:
            for kk in range(2):
                signal(known, member(jh, jp, kk))
        signal(known, dev(p, x, z, h, 0))
        above_and_below(rounds.at[0])

    chip_lines = pl.ds(pl.multiple_of((zl * 2 + h) * 4 * LANES, 4 * LANES), 4 * LANES)

    def first_copy(dx, kk):
        return send(
            dip.at[:, chip_lines], uc0, s0.at[0], r0.at[0], dev(p, (x + dx) % nx, z, h, kk)
        )

    for dx in (2, 1, 3):
        for kk in range(2):
            start(functools.partial(first_copy, dx, kk), jnp.logical_and(is_home, owner))

    @pl.when(is_home)
    def _():
        uc0[...] = dip[:, chip_lines]

    for c in loads[1:]:
        c.wait()
    for c in range(4):
        for q in range(POLS):
            for t in range(LINES):
                at = ((t // 2) * 8 + (c // 2) * 4 + (t % 2) * 2 + c % 2) * LANES
                u[0, c, LINES * q + t : LINES * q + t + 1, :] = dip[q : q + 1, at : at + LANES]
    offsets = []
    for i in range(2 * CORES):
        level = index[i]
        off = jnp.float32(0.0)
        for j in range(CORES):
            off = jnp.where(level == j, core[j], off)
        offsets.append(off)
    row8 = lax.broadcasted_iota(jnp.int32, (8, LANES), 0)
    for c in range(4):
        value = jnp.zeros((8, LANES), F32)
        for t in range(LINES):
            line = (t // 2) * 8 + (c // 2) * 4 + (t % 2) * 2 + c % 2
            at = (line % 4) * LANES
            level = band[line // 16 : line // 16 + 1, at : at + LANES] - offsets[line // 4]
            value = jnp.where(row8 == t, jnp.broadcast_to(level, (8, LANES)), value)
        en[c] = value

    pltpu.make_async_copy(w_hbm, w, load_sem.at[2]).wait()

    line_of_row_wide = lax.broadcasted_iota(jnp.int32, (ROWS, 2 * LANES), 0) % LINES
    line_of_row = lax.broadcasted_iota(jnp.int32, (ROWS, LANES), 0) % LINES
    row8_wide = lax.broadcasted_iota(jnp.int32, (8, 2 * LANES), 0)

    def line_rows(hh, pp, t):
        line = (t // 2) * 8 + hh * 4 + (t % 2) * 2 + pp
        return pl.ds(pl.multiple_of(line * LANES, LANES), LANES)

    def columns_of(left, block, hh, pp):
        out = jnp.zeros((ROWS, 2 * LANES), F32)
        for t in range(LINES):
            part = joined(jnp.dot(left, block[line_rows(hh, pp, t), :], preferred_element_type=F32))
            out = jnp.where(line_of_row_wide == t, part, out)
        return out

    def send_columns(step, tiles):
        slot = x * 2 + k if step == 0 else 2 * nx + x
        for half in range(2):
            sendc[step, half] = tiles[half]

        def col_copy(half):
            return send(
                sendc.at[step, half], recvc.at[slot], sc.at[0], rc.at[step], dev(half, home, z, h, 1)
            )

        for half in range(2):
            mine = jnp.logical_and(owner, jnp.logical_and(is_home, p == half))

            @pl.when(mine)
            def _(half=half):
                recvc[slot] = sendc[step, half]

            start(functools.partial(col_copy, half), jnp.logical_not(mine))

    def transpose():
        side = 2 * LANES

        @pl.loop(0, w.shape[0] // side)
        def _(i):
            tile = w[pl.ds(pl.multiple_of(i * side, side), side), :].T
            at = pl.ds(pl.multiple_of((i // 4 * 2 + i % 2) * LANES, LANES), LANES)
            for pp in range(2):
                wt[i // 2 % 2 * 2 + pp, :, at] = tile[:, pp * LANES : (pp + 1) * LANES]

    def plane_sums():
        whole = recvx[0]
        for xx in range(1, nx):
            whole += recvx[xx]
        return jnp.broadcast_to(jnp.sum(whole, axis=1, keepdims=True), (8, LANES))

    def first_sums():
        whole = plane_sums()
        norms = [whole[q : q + 1] for q in range(POLS)]
        return norms, [whole[4 + q : 5 + q] / norms[q] for q in range(POLS)]

    def line_tile(value):
        mod = lax.broadcasted_iota(jnp.int32, (ROWS, LANES), 0) % LINES
        tile = jnp.zeros((8, LANES), F32)
        for kk in range(2):
            tile += placed(over_lines(jnp.where(mod == zl * 2 + kk, value, 0.0)), 4 * kk)
        return tile

    alpha = norms = None
    for step in range(2):
        def row_copy(j, step=step):
            jh, jp = near[j]
            return send(
                send1.at[step, j], recv1.at[y * 2 + k if step == 0 else 8 + y], s1.at[0], r1.at[step],
                member(jh, jp, 1),
            )

        def first_products():
            sums = jnp.zeros((ROWS, 2 * LANES), F32)
            for c in range(4):
                sums += columns_of(two_terms(u[0, c]), w, c // 2, c % 2)
            col_lines = over_lines(sums)
            col_part = stacked(col_lines)

            pl.when(away)(functools.partial(arrived, uc0, r0.at[0]))
            mine = pl.ds(pl.multiple_of(k * 2 * LANES, 2 * LANES), 2 * LANES)
            column = [uc0[q : q + 1, mine] for q in range(POLS)]
            pl.semaphore_wait(known, jnp.where(owner, 3, 4))
            send_columns(0, [col_part[:, :LANES], col_part[:, LANES:]])

            @pl.when(owner)
            def _():
                pl.semaphore_wait(rounds.at[0], 2)
                above_and_below(rounds.at[1])

            twice = []
            for q in range(POLS):
                line = 2.0 * col_lines[q] * column[q]
                twice.append(line[:, :LANES] + line[:, LANES:])
            sum_rows = placed(twice)
            left = two_terms(spread(column))

            for j in (3, 2, 1, 0):
                jh, jp = near[j]
                hh, pp = (h + jh) % 2, (p + jp) % 2
                lines = jnp.zeros((ROWS, LANES), F32)
                for t in range(LINES):
                    part = joined(
                        lax.dot_general(
                            left, w[line_rows(hh, pp, t), :], (((1,), (1,)), ((), ())),
                            preferred_element_type=F32,
                        )
                    )
                    lines = jnp.where(line_of_row == t, part, lines)
                send1[0, j, :ROWS] = lines
                send1[0, j, ROWS:] = sum_rows
                start(functools.partial(row_copy, j), None if j else jnp.logical_not(owner))

        def chip_copy(i):
            src, dst = ((w, wb), (wt, wtb))[i]
            return send(src, dst, sb.at[i], rb.at[i], dev(p, x, z, h, 1))

        def second_products():
            arrived(wb, rb.at[0])
            sums = [jnp.zeros((ROWS, 2 * LANES), F32)] * 2
            for jh, jp in near:
                hh, pp = (h + jh) % 2, (p + jp) % 2
                if (jh, jp) != (0, 0):
                    arrived(recv3.at[hh * 2 + pp], r3.at[hh * 2 + pp])
                left = two_terms(recv3[hh * 2 + pp])
                for b, block in enumerate((wb, w)):
                    sums[b] = sums[b] + columns_of(left, block, hh, pp)
            parts = [stacked(over_lines(sums[b])) for b in range(2)]
            tiles = jnp.where(row8_wide < 4, parts[0], other_rows(parts[1]))
            send_columns(1, [tiles[:, :LANES], tiles[:, LANES:]])

            @pl.when(is_home)
            def _():
                for half in range(2):
                    recvt[half] = line_tile(recv3[h * 2 + half])

            pl.when(away)(functools.partial(arrived, recvt, rt.at[0]))
            got = jnp.concatenate([recvt[0], recvt[1]], axis=1)
            lefts = [two_terms(got), two_terms(other_rows(got))]
            arrived(wtb, rb.at[1])
            for j in (3, 2, 1, 0):
                jh, jp = near[j]
                c = (h + jh) % 2 * 2 + (p + jp) % 2
                wide = joined(
                    jnp.dot(lefts[0], wtb[c], preferred_element_type=F32)
                    + jnp.dot(lefts[1], wt[c], preferred_element_type=F32)
                )
                for t in range(LINES):
                    turn[j, 8 * t : 8 * t + 8, :] = wide[:, t * LANES : (t + 1) * LANES]
                for q in range(POLS):
                    send1[1, j, LINES * q : LINES * (q + 1)] = turn[j, pl.ds(q, LINES, stride=8), :]
                send1[1, j, ROWS:] = jnp.zeros((8, LANES), F32)
                if j:
                    start(functools.partial(row_copy, j))
            arrived(recvx.at[pl.ds(0, nx - 1)], rx.at[0])

        if step == 0:
            first_products()
        else:

            def only_wait():
                for c in range(4):
                    arrived(recv3.at[c], r3.at[c])
                arrived(recvx.at[pl.ds(0, nx)], rx.at[0])

            either(owner, second_products, only_wait)
            norms, alpha = first_sums()

        if step == 1:
            factor = spread(alpha)
            for c in range(4):
                u[1, c] = recv3[c] - factor * u[0, c]
        squares = jnp.zeros((ROWS, LANES), F32)
        weighted = jnp.zeros((ROWS, LANES), F32)
        for c in range(4):
            sq = u[step, c] * u[step, c]
            squares += sq
            weighted += jnp.concatenate([en[c]] * POLS, axis=0) * sq
        own_sums = placed(over_lines(squares))

        def x_copy(dx, kk, at):
            return send(
                sendx.at[at], recvx.at[at * nx + x], sx.at[0], rx.at[at],
                dev(p, (x + dx) % nx, z, h, kk),
            )

        def share(at, kk):
            for dx in (2, 1, 3):
                start(functools.partial(x_copy, dx, kk, at))
            if kk == 0:
                start(functools.partial(x_copy, 0, 0, at))
            else:
                recvx[at * nx + x] = sendx[at]

        if step == 0:
            own_sums += placed(over_lines(weighted), 4)

        if step == 0:

            @pl.when(jnp.logical_not(owner))
            def _():
                chip_copy(0).start()
                transpose()
                chip_copy(1).start()

        @pl.when(owner)
        def _(step=step, own_sums=own_sums):
            if step == 0:
                pl.semaphore_wait(rounds.at[1], 2)
                above_and_below(rounds.at[2])
            if step == 1:
                sendx[1] = own_sums
                share(1, 1)
                share(1, 0)
            recv1[y * 2 + k if step == 0 else 8 + y] = send1[step, 0]
            members = 4 if step else 8
            arrived(recv1.at[pl.ds(step * 8, members - 1)], r1.at[step])
            total = recv1[step * 8]
            for g in range(1, members):
                total += recv1[step * 8 + g]
            send2[step] = total

            @pl.when(keeper)
            def _():
                base, many = (0, 2 * nx) if step == 0 else (2 * nx, nx)
                either(
                    p == p_keep,
                    lambda: arrived(recvc.at[pl.ds(base, many - 1)], rc.at[step]),
                    lambda: arrived(recvc.at[pl.ds(base, many)], rc.at[step]),
                )
                for kk in range(2):
                    slots = [base + 2 * xx + kk if step == 0 else base + xx for xx in range(nx)]
                    cols = recvc[slots[0]]
                    for slot in slots[1:]:
                        cols += recvc[slot]
                    first = 0 if step == 0 else 4 * kk
                    for q in range(POLS):
                        at = pl.ds(LINES * q, LINES)
                        line = jnp.broadcast_to(cols[first + q : first + q + 1], (8, LANES))
                        send2[step, at] = send2[step, at] + jnp.where(row8 == zl * 2 + kk, line, 0.0)

            if step == 0:
                pl.semaphore_wait(rounds.at[2], 2)
            def z_copy(d):
                return send(
                    send2.at[step], recv2.at[step * nz + z], s2.at[0], r2.at[step],
                    dev(p, x, (z + d) % nz, h, 1),
                )

            for d in far_first:
                start(functools.partial(z_copy, d))
            recv2[step * nz + z] = send2[step]
            rest = jnp.concatenate([en[y]] * POLS, axis=0) * u[step, y]
            if step == 0:
                transpose()
            else:
                arrived(recvx.at[pl.ds(nx, nx - 1)], rx.at[1])
                coupled = send3[0] - jnp.concatenate([en[y]] * POLS, axis=0) * u[0, y]
                rest = rest - spread(alpha) * (u[1, y] + coupled) - spread(ratio_of(1)) * u[0, y]
            arrived(recv2.at[pl.ds(step * nz, nz - 1)], r2.at[step])
            total = recv2[step * nz]
            for zz in range(1, nz):
                total += recv2[step * nz + zz]
            value = total[:ROWS] + rest

            def chunk_copy(j, kk):
                jh, jp = near[j]
                return send(
                    send3.at[step], recv3.at[step * 4 + y], s3.at[step], r3.at[step * 4 + y],
                    dev((p + jp) % 2, x, z, (h + jh) % 2, kk),
                )

            def send_chunk(j, kk):
                start(functools.partial(chunk_copy, j, kk))

            if step == 0:
                send3[0] = value
                send_chunk(3, 1)
                sendt[...] = line_tile(value)

                def tile_copy(dx):
                    return send(
                        sendt, recvt.at[p], st.at[0], rt.at[0], dev(p_keep, (x + dx) % nx, z, h, 1)
                    )

                for dx in (2, 1, 3):
                    start(functools.partial(tile_copy, dx), keeper)
                send_chunk(2, 1)
                send_chunk(1, 1)
                sendx[0] = jnp.concatenate([total[ROWS + 4 :], total[ROWS : ROWS + 4]], axis=0) + own_sums
                share(0, 1)
                for j in (3, 2, 1, 0):
                    send_chunk(j, 0)
                share(0, 0)
            else:
                sendn[...] = placed(over_lines(value * value)) + placed(over_lines(value * u[1, y]), 4)

                def sums_copy(dx, j, kk):
                    jh, jp = near[j]
                    return send(
                        sendn, recvn.at[x * 4 + y], sn.at[kk], rn.at[0],
                        dev((p + jp) % 2, (x + dx) % nx, z, (h + jh) % 2, kk),
                    )

                for dx in (2, 1, 3, 0):
                    for j in (3, 2, 1, 0):
                        for kk in range(2):
                            if (dx, j, kk) != (0, 0, 1):
                                start(functools.partial(sums_copy, dx, j, kk))
                recvn[x * 4 + y] = sendn[...]
                send3[1] = value

            if step == 1:
                for j in (3, 2, 1, 0):
                    send_chunk(j, 0)
                    if j:
                        send_chunk(j, 1)
            recv3[step * 4 + y] = send3[step]

        def ratio_of(at):
            whole = recvx[at * nx]
            for xx in range(1, nx):
                whole += recvx[at * nx + xx]
            whole = jnp.broadcast_to(jnp.sum(whole, axis=1, keepdims=True), (8, LANES))
            return [whole[q : q + 1] / norms[q] for q in range(POLS)]

    @pl.when(jnp.logical_not(owner))
    def _():
        arrived(recvx.at[pl.ds(nx, nx)], rx.at[1])

    ratio = ratio_of(1)
    norm1 = [ratio[q] * norms[q] for q in range(POLS)]
    either(
        owner,
        lambda: arrived(recvn.at[pl.ds(0, 4 * nx - 1)], rn.at[0]),
        lambda: arrived(recvn.at[pl.ds(0, 4 * nx)], rn.at[0]),
    )
    whole = recvn[0]
    for c in range(1, 4 * nx):
        whole += recvn[c]
    whole = jnp.broadcast_to(jnp.sum(whole, axis=1, keepdims=True), (8, LANES))
    shift = [whole[4 + q : 5 + q] / norm1[q] for q in range(POLS)]
    norm2 = [whole[q : q + 1] - shift[q] * whole[4 + q : 5 + q] for q in range(POLS)]
    inverse = spread([1.0 / jnp.sqrt(t) for t in norm2])
    back = spread(shift)
    for jh, jp in near:
        c = (h + jh) % 2 * 2 + (p + jp) % 2
        hear = functools.partial(arrived, recv3.at[4 + c], r3.at[4 + c])
        if (jh, jp) == (0, 0):
            pl.when(jnp.logical_not(owner))(hear)
        else:
            hear()
    for c in range(4):
        value = (recv3[4 + c] - back * u[1, c]) * inverse
        for q in range(POLS):
            for t in range(LINES):
                at = ((t // 2) * 8 + (c // 2) * 4 + (t % 2) * 2 + c % 2) * LANES
                last_ref[q : q + 1, at : at + LANES] = value[LINES * q + t : LINES * q + t + 1, :]
    for q in range(POLS):
        alpha_ref[0:1, q : q + 1] = alpha[q][:, :1]
        alpha_ref[1:2, q : q + 1] = (alpha[q] + shift[q])[:, :1]
        beta_ref[0:1, q : q + 1] = jnp.sqrt(ratio[q])[:, :1]
        beta_ref[1:2, q : q + 1] = jnp.sqrt(norm2[q] / norm1[q])[:, :1]
    finish()


def write_out(*refs):
    sources, targets, sems = refs[:3], refs[3:6], refs[6]
    copies = [pltpu.make_async_copy(a, b, sems.at[i]) for i, (a, b) in enumerate(zip(sources, targets, strict=True))]
    for c in copies:
        c.start()
    for c in copies:
        c.wait()


def lanczos(sizes, kernel_half, dipole, band_energy, core_energy, core_index):
    nx, nz, _ = sizes
    rows, cols = kernel_half.shape
    dma = pltpu.SemaphoreType.DMA
    chunk = (ROWS, LANES)
    longer = (ROWS + 8, LANES)
    tile = (8, LANES)
    results = pl.pallas_call(
        functools.partial(kernel, sizes),
        out_shape=(pltpu.VMEM((2, POLS), F32), pltpu.VMEM((2, POLS), F32), pltpu.VMEM(dipole.shape, F32)),
        in_specs=[pl.BlockSpec(memory_space=pl.ANY)] * 5,
        out_specs=[pl.BlockSpec(memory_space=pltpu.VMEM)] * 3,
        scratch_shapes=[
            pltpu.VMEM((rows, cols), BF),
            pltpu.VMEM((4, cols, LINES * LANES), BF),
            pltpu.VMEM((rows, cols), BF),
            pltpu.VMEM((4, cols, LINES * LANES), BF),
            pltpu.VMEM((4, 8 * LINES, LANES), F32),
            pltpu.VMEM(dipole.shape, F32),
            pltpu.VMEM(band_energy.shape, F32),
            pltpu.SMEM(core_energy.shape, F32),
            pltpu.SMEM(core_index.shape, jnp.int32),
            pltpu.VMEM((POLS, 2 * cols), F32),
            pltpu.VMEM((2, 4, *chunk), F32),
            pltpu.VMEM((4, *tile), F32),
            pltpu.VMEM((2, 4, *longer), F32),
            pltpu.VMEM((2 * 8, *longer), F32),
            pltpu.VMEM((2, 2, *tile), F32),
            pltpu.VMEM((2 * nx * 2, *tile), F32),
            pltpu.VMEM((2, *longer), F32),
            pltpu.VMEM((2 * nz, *longer), F32),
            pltpu.VMEM((2, *chunk), F32),
            pltpu.VMEM((2 * 4, *chunk), F32),
            pltpu.VMEM(tile, F32),
            pltpu.VMEM((2, *tile), F32),
            pltpu.VMEM((2, *tile), F32),
            pltpu.VMEM((2 * nx, *tile), F32),
            pltpu.VMEM(tile, F32),
            pltpu.VMEM((nx * 4, *tile), F32),
            dma((3,)), dma((2,)),
            dma((1,)), dma((1,)),
            dma((1,)), dma((2,)),
            dma((1,)), dma((2,)),
            dma((1,)), dma((2,)),
            dma((2,)), dma((8,)),
            dma((1,)), dma((1,)),
            dma((1,)), dma((2,)),
            dma((2,)), dma((1,)),
            pltpu.SemaphoreType.REGULAR, pltpu.SemaphoreType.REGULAR((3,)),
            dma((2,)), dma((2,)),
        ],
        compiler_params=pltpu.CompilerParams(collective_id=0, has_side_effects=True),
    )(kernel_half, dipole, band_energy, core_energy, core_index)
    alphas, betas, last = pl.pallas_call(
        write_out,
        out_shape=(
            jax.ShapeDtypeStruct((2, POLS), F32),
            jax.ShapeDtypeStruct((2, POLS), F32),
            jax.ShapeDtypeStruct(dipole.shape, F32),
        ),
        in_specs=[pl.BlockSpec(memory_space=pltpu.VMEM)] * 3,
        out_specs=[pl.BlockSpec(memory_space=pl.ANY)] * 3,
        scratch_shapes=[dma((3,))],
    )(*[pltpu.with_memory_space_constraint(r, pltpu.VMEM) for r in results])
    return alphas.T, betas.T, last


def solution(mesh):
    nx, np_, nz = mesh.shape["row"], mesh.shape["pol"], mesh.shape["col"] // 4
    sizes = (nx, nz, nz * np_ // nx)
    in_specs = (P("row", ("pol", "col")), P(None, "row"), P("row", None), P(), P("row"))
    out_specs = (P(), P(), P(None, "row"))
    return jax.shard_map(
        functools.partial(lanczos, sizes), mesh=mesh, in_specs=in_specs, out_specs=out_specs, check_vma=False
    )
```

```python
import functools

import jax
import jax.numpy as jnp
from jax import lax
from jax.experimental import pallas as pl
from jax.experimental.pallas import tpu as pltpu
from jax.sharding import PartitionSpec as P

F32 = jnp.float32
BF = jnp.bfloat16
MESH = pl.DeviceIdType.MESH
CORES = 4
LANES = 128
POLS = 3
LINES = 8
ROWS = POLS * LINES


def spread(parts):
    return jnp.concatenate([jnp.broadcast_to(t, (LINES, t.shape[1])) for t in parts], axis=0)


def over_lines(x):
    return [jnp.sum(x[LINES * q : LINES * (q + 1)], axis=0, keepdims=True) for q in range(POLS)]


def placed(parts, first=0):
    row = lax.broadcasted_iota(jnp.int32, (8, LANES), 0)
    out = jnp.zeros((8, LANES), F32)
    for q, part in enumerate(parts):
        out = jnp.where(row == first + q, jnp.broadcast_to(part, (8, LANES)), out)
    return out


def stacked(parts):
    width = parts[0].shape[1]
    row = lax.broadcasted_iota(jnp.int32, (8, width), 0)
    a, b, c = (jnp.broadcast_to(t, (8, width)) for t in parts)
    return jnp.where(row == 0, a, jnp.where(row == 1, b, c))


def other_rows(x):
    return jnp.concatenate([x[4:], x[:4]], axis=0)


def two_terms(x):
    high = x.astype(BF).astype(F32)
    return jnp.concatenate([high, x - high], axis=0).astype(BF)


def joined(x):
    half = x.shape[0] // 2
    return x[:half] + x[half:]


def kernel(
    sizes,
    w_hbm, dip_hbm, band_hbm, core_hbm, index_hbm,
    alpha_ref, beta_ref, last_ref,
    w, wt, wb, wtb, turn, recvd, dip, band, core, index,
    uc0, u, en,
    send1, recv1, sendc, recvc, send2, recv2, send3, recv3, sendt, recvt, sendx, recvx, sendn, recvn,
    load_sem, core_sem, s0, r0, s1, r1, sc, rc, s2, r2, s3, r3, st, rt, sx, rx, sn, rn, known, rounds, sb, rb, sd, rd,
):
    nx, nz, zl_count = sizes
    zh_count = nz // zl_count
    p = lax.axis_index("pol")
    x = lax.axis_index("row")
    col = lax.axis_index("col")
    z = col // 4
    h = (col // 2) % 2
    k = col % 2
    y = h * 2 + p
    zl = z % zl_count
    home = p * zh_count + z // zl_count
    is_home = x == home
    away = jnp.logical_not(is_home)
    owner = k == 1
    keeper = (z // zl_count) == (x % zh_count)
    p_keep = x // zh_count

    def dev(pp, xx, zz, hh, kk):
        return (pp, xx, zz * 4 + hh * 2 + kk)

    barrier = pltpu.get_barrier_semaphore()
    far_first = sorted(range(1, nz), key=lambda d: -min(d, nz - d))
    near = [(0, 0), (0, 1), (1, 1), (1, 0)]

    def signal(sem, d):
        pl.semaphore_signal(sem, inc=1, device_id=d, device_id_type=MESH)

    def member(jh, jp, kk):
        return dev((p + jp) % 2, x, z, (h + jh) % 2, kk)

    def above_and_below(sem):
        for d in (1, nz - 1):
            signal(sem, dev(p, x, (z + d) % nz, h, 1))

    for dx in (2, 1, 3):
        signal(barrier, dev(p, (x + dx) % nx, z, h, 1))
    for jh, jp in near[:0:-1]:
        signal(barrier, member(jh, jp, 1))
    signal(barrier, dev(p, x, z, h, 1 - k))

    @pl.when(owner)
    def _():
        for dx in (2, 1, 3):
            signal(barrier, dev(p, (x + dx) % nx, z, h, 0))
        for jh, jp in near[:0:-1]:
            signal(barrier, member(jh, jp, 0))
        above_and_below(barrier)

    loads = [
        pltpu.make_async_copy(dip_hbm, dip, load_sem.at[0]),
        pltpu.make_async_copy(band_hbm, band, load_sem.at[1]),
        pltpu.make_async_copy(core_hbm, core, core_sem.at[0]),
        pltpu.make_async_copy(index_hbm, index, core_sem.at[1]),
    ]
    for c in loads:
        c.start()
    big = w.shape[0] // 4
    w_loads = [
        pltpu.make_async_copy(
            w_hbm.at[pl.ds(i * big, big)], w.at[pl.ds(i * big, big)], load_sem.at[2]
        )
        for i in range(4)
    ]
    for c in w_loads:
        c.start()

    def start(copy, condition=None):
        if condition is None:
            copy().start()
        else:
            pl.when(condition)(lambda: copy().start())

    def send(src, dst, send_sem, recv_sem, device):
        return pltpu.make_async_remote_copy(
            src_ref=src, dst_ref=dst, send_sem=send_sem, recv_sem=recv_sem, device_id=device,
            device_id_type=MESH,
        )

    me = dev(p, x, z, h, k)

    def arrived(dst, recv_sem):
        send(dst, dst, s1.at[0], recv_sem, me).wait_recv()

    def left_here(src, send_sem):
        send(src, src, send_sem, r1.at[0], me).wait_send()

    def either(condition, then, other):
        pl.when(condition)(then)
        pl.when(jnp.logical_not(condition))(other)

    def finish():
        @pl.when(owner)
        def _():
            @pl.when(is_home)
            def _():
                left_here(dip.at[:, pl.ds(0, 6 * 4 * LANES)], s0.at[0])

            @pl.when(keeper)
            def _():
                left_here(recvc.at[pl.ds(0, 3)], st.at[0])

            left_here(recv2.at[pl.ds(0, 2 * (nz - 1))], s2.at[0])
            for step in range(2):
                left_here(recv3.at[pl.ds(0, 7)], s3.at[step])
                left_here(recvn.at[pl.ds(0, 16 - step)], sn.at[step])
            left_here(recvc.at[pl.ds(0, 14)], sx.at[0])

        either(
            owner,
            lambda: left_here(recv1.at[pl.ds(0, 6)], s1.at[0]),
            lambda: left_here(recv1.at[pl.ds(0, 4)], s1.at[0]),
        )

        @pl.when(jnp.logical_not(owner))
        def _():
            left_here(w, sb.at[0])
            left_here(wt, sb.at[1])

        mine = jnp.logical_and(owner, is_home)
        either(
            mine,
            lambda: left_here(recvc.at[pl.ds(0, 1)], sc.at[0]),
            lambda: left_here(recvc.at[pl.ds(0, 2)], sc.at[0]),
        )
        pl.when(mine)(lambda: left_here(recvd.at[pl.ds(0, 2 * nz - 1)], sd.at[0]))
        pl.when(jnp.logical_and(owner, away))(lambda: left_here(recvd.at[pl.ds(0, 2 * nz)], sd.at[0]))

    loads[0].wait()
    pl.semaphore_wait(barrier, jnp.where(owner, 7 + 2 * (nx - 1) + 2, 4 + nx - 1))

    @pl.when(owner)
    def _():
        for jh, jp in near[:0:-1]:
            for kk in range(2):
                signal(known, member(jh, jp, kk))
        signal(known, dev(p, x, z, h, 0))
        above_and_below(rounds.at[0])

    chip_lines = pl.ds(pl.multiple_of((zl * 2 + h) * 4 * LANES, 4 * LANES), 4 * LANES)

    def first_copy(dx, kk):
        return send(
            dip.at[:, chip_lines], uc0, s0.at[0], r0.at[0], dev(p, (x + dx) % nx, z, h, kk)
        )

    for dx in (2, 1, 3):
        for kk in range(2):
            start(functools.partial(first_copy, dx, kk), jnp.logical_and(is_home, owner))

    @pl.when(is_home)
    def _():
        uc0[...] = dip[:, chip_lines]

    for c in loads[1:]:
        c.wait()
    for c in range(4):
        for q in range(POLS):
            for t in range(LINES):
                at = ((t // 2) * 8 + (c // 2) * 4 + (t % 2) * 2 + c % 2) * LANES
                u[0, c, LINES * q + t : LINES * q + t + 1, :] = dip[q : q + 1, at : at + LANES]
    offsets = []
    for i in range(2 * CORES):
        level = index[i]
        off = jnp.float32(0.0)
        for j in range(CORES):
            off = jnp.where(level == j, core[j], off)
        offsets.append(off)
    row8 = lax.broadcasted_iota(jnp.int32, (8, LANES), 0)
    for c in range(4):
        value = jnp.zeros((8, LANES), F32)
        for t in range(LINES):
            line = (t // 2) * 8 + (c // 2) * 4 + (t % 2) * 2 + c % 2
            at = (line % 4) * LANES
            level = band[line // 16 : line // 16 + 1, at : at + LANES] - offsets[line // 4]
            value = jnp.where(row8 == t, jnp.broadcast_to(level, (8, LANES)), value)
        en[c] = value

    pltpu.make_async_copy(w_hbm, w, load_sem.at[2]).wait()

    line_of_row_wide = lax.broadcasted_iota(jnp.int32, (ROWS, 2 * LANES), 0) % LINES
    line_of_row = lax.broadcasted_iota(jnp.int32, (ROWS, LANES), 0) % LINES
    row8_wide = lax.broadcasted_iota(jnp.int32, (8, 2 * LANES), 0)

    def line_rows(hh, pp, t):
        line = (t // 2) * 8 + hh * 4 + (t % 2) * 2 + pp
        return pl.ds(pl.multiple_of(line * LANES, LANES), LANES)

    def columns_of(left, block, hh, pp):
        out = jnp.zeros((ROWS, 2 * LANES), F32)
        for t in range(LINES):
            part = joined(jnp.dot(left, block[line_rows(hh, pp, t), :], preferred_element_type=F32))
            out = jnp.where(line_of_row_wide == t, part, out)
        return out

    def send_columns(step, tiles):
        slot = x * 2 + k
        for half in range(2):
            sendc[step, half] = tiles[half]

        def col_copy(half):
            return send(
                sendc.at[step, half], recvc.at[slot], sc.at[0], rc.at[step], dev(half, home, z, h, 1)
            )

        for half in range(2):
            mine = jnp.logical_and(owner, jnp.logical_and(is_home, p == half))

            @pl.when(mine)
            def _(half=half):
                recvc[slot] = sendc[step, half]

            start(functools.partial(col_copy, half), jnp.logical_not(mine))

    def transpose():
        side = 2 * LANES

        @pl.loop(0, w.shape[0] // side)
        def _(i):
            tile = w[pl.ds(pl.multiple_of(i * side, side), side), :].T
            at = pl.ds(pl.multiple_of((i // 4 * 2 + i % 2) * LANES, LANES), LANES)
            for pp in range(2):
                wt[i // 2 % 2 * 2 + pp, :, at] = tile[:, pp * LANES : (pp + 1) * LANES]

    def plane_sums():
        whole = recvx[0]
        for xx in range(1, nx):
            whole += recvx[xx]
        return jnp.broadcast_to(jnp.sum(whole, axis=1, keepdims=True), (8, LANES))

    def first_sums():
        whole = plane_sums()
        norms = [whole[q : q + 1] for q in range(POLS)]
        return norms, [whole[4 + q : 5 + q] / norms[q] for q in range(POLS)]

    def line_tile(value):
        mod = lax.broadcasted_iota(jnp.int32, (ROWS, LANES), 0) % LINES
        tile = jnp.zeros((8, LANES), F32)
        for kk in range(2):
            tile += placed(over_lines(jnp.where(mod == zl * 2 + kk, value, 0.0)), 4 * kk)
        return tile

    alpha = norms = None
    for step in range(2):
        def row_copy(j, step=step):
            jh, jp = near[j]
            return send(
                send1.at[step, j], recv1.at[y * 2 + k if step == 0 else 8 + y], s1.at[0], r1.at[step],
                member(jh, jp, 1),
            )

        def first_products():
            sums = jnp.zeros((ROWS, 2 * LANES), F32)
            for c in range(4):
                sums += columns_of(two_terms(u[0, c]), w, c // 2, c % 2)
            col_lines = over_lines(sums)
            col_part = stacked(col_lines)

            pl.when(away)(functools.partial(arrived, uc0, r0.at[0]))
            mine = pl.ds(pl.multiple_of(k * 2 * LANES, 2 * LANES), 2 * LANES)
            column = [uc0[q : q + 1, mine] for q in range(POLS)]
            pl.semaphore_wait(known, jnp.where(owner, 3, 4))
            send_columns(0, [col_part[:, :LANES], col_part[:, LANES:]])

            @pl.when(owner)
            def _():
                pl.semaphore_wait(rounds.at[0], 2)
                above_and_below(rounds.at[1])

            twice = []
            for q in range(POLS):
                line = 2.0 * col_lines[q] * column[q]
                twice.append(line[:, :LANES] + line[:, LANES:])
            sum_rows = placed(twice)
            left = two_terms(spread(column))

            for j in (3, 2, 1, 0):
                jh, jp = near[j]
                hh, pp = (h + jh) % 2, (p + jp) % 2
                lines = jnp.zeros((ROWS, LANES), F32)
                for t in range(LINES):
                    part = joined(
                        lax.dot_general(
                            left, w[line_rows(hh, pp, t), :], (((1,), (1,)), ((), ())),
                            preferred_element_type=F32,
                        )
                    )
                    lines = jnp.where(line_of_row == t, part, lines)
                send1[0, j, :ROWS] = lines
                send1[0, j, ROWS:] = sum_rows
                start(functools.partial(row_copy, j), None if j else jnp.logical_not(owner))

        def chip_copy(i):
            src, dst = ((w, wb), (wt, wtb))[i]
            return send(src, dst, sb.at[i], rb.at[i], dev(p, x, z, h, 1))

        def second_products():
            arrived(wb, rb.at[0])
            sums = [jnp.zeros((ROWS, 2 * LANES), F32)] * 2
            for jh, jp in near:
                hh, pp = (h + jh) % 2, (p + jp) % 2
                if (jh, jp) != (0, 0):
                    arrived(recv3.at[hh * 2 + pp], r3.at[hh * 2 + pp])
                left = two_terms(recv3[hh * 2 + pp])
                for b, block in enumerate((wb, w)):
                    sums[b] = sums[b] + columns_of(left, block, hh, pp)
            parts = [stacked(over_lines(sums[b])) for b in range(2)]
            tiles = jnp.where(row8_wide < 4, parts[0], other_rows(parts[1]))
            for half in range(2):
                sendc[1, half] = tiles[:, half * LANES : (half + 1) * LANES]

            @pl.when(is_home)
            def _():
                for half in range(2):
                    recvt[half] = line_tile(recv3[h * 2 + half])

            pl.when(away)(functools.partial(arrived, recvt, rt.at[0]))
            got = jnp.concatenate([recvt[0], recvt[1]], axis=1)
            lefts = [two_terms(got), two_terms(other_rows(got))]

            def direct_copy(d, half):
                return send(
                    sendc.at[1, half], recvd.at[x * zl_count + zl], sd.at[0], rd.at[0],
                    dev(half, home, (z + d) % nz, h, 1),
                )

            def send_direct():
                for d in (*far_first, 0):
                    for half in range(2):
                        if d:
                            start(functools.partial(direct_copy, d, half))
                        else:
                            mine = jnp.logical_and(is_home, p == half)

                            @pl.when(mine)
                            def _(half=half):
                                recvd[x * zl_count + zl] = sendc[1, half]

                            start(functools.partial(direct_copy, d, half), jnp.logical_not(mine))

            arrived(wtb, rb.at[1])
            for j in (3, 2, 1, 0):
                jh, jp = near[j]
                c = (h + jh) % 2 * 2 + (p + jp) % 2
                wide = joined(
                    jnp.dot(lefts[0], wtb[c], preferred_element_type=F32)
                    + jnp.dot(lefts[1], wt[c], preferred_element_type=F32)
                )
                for t in range(LINES):
                    turn[j, 8 * t : 8 * t + 8, :] = wide[:, t * LANES : (t + 1) * LANES]
                for q in range(POLS):
                    send1[1, j, LINES * q : LINES * (q + 1)] = turn[j, pl.ds(q, LINES, stride=8), :]
                send1[1, j, ROWS:] = jnp.zeros((8, LANES), F32)
                if j:
                    start(functools.partial(row_copy, j))
                if j == 1:
                    send_direct()
            arrived(recvx.at[pl.ds(0, nx - 1)], rx.at[0])

        if step == 0:
            first_products()
        else:

            def only_wait():
                for c in range(4):
                    arrived(recv3.at[c], r3.at[c])
                arrived(recvx.at[pl.ds(0, nx)], rx.at[0])

            either(owner, second_products, only_wait)
            norms, alpha = first_sums()

        if step == 1:
            factor = spread(alpha)
            for c in range(4):
                u[1, c] = recv3[c] - factor * u[0, c]
        squares = jnp.zeros((ROWS, LANES), F32)
        weighted = jnp.zeros((ROWS, LANES), F32)
        for c in range(4):
            sq = u[step, c] * u[step, c]
            squares += sq
            weighted += jnp.concatenate([en[c]] * POLS, axis=0) * sq
        own_sums = placed(over_lines(squares))

        def x_copy(dx, kk, at):
            return send(
                sendx.at[at], recvx.at[at * nx + x], sx.at[0], rx.at[at],
                dev(p, (x + dx) % nx, z, h, kk),
            )

        def share(at, kk):
            for dx in (2, 1, 3):
                start(functools.partial(x_copy, dx, kk, at))
            if kk == 0:
                start(functools.partial(x_copy, 0, 0, at))
            else:
                recvx[at * nx + x] = sendx[at]

        if step == 0:
            own_sums += placed(over_lines(weighted), 4)

        if step == 0:

            @pl.when(jnp.logical_not(owner))
            def _():
                chip_copy(0).start()
                transpose()
                chip_copy(1).start()

        @pl.when(owner)
        def _(step=step, own_sums=own_sums):
            if step == 0:
                pl.semaphore_wait(rounds.at[1], 2)
                above_and_below(rounds.at[2])
            if step == 1:
                sendx[1] = own_sums
                share(1, 1)
                share(1, 0)
            recv1[y * 2 + k if step == 0 else 8 + y] = send1[step, 0]
            members = 4 if step else 8
            arrived(recv1.at[pl.ds(step * 8, members - 1)], r1.at[step])
            total = recv1[step * 8]
            for g in range(1, members):
                total += recv1[step * 8 + g]
            send2[step] = total

            def add_columns():
                either(
                    p == p_keep,
                    lambda: arrived(recvc.at[pl.ds(0, 2 * nx - 1)], rc.at[0]),
                    lambda: arrived(recvc.at[pl.ds(0, 2 * nx)], rc.at[0]),
                )
                for kk in range(2):
                    cols = recvc[kk]
                    for xx in range(1, nx):
                        cols += recvc[2 * xx + kk]
                    for q in range(POLS):
                        at = pl.ds(LINES * q, LINES)
                        line = jnp.broadcast_to(cols[q : q + 1], (8, LANES))
                        send2[0, at] = send2[0, at] + jnp.where(row8 == zl * 2 + kk, line, 0.0)

            if step == 0:
                pl.when(keeper)(add_columns)

            if step == 0:
                pl.semaphore_wait(rounds.at[2], 2)
            def z_copy(d):
                return send(
                    send2.at[step], recv2.at[step * nz + z], s2.at[0], r2.at[step],
                    dev(p, x, (z + d) % nz, h, 1),
                )

            for d in far_first:
                start(functools.partial(z_copy, d))
            recv2[step * nz + z] = send2[step]
            rest = jnp.concatenate([en[y]] * POLS, axis=0) * u[step, y]
            if step == 0:
                transpose()
            else:
                arrived(recvx.at[pl.ds(nx, nx - 1)], rx.at[1])
                coupled = send3[0] - jnp.concatenate([en[y]] * POLS, axis=0) * u[0, y]
                rest = rest - spread(alpha) * (u[1, y] + coupled) - spread(ratio_of(1)) * u[0, y]
                many = nx * zl_count
                either(
                    jnp.logical_and(keeper, p == p_keep),
                    lambda: arrived(recvd.at[pl.ds(0, many - 1)], rd.at[0]),
                    lambda: arrived(recvd.at[pl.ds(0, many)], rd.at[0]),
                )
                lines = [jnp.zeros((8, LANES), F32)] * POLS
                for t in range(zl_count):
                    cols = recvd[t]
                    for xx in range(1, nx):
                        cols += recvd[xx * zl_count + t]
                    for q in range(POLS):
                        for kk in range(2):
                            line = jnp.broadcast_to(cols[4 * kk + q : 4 * kk + q + 1], (8, LANES))
                            lines[q] = jnp.where(row8 == 2 * t + kk, line, lines[q])
                rest = rest + jnp.concatenate(lines, axis=0)
            arrived(recv2.at[pl.ds(step * nz, nz - 1)], r2.at[step])
            total = recv2[step * nz]
            for zz in range(1, nz):
                total += recv2[step * nz + zz]
            value = total[:ROWS] + rest

            def chunk_copy(j, kk):
                jh, jp = near[j]
                return send(
                    send3.at[step], recv3.at[step * 4 + y], s3.at[step], r3.at[step * 4 + y],
                    dev((p + jp) % 2, x, z, (h + jh) % 2, kk),
                )

            def send_chunk(j, kk):
                start(functools.partial(chunk_copy, j, kk))

            if step == 0:
                send3[0] = value
                send_chunk(3, 1)
                sendt[...] = line_tile(value)

                def tile_copy(dx):
                    return send(
                        sendt, recvt.at[p], st.at[0], rt.at[0], dev(p_keep, (x + dx) % nx, z, h, 1)
                    )

                for dx in (2, 1, 3):
                    start(functools.partial(tile_copy, dx), keeper)
                send_chunk(2, 1)
                send_chunk(1, 1)
                sendx[0] = jnp.concatenate([total[ROWS + 4 :], total[ROWS : ROWS + 4]], axis=0) + own_sums
                share(0, 1)
                for j in (3, 2, 1, 0):
                    send_chunk(j, 0)
                share(0, 0)
            else:
                sendn[...] = placed(over_lines(value * value)) + placed(over_lines(value * u[1, y]), 4)

                def sums_copy(dx, j, kk):
                    jh, jp = near[j]
                    return send(
                        sendn, recvn.at[x * 4 + y], sn.at[kk], rn.at[0],
                        dev((p + jp) % 2, (x + dx) % nx, z, (h + jh) % 2, kk),
                    )

                targets = [(dx, j, kk) for dx in range(nx) for j in range(4) for kk in range(2)]
                targets.sort(key=lambda t: -min(t[0], nx - t[0]) - (0, 1, 1, 2)[t[1]] - 0.6 * (t[2] == 0))
                for target in targets:
                    if target != (0, 0, 1):
                        start(functools.partial(sums_copy, *target))
                recvn[x * 4 + y] = sendn[...]
                send3[1] = value

            if step == 1:
                for j in (3, 2, 1, 0):
                    send_chunk(j, 0)
                    if j:
                        send_chunk(j, 1)
            recv3[step * 4 + y] = send3[step]

        def ratio_of(at):
            whole = recvx[at * nx]
            for xx in range(1, nx):
                whole += recvx[at * nx + xx]
            whole = jnp.broadcast_to(jnp.sum(whole, axis=1, keepdims=True), (8, LANES))
            return [whole[q : q + 1] / norms[q] for q in range(POLS)]

    @pl.when(jnp.logical_not(owner))
    def _():
        arrived(recvx.at[pl.ds(nx, nx)], rx.at[1])

    ratio = ratio_of(1)
    norm1 = [ratio[q] * norms[q] for q in range(POLS)]
    either(
        owner,
        lambda: arrived(recvn.at[pl.ds(0, 4 * nx - 1)], rn.at[0]),
        lambda: arrived(recvn.at[pl.ds(0, 4 * nx)], rn.at[0]),
    )
    whole = recvn[0]
    for c in range(1, 4 * nx):
        whole += recvn[c]
    whole = jnp.broadcast_to(jnp.sum(whole, axis=1, keepdims=True), (8, LANES))
    shift = [whole[4 + q : 5 + q] / norm1[q] for q in range(POLS)]
    norm2 = [whole[q : q + 1] - shift[q] * whole[4 + q : 5 + q] for q in range(POLS)]
    inverse = spread([1.0 / jnp.sqrt(t) for t in norm2])
    back = spread(shift)
    for jh, jp in near:
        c = (h + jh) % 2 * 2 + (p + jp) % 2
        hear = functools.partial(arrived, recv3.at[4 + c], r3.at[4 + c])
        if (jh, jp) == (0, 0):
            pl.when(jnp.logical_not(owner))(hear)
        else:
            hear()
    for c in range(4):
        value = (recv3[4 + c] - back * u[1, c]) * inverse
        for q in range(POLS):
            for t in range(LINES):
                at = ((t // 2) * 8 + (c // 2) * 4 + (t % 2) * 2 + c % 2) * LANES
                last_ref[q : q + 1, at : at + LANES] = value[LINES * q + t : LINES * q + t + 1, :]
    for q in range(POLS):
        alpha_ref[0:1, q : q + 1] = alpha[q][:, :1]
        alpha_ref[1:2, q : q + 1] = (alpha[q] + shift[q])[:, :1]
        beta_ref[0:1, q : q + 1] = jnp.sqrt(ratio[q])[:, :1]
        beta_ref[1:2, q : q + 1] = jnp.sqrt(norm2[q] / norm1[q])[:, :1]
    finish()


def write_out(*refs):
    sources, targets, sems = refs[:3], refs[3:6], refs[6]
    copies = [pltpu.make_async_copy(a, b, sems.at[i]) for i, (a, b) in enumerate(zip(sources, targets, strict=True))]
    for c in copies:
        c.start()
    for c in copies:
        c.wait()


def lanczos(sizes, kernel_half, dipole, band_energy, core_energy, core_index):
    nx, nz, _ = sizes
    rows, cols = kernel_half.shape
    dma = pltpu.SemaphoreType.DMA
    chunk = (ROWS, LANES)
    longer = (ROWS + 8, LANES)
    tile = (8, LANES)
    results = pl.pallas_call(
        functools.partial(kernel, sizes),
        out_shape=(pltpu.VMEM((2, POLS), F32), pltpu.VMEM((2, POLS), F32), pltpu.VMEM(dipole.shape, F32)),
        in_specs=[pl.BlockSpec(memory_space=pl.ANY)] * 5,
        out_specs=[pl.BlockSpec(memory_space=pltpu.VMEM)] * 3,
        scratch_shapes=[
            pltpu.VMEM((rows, cols), BF),
            pltpu.VMEM((4, cols, LINES * LANES), BF),
            pltpu.VMEM((rows, cols), BF),
            pltpu.VMEM((4, cols, LINES * LANES), BF),
            pltpu.VMEM((4, 8 * LINES, LANES), F32),
            pltpu.VMEM((16, *tile), F32),
            pltpu.VMEM(dipole.shape, F32),
            pltpu.VMEM(band_energy.shape, F32),
            pltpu.SMEM(core_energy.shape, F32),
            pltpu.SMEM(core_index.shape, jnp.int32),
            pltpu.VMEM((POLS, 2 * cols), F32),
            pltpu.VMEM((2, 4, *chunk), F32),
            pltpu.VMEM((4, *tile), F32),
            pltpu.VMEM((2, 4, *longer), F32),
            pltpu.VMEM((2 * 8, *longer), F32),
            pltpu.VMEM((2, 2, *tile), F32),
            pltpu.VMEM((2 * nx * 2, *tile), F32),
            pltpu.VMEM((2, *longer), F32),
            pltpu.VMEM((2 * nz, *longer), F32),
            pltpu.VMEM((2, *chunk), F32),
            pltpu.VMEM((2 * 4, *chunk), F32),
            pltpu.VMEM(tile, F32),
            pltpu.VMEM((2, *tile), F32),
            pltpu.VMEM((2, *tile), F32),
            pltpu.VMEM((2 * nx, *tile), F32),
            pltpu.VMEM(tile, F32),
            pltpu.VMEM((nx * 4, *tile), F32),
            dma((3,)), dma((2,)),
            dma((1,)), dma((1,)),
            dma((1,)), dma((2,)),
            dma((1,)), dma((2,)),
            dma((1,)), dma((2,)),
            dma((2,)), dma((8,)),
            dma((1,)), dma((1,)),
            dma((1,)), dma((2,)),
            dma((2,)), dma((1,)),
            pltpu.SemaphoreType.REGULAR, pltpu.SemaphoreType.REGULAR((3,)),
            dma((2,)), dma((2,)),
            dma((1,)), dma((1,)),
        ],
        compiler_params=pltpu.CompilerParams(collective_id=0, has_side_effects=True),
    )(kernel_half, dipole, band_energy, core_energy, core_index)
    alphas, betas, last = pl.pallas_call(
        write_out,
        out_shape=(
            jax.ShapeDtypeStruct((2, POLS), F32),
            jax.ShapeDtypeStruct((2, POLS), F32),
            jax.ShapeDtypeStruct(dipole.shape, F32),
        ),
        in_specs=[pl.BlockSpec(memory_space=pltpu.VMEM)] * 3,
        out_specs=[pl.BlockSpec(memory_space=pl.ANY)] * 3,
        scratch_shapes=[dma((3,))],
    )(*[pltpu.with_memory_space_constraint(r, pltpu.VMEM) for r in results])
    return alphas.T, betas.T, last


def solution(mesh):
    nx, np_, nz = mesh.shape["row"], mesh.shape["pol"], mesh.shape["col"] // 4
    sizes = (nx, nz, nz * np_ // nx)
    in_specs = (P("row", ("pol", "col")), P(None, "row"), P("row", None), P(), P("row"))
    out_specs = (P(), P(), P(None, "row"))
    return jax.shard_map(
        functools.partial(lanczos, sizes), mesh=mesh, in_specs=in_specs, out_specs=out_specs, check_vma=False
    )
```

```python
import functools

import jax
import jax.numpy as jnp
from jax import lax
from jax.experimental import pallas as pl
from jax.experimental.pallas import tpu as pltpu
from jax.sharding import PartitionSpec as P

F32 = jnp.float32
BF = jnp.bfloat16
MESH = pl.DeviceIdType.MESH
CORES = 4
LANES = 128
POLS = 3
LINES = 8
ROWS = POLS * LINES


def spread(parts):
    return jnp.concatenate([jnp.broadcast_to(t, (LINES, t.shape[1])) for t in parts], axis=0)


def over_lines(x):
    return [jnp.sum(x[LINES * q : LINES * (q + 1)], axis=0, keepdims=True) for q in range(POLS)]


def placed(parts, first=0):
    row = lax.broadcasted_iota(jnp.int32, (8, LANES), 0)
    out = jnp.zeros((8, LANES), F32)
    for q, part in enumerate(parts):
        out = jnp.where(row == first + q, jnp.broadcast_to(part, (8, LANES)), out)
    return out


def stacked(parts):
    width = parts[0].shape[1]
    row = lax.broadcasted_iota(jnp.int32, (8, width), 0)
    a, b, c = (jnp.broadcast_to(t, (8, width)) for t in parts)
    return jnp.where(row == 0, a, jnp.where(row == 1, b, c))


def other_rows(x):
    return jnp.concatenate([x[4:], x[:4]], axis=0)


def two_terms(x):
    high = x.astype(BF).astype(F32)
    return jnp.concatenate([high, x - high], axis=0).astype(BF)


def joined(x):
    half = x.shape[0] // 2
    return x[:half] + x[half:]


def kernel(
    sizes,
    w_hbm, dip_hbm, band_hbm, core_hbm, index_hbm,
    alpha_ref, beta_ref, last_ref,
    w, wt, wb, wtb, turn, dip, band, core, index,
    uc0, u, en,
    send1, recv1, sendc, recvc, send2, recv2, send3, recv3, sendt, recvt, sendx, recvx, sendn, recvn,
    load_sem, core_sem, s0, r0, s1, r1, sc, rc, s2, r2, s3, r3, st, rt, sx, rx, sn, rn, known, rounds, sb, rb,
):
    nx, nz, zl_count = sizes
    zh_count = nz // zl_count
    p = lax.axis_index("pol")
    x = lax.axis_index("row")
    col = lax.axis_index("col")
    z = col // 4
    h = (col // 2) % 2
    k = col % 2
    y = h * 2 + p
    zl = z % zl_count
    home = p * zh_count + z // zl_count
    is_home = x == home
    away = jnp.logical_not(is_home)
    owner = k == 1
    keeper = (z // zl_count) == (x % zh_count)
    p_keep = x // zh_count

    def dev(pp, xx, zz, hh, kk):
        return (pp, xx, zz * 4 + hh * 2 + kk)

    barrier = pltpu.get_barrier_semaphore()
    far_first = sorted(range(1, nz), key=lambda d: -min(d, nz - d))
    near = [(0, 0), (0, 1), (1, 1), (1, 0)]

    def signal(sem, d):
        pl.semaphore_signal(sem, inc=1, device_id=d, device_id_type=MESH)

    def member(jh, jp, kk):
        return dev((p + jp) % 2, x, z, (h + jh) % 2, kk)

    def above_and_below(sem):
        for d in (1, nz - 1):
            signal(sem, dev(p, x, (z + d) % nz, h, 1))

    for dx in (2, 1, 3):
        signal(barrier, dev(p, (x + dx) % nx, z, h, 1))
    for jh, jp in near[:0:-1]:
        signal(barrier, member(jh, jp, 1))
    signal(barrier, dev(p, x, z, h, 1 - k))

    @pl.when(owner)
    def _():
        for dx in (2, 1, 3):
            signal(barrier, dev(p, (x + dx) % nx, z, h, 0))
        for jh, jp in near[:0:-1]:
            signal(barrier, member(jh, jp, 0))
        above_and_below(barrier)

    loads = [
        pltpu.make_async_copy(dip_hbm, dip, load_sem.at[0]),
        pltpu.make_async_copy(band_hbm, band, load_sem.at[1]),
        pltpu.make_async_copy(core_hbm, core, core_sem.at[0]),
        pltpu.make_async_copy(index_hbm, index, core_sem.at[1]),
    ]
    for c in loads:
        c.start()
    big = w.shape[0] // 4
    w_loads = [
        pltpu.make_async_copy(
            w_hbm.at[pl.ds(i * big, big)], w.at[pl.ds(i * big, big)], load_sem.at[2]
        )
        for i in range(4)
    ]
    for c in w_loads:
        c.start()

    def start(copy, condition=None):
        if condition is None:
            copy().start()
        else:
            pl.when(condition)(lambda: copy().start())

    def send(src, dst, send_sem, recv_sem, device):
        return pltpu.make_async_remote_copy(
            src_ref=src, dst_ref=dst, send_sem=send_sem, recv_sem=recv_sem, device_id=device,
            device_id_type=MESH,
        )

    me = dev(p, x, z, h, k)

    def arrived(dst, recv_sem):
        send(dst, dst, s1.at[0], recv_sem, me).wait_recv()

    def left_here(src, send_sem):
        send(src, src, send_sem, r1.at[0], me).wait_send()

    def either(condition, then, other):
        pl.when(condition)(then)
        pl.when(jnp.logical_not(condition))(other)

    def finish():
        @pl.when(owner)
        def _():
            @pl.when(is_home)
            def _():
                left_here(dip.at[:, pl.ds(0, 6 * 4 * LANES)], s0.at[0])

            @pl.when(keeper)
            def _():
                left_here(recvc.at[pl.ds(0, 3)], st.at[0])

            left_here(recv2.at[pl.ds(0, nz - 1)], s2.at[0])
            left_here(recv3.at[pl.ds(0, nz - 1)], s2.at[1])
            left_here(recv3.at[pl.ds(0, 3)], s1.at[1])
            for step in range(2):
                left_here(recv3.at[pl.ds(0, 7)], s3.at[step])
                left_here(recvn.at[pl.ds(0, 16 - step)], sn.at[step])
            left_here(recvc.at[pl.ds(0, 14)], sx.at[0])

        either(
            owner,
            lambda: left_here(recv1.at[pl.ds(0, 3)], s1.at[0]),
            lambda: left_here(recv1.at[pl.ds(0, 4)], s1.at[0]),
        )

        @pl.when(jnp.logical_not(owner))
        def _():
            left_here(w, sb.at[0])
            left_here(wt, sb.at[1])

        either(
            jnp.logical_or(jnp.logical_not(owner), is_home),
            lambda: left_here(recvc.at[pl.ds(0, 2)], sc.at[0]),
            lambda: left_here(recvc.at[pl.ds(0, 4)], sc.at[0]),
        )

    loads[0].wait()
    pl.semaphore_wait(barrier, jnp.where(owner, 7 + 2 * (nx - 1) + 2, 4 + nx - 1))

    @pl.when(owner)
    def _():
        for jh, jp in near[:0:-1]:
            for kk in range(2):
                signal(known, member(jh, jp, kk))
        signal(known, dev(p, x, z, h, 0))
        above_and_below(rounds.at[0])

    chip_lines = pl.ds(pl.multiple_of((zl * 2 + h) * 4 * LANES, 4 * LANES), 4 * LANES)

    def first_copy(dx, kk):
        return send(
            dip.at[:, chip_lines], uc0, s0.at[0], r0.at[0], dev(p, (x + dx) % nx, z, h, kk)
        )

    for dx in (2, 1, 3):
        for kk in range(2):
            start(functools.partial(first_copy, dx, kk), jnp.logical_and(is_home, owner))

    @pl.when(is_home)
    def _():
        uc0[...] = dip[:, chip_lines]

    for c in loads[1:]:
        c.wait()
    for c in range(4):
        for q in range(POLS):
            for t in range(LINES):
                at = ((t // 2) * 8 + (c // 2) * 4 + (t % 2) * 2 + c % 2) * LANES
                u[0, c, LINES * q + t : LINES * q + t + 1, :] = dip[q : q + 1, at : at + LANES]
    offsets = []
    for i in range(2 * CORES):
        level = index[i]
        off = jnp.float32(0.0)
        for j in range(CORES):
            off = jnp.where(level == j, core[j], off)
        offsets.append(off)
    row8 = lax.broadcasted_iota(jnp.int32, (8, LANES), 0)
    for c in range(4):
        value = jnp.zeros((8, LANES), F32)
        for t in range(LINES):
            line = (t // 2) * 8 + (c // 2) * 4 + (t % 2) * 2 + c % 2
            at = (line % 4) * LANES
            level = band[line // 16 : line // 16 + 1, at : at + LANES] - offsets[line // 4]
            value = jnp.where(row8 == t, jnp.broadcast_to(level, (8, LANES)), value)
        en[c] = value

    pltpu.make_async_copy(w_hbm, w, load_sem.at[2]).wait()

    line_of_row_wide = lax.broadcasted_iota(jnp.int32, (ROWS, 2 * LANES), 0) % LINES
    line_of_row = lax.broadcasted_iota(jnp.int32, (ROWS, LANES), 0) % LINES
    row8_wide = lax.broadcasted_iota(jnp.int32, (8, 2 * LANES), 0)

    def line_rows(hh, pp, t):
        line = (t // 2) * 8 + hh * 4 + (t % 2) * 2 + pp
        return pl.ds(pl.multiple_of(line * LANES, LANES), LANES)

    def columns_of(left, block, hh, pp):
        out = jnp.zeros((ROWS, 2 * LANES), F32)
        for t in range(LINES):
            part = joined(jnp.dot(left, block[line_rows(hh, pp, t), :], preferred_element_type=F32))
            out = jnp.where(line_of_row_wide == t, part, out)
        return out

    def send_columns(step, tiles):
        slot = x * 2 + k if step == 0 else 2 * nx + x
        for half in range(2):
            sendc[step, half] = tiles[half]

        def col_copy(half):
            return send(
                sendc.at[step, half], recvc.at[slot], sc.at[0], rc.at[step], dev(half, home, z, h, 1)
            )

        for half in range(2):
            mine = jnp.logical_and(owner, jnp.logical_and(is_home, p == half))

            @pl.when(mine)
            def _(half=half):
                recvc[slot] = sendc[step, half]

            start(functools.partial(col_copy, half), jnp.logical_not(mine))

    def transpose():
        side = 2 * LANES

        @pl.loop(0, w.shape[0] // side)
        def _(i):
            tile = w[pl.ds(pl.multiple_of(i * side, side), side), :].T
            at = pl.ds(pl.multiple_of((i // 4 * 2 + i % 2) * LANES, LANES), LANES)
            for pp in range(2):
                wt[i // 2 % 2 * 2 + pp, :, at] = tile[:, pp * LANES : (pp + 1) * LANES]

    def plane_sums():
        whole = recvx[0]
        for xx in range(1, nx):
            whole += recvx[xx]
        return jnp.broadcast_to(jnp.sum(whole, axis=1, keepdims=True), (8, LANES))

    def first_sums():
        whole = plane_sums()
        norms = [whole[q : q + 1] for q in range(POLS)]
        return norms, [whole[4 + q : 5 + q] / norms[q] for q in range(POLS)]

    def line_tile(value):
        mod = lax.broadcasted_iota(jnp.int32, (ROWS, LANES), 0) % LINES
        tile = jnp.zeros((8, LANES), F32)
        for kk in range(2):
            tile += placed(over_lines(jnp.where(mod == zl * 2 + kk, value, 0.0)), 4 * kk)
        return tile

    alpha = norms = None
    for step in range(2):
        rows = ROWS if step else ROWS + 8

        def row_copy(j, step=step, rows=rows):
            jh, jp = near[j]
            return send(
                send1.at[step, j, pl.ds(0, rows)], recv1.at[y * 2 + k if step == 0 else 8 + y, pl.ds(0, rows)],
                s1.at[step], r1.at[step],
                member(jh, jp, 1),
            )

        def first_products():
            sums = jnp.zeros((ROWS, 2 * LANES), F32)
            for c in range(4):
                sums += columns_of(two_terms(u[0, c]), w, c // 2, c % 2)
            col_lines = over_lines(sums)
            col_part = stacked(col_lines)

            pl.when(away)(functools.partial(arrived, uc0, r0.at[0]))
            mine = pl.ds(pl.multiple_of(k * 2 * LANES, 2 * LANES), 2 * LANES)
            column = [uc0[q : q + 1, mine] for q in range(POLS)]
            pl.semaphore_wait(known, jnp.where(owner, 3, 4))
            send_columns(0, [col_part[:, :LANES], col_part[:, LANES:]])

            @pl.when(owner)
            def _():
                pl.semaphore_wait(rounds.at[0], 2)
                above_and_below(rounds.at[1])

            twice = []
            for q in range(POLS):
                line = 2.0 * col_lines[q] * column[q]
                twice.append(line[:, :LANES] + line[:, LANES:])
            sum_rows = placed(twice)
            left = two_terms(spread(column))

            for j in (3, 2, 1, 0):
                jh, jp = near[j]
                hh, pp = (h + jh) % 2, (p + jp) % 2
                lines = jnp.zeros((ROWS, LANES), F32)
                for t in range(LINES):
                    part = joined(
                        lax.dot_general(
                            left, w[line_rows(hh, pp, t), :], (((1,), (1,)), ((), ())),
                            preferred_element_type=F32,
                        )
                    )
                    lines = jnp.where(line_of_row == t, part, lines)
                send1[0, j, :ROWS] = lines
                send1[0, j, ROWS:] = sum_rows
                start(functools.partial(row_copy, j), None if j else jnp.logical_not(owner))

        def chip_copy(i):
            src, dst = ((w, wb), (wt, wtb))[i]
            return send(src, dst, sb.at[i], rb.at[i], dev(p, x, z, h, 1))

        def second_products():
            arrived(wb, rb.at[0])
            sums = [jnp.zeros((ROWS, 2 * LANES), F32)] * 2
            for jh, jp in near:
                hh, pp = (h + jh) % 2, (p + jp) % 2
                if (jh, jp) != (0, 0):
                    arrived(recv3.at[hh * 2 + pp], r3.at[hh * 2 + pp])
                left = two_terms(recv3[hh * 2 + pp])
                for b, block in enumerate((wb, w)):
                    sums[b] = sums[b] + columns_of(left, block, hh, pp)
            parts = [stacked(over_lines(sums[b])) for b in range(2)]
            tiles = jnp.where(row8_wide < 4, parts[0], other_rows(parts[1]))
            send_columns(1, [tiles[:, :LANES], tiles[:, LANES:]])

            @pl.when(is_home)
            def _():
                for half in range(2):
                    recvt[half] = line_tile(recv3[h * 2 + half])

            pl.when(away)(functools.partial(arrived, recvt, rt.at[0]))
            got = jnp.concatenate([recvt[0], recvt[1]], axis=1)
            lefts = [two_terms(got), two_terms(other_rows(got))]
            arrived(wtb, rb.at[1])
            for j in (3, 2, 1, 0):
                jh, jp = near[j]
                c = (h + jh) % 2 * 2 + (p + jp) % 2
                wide = joined(
                    jnp.dot(lefts[0], wtb[c], preferred_element_type=F32)
                    + jnp.dot(lefts[1], wt[c], preferred_element_type=F32)
                )
                for t in range(LINES):
                    turn[j, 8 * t : 8 * t + 8, :] = wide[:, t * LANES : (t + 1) * LANES]
                for q in range(POLS):
                    send1[1, j, LINES * q : LINES * (q + 1)] = turn[j, pl.ds(q, LINES, stride=8), :]
                if j:
                    start(functools.partial(row_copy, j))
            arrived(recvx.at[pl.ds(0, nx - 1)], rx.at[0])

        if step == 0:
            first_products()
        else:

            def only_wait():
                for c in range(4):
                    arrived(recv3.at[c], r3.at[c])
                arrived(recvx.at[pl.ds(0, nx)], rx.at[0])

            either(owner, second_products, only_wait)
            norms, alpha = first_sums()

        if step == 1:
            factor = spread(alpha)
            for c in range(4):
                u[1, c] = recv3[c] - factor * u[0, c]
        squares = jnp.zeros((ROWS, LANES), F32)
        weighted = jnp.zeros((ROWS, LANES), F32)
        for c in range(4):
            sq = u[step, c] * u[step, c]
            squares += sq
            weighted += jnp.concatenate([en[c]] * POLS, axis=0) * sq
        own_sums = placed(over_lines(squares))

        def x_copy(dx, kk, at):
            return send(
                sendx.at[at], recvx.at[at * nx + x], sx.at[0], rx.at[at],
                dev(p, (x + dx) % nx, z, h, kk),
            )

        def share(at, kk):
            for dx in (2, 1, 3):
                start(functools.partial(x_copy, dx, kk, at))
            if kk == 0:
                start(functools.partial(x_copy, 0, 0, at))
            else:
                recvx[at * nx + x] = sendx[at]

        if step == 0:
            own_sums += placed(over_lines(weighted), 4)

        if step == 0:

            @pl.when(jnp.logical_not(owner))
            def _():
                chip_copy(0).start()
                transpose()
                chip_copy(1).start()

        @pl.when(owner)
        def _(step=step, own_sums=own_sums, rows=rows):
            if step == 0:
                pl.semaphore_wait(rounds.at[1], 2)
                above_and_below(rounds.at[2])
            if step == 1:
                sendx[1] = own_sums
                share(1, 1)
                share(1, 0)
            part = pl.ds(0, rows)
            recv1[y * 2 + k if step == 0 else 8 + y, part] = send1[step, 0, part]
            members = 4 if step else 8
            arrived(recv1.at[pl.ds(step * 8, members - 1), part], r1.at[step])
            total = recv1[step * 8, part]
            for g in range(1, members):
                total += recv1[step * 8 + g, part]
            send2[step, part] = total

            @pl.when(keeper)
            def _():
                base, many = (0, 2 * nx) if step == 0 else (2 * nx, nx)
                either(
                    p == p_keep,
                    lambda: arrived(recvc.at[pl.ds(base, many - 1)], rc.at[step]),
                    lambda: arrived(recvc.at[pl.ds(base, many)], rc.at[step]),
                )
                for kk in range(2):
                    slots = [base + 2 * xx + kk if step == 0 else base + xx for xx in range(nx)]
                    cols = recvc[slots[0]]
                    for slot in slots[1:]:
                        cols += recvc[slot]
                    first = 0 if step == 0 else 4 * kk
                    for q in range(POLS):
                        at = pl.ds(LINES * q, LINES)
                        line = jnp.broadcast_to(cols[first + q : first + q + 1], (8, LANES))
                        send2[step, at] = send2[step, at] + jnp.where(row8 == zl * 2 + kk, line, 0.0)

            if step == 0:
                pl.semaphore_wait(rounds.at[2], 2)
            def z_copy(d):
                return send(
                    send2.at[step, part], recv2.at[step * nz + z, part], s2.at[step], r2.at[step],
                    dev(p, x, (z + d) % nz, h, 1),
                )

            for d in far_first:
                start(functools.partial(z_copy, d))
            recv2[step * nz + z, part] = send2[step, part]
            rest = jnp.concatenate([en[y]] * POLS, axis=0) * u[step, y]
            if step == 0:
                transpose()
            else:
                arrived(recvx.at[pl.ds(nx, nx - 1)], rx.at[1])
                coupled = send3[0] - jnp.concatenate([en[y]] * POLS, axis=0) * u[0, y]
                rest = rest - spread(alpha) * (u[1, y] + coupled) - spread(ratio_of(1)) * u[0, y]
            arrived(recv2.at[pl.ds(step * nz, nz - 1), part], r2.at[step])
            total = recv2[step * nz, part]
            for zz in range(1, nz):
                total += recv2[step * nz + zz, part]
            value = total[:ROWS] + rest

            def chunk_copy(j, kk):
                jh, jp = near[j]
                return send(
                    send3.at[step], recv3.at[step * 4 + y], s3.at[step], r3.at[step * 4 + y],
                    dev((p + jp) % 2, x, z, (h + jh) % 2, kk),
                )

            def send_chunk(j, kk):
                start(functools.partial(chunk_copy, j, kk))

            if step == 0:
                send3[0] = value
                send_chunk(3, 1)
                sendt[...] = line_tile(value)

                def tile_copy(dx):
                    return send(
                        sendt, recvt.at[p], st.at[0], rt.at[0], dev(p_keep, (x + dx) % nx, z, h, 1)
                    )

                for dx in (2, 1, 3):
                    start(functools.partial(tile_copy, dx), keeper)
                send_chunk(2, 1)
                send_chunk(1, 1)
                sendx[0] = jnp.concatenate([total[ROWS + 4 :], total[ROWS : ROWS + 4]], axis=0) + own_sums
                share(0, 1)
                for j in (3, 2, 1, 0):
                    send_chunk(j, 0)
                share(0, 0)
            else:
                sendn[...] = placed(over_lines(value * value)) + placed(over_lines(value * u[1, y]), 4)

                def sums_copy(dx, j, kk):
                    jh, jp = near[j]
                    return send(
                        sendn, recvn.at[x * 4 + y], sn.at[kk], rn.at[0],
                        dev((p + jp) % 2, (x + dx) % nx, z, (h + jh) % 2, kk),
                    )

                for dx in (2, 1, 3, 0):
                    for j in (3, 2, 1, 0):
                        for kk in range(2):
                            if (dx, j, kk) != (0, 0, 1):
                                start(functools.partial(sums_copy, dx, j, kk))
                recvn[x * 4 + y] = sendn[...]
                send3[1] = value

            if step == 1:
                for j in (3, 2, 1, 0):
                    send_chunk(j, 0)
                    if j:
                        send_chunk(j, 1)
            recv3[step * 4 + y] = send3[step]

        def ratio_of(at):
            whole = recvx[at * nx]
            for xx in range(1, nx):
                whole += recvx[at * nx + xx]
            whole = jnp.broadcast_to(jnp.sum(whole, axis=1, keepdims=True), (8, LANES))
            return [whole[q : q + 1] / norms[q] for q in range(POLS)]

    @pl.when(jnp.logical_not(owner))
    def _():
        arrived(recvx.at[pl.ds(nx, nx)], rx.at[1])

    ratio = ratio_of(1)
    norm1 = [ratio[q] * norms[q] for q in range(POLS)]
    either(
        owner,
        lambda: arrived(recvn.at[pl.ds(0, 4 * nx - 1)], rn.at[0]),
        lambda: arrived(recvn.at[pl.ds(0, 4 * nx)], rn.at[0]),
    )
    whole = recvn[0]
    for c in range(1, 4 * nx):
        whole += recvn[c]
    whole = jnp.broadcast_to(jnp.sum(whole, axis=1, keepdims=True), (8, LANES))
    shift = [whole[4 + q : 5 + q] / norm1[q] for q in range(POLS)]
    norm2 = [whole[q : q + 1] - shift[q] * whole[4 + q : 5 + q] for q in range(POLS)]
    inverse = spread([1.0 / jnp.sqrt(t) for t in norm2])
    back = spread(shift)
    for jh, jp in near:
        c = (h + jh) % 2 * 2 + (p + jp) % 2
        hear = functools.partial(arrived, recv3.at[4 + c], r3.at[4 + c])
        if (jh, jp) == (0, 0):
            pl.when(jnp.logical_not(owner))(hear)
        else:
            hear()
    for c in range(4):
        value = (recv3[4 + c] - back * u[1, c]) * inverse
        for q in range(POLS):
            for t in range(LINES):
                at = ((t // 2) * 8 + (c // 2) * 4 + (t % 2) * 2 + c % 2) * LANES
                last_ref[q : q + 1, at : at + LANES] = value[LINES * q + t : LINES * q + t + 1, :]
    for q in range(POLS):
        alpha_ref[0:1, q : q + 1] = alpha[q][:, :1]
        alpha_ref[1:2, q : q + 1] = (alpha[q] + shift[q])[:, :1]
        beta_ref[0:1, q : q + 1] = jnp.sqrt(ratio[q])[:, :1]
        beta_ref[1:2, q : q + 1] = jnp.sqrt(norm2[q] / norm1[q])[:, :1]
    finish()


def write_out(*refs):
    sources, targets, sems = refs[:3], refs[3:6], refs[6]
    copies = [pltpu.make_async_copy(a, b, sems.at[i]) for i, (a, b) in enumerate(zip(sources, targets, strict=True))]
    for c in copies:
        c.start()
    for c in copies:
        c.wait()


def lanczos(sizes, kernel_half, dipole, band_energy, core_energy, core_index):
    nx, nz, _ = sizes
    rows, cols = kernel_half.shape
    dma = pltpu.SemaphoreType.DMA
    chunk = (ROWS, LANES)
    longer = (ROWS + 8, LANES)
    tile = (8, LANES)
    results = pl.pallas_call(
        functools.partial(kernel, sizes),
        out_shape=(pltpu.VMEM((2, POLS), F32), pltpu.VMEM((2, POLS), F32), pltpu.VMEM(dipole.shape, F32)),
        in_specs=[pl.BlockSpec(memory_space=pl.ANY)] * 5,
        out_specs=[pl.BlockSpec(memory_space=pltpu.VMEM)] * 3,
        scratch_shapes=[
            pltpu.VMEM((rows, cols), BF),
            pltpu.VMEM((4, cols, LINES * LANES), BF),
            pltpu.VMEM((rows, cols), BF),
            pltpu.VMEM((4, cols, LINES * LANES), BF),
            pltpu.VMEM((4, 8 * LINES, LANES), F32),
            pltpu.VMEM(dipole.shape, F32),
            pltpu.VMEM(band_energy.shape, F32),
            pltpu.SMEM(core_energy.shape, F32),
            pltpu.SMEM(core_index.shape, jnp.int32),
            pltpu.VMEM((POLS, 2 * cols), F32),
            pltpu.VMEM((2, 4, *chunk), F32),
            pltpu.VMEM((4, *tile), F32),
            pltpu.VMEM((2, 4, *longer), F32),
            pltpu.VMEM((2 * 8, *longer), F32),
            pltpu.VMEM((2, 2, *tile), F32),
            pltpu.VMEM((2 * nx * 2, *tile), F32),
            pltpu.VMEM((2, *longer), F32),
            pltpu.VMEM((2 * nz, *longer), F32),
            pltpu.VMEM((2, *chunk), F32),
            pltpu.VMEM((2 * 4, *chunk), F32),
            pltpu.VMEM(tile, F32),
            pltpu.VMEM((2, *tile), F32),
            pltpu.VMEM((2, *tile), F32),
            pltpu.VMEM((2 * nx, *tile), F32),
            pltpu.VMEM(tile, F32),
            pltpu.VMEM((nx * 4, *tile), F32),
            dma((3,)), dma((2,)),
            dma((1,)), dma((1,)),
            dma((2,)), dma((2,)),
            dma((1,)), dma((2,)),
            dma((2,)), dma((2,)),
            dma((2,)), dma((8,)),
            dma((1,)), dma((1,)),
            dma((1,)), dma((2,)),
            dma((2,)), dma((1,)),
            pltpu.SemaphoreType.REGULAR, pltpu.SemaphoreType.REGULAR((3,)),
            dma((2,)), dma((2,)),
        ],
        compiler_params=pltpu.CompilerParams(collective_id=0, has_side_effects=True),
    )(kernel_half, dipole, band_energy, core_energy, core_index)
    alphas, betas, last = pl.pallas_call(
        write_out,
        out_shape=(
            jax.ShapeDtypeStruct((2, POLS), F32),
            jax.ShapeDtypeStruct((2, POLS), F32),
            jax.ShapeDtypeStruct(dipole.shape, F32),
        ),
        in_specs=[pl.BlockSpec(memory_space=pltpu.VMEM)] * 3,
        out_specs=[pl.BlockSpec(memory_space=pl.ANY)] * 3,
        scratch_shapes=[dma((3,))],
    )(*[pltpu.with_memory_space_constraint(r, pltpu.VMEM) for r in results])
    return alphas.T, betas.T, last


def solution(mesh):
    nx, np_, nz = mesh.shape["row"], mesh.shape["pol"], mesh.shape["col"] // 4
    sizes = (nx, nz, nz * np_ // nx)
    in_specs = (P("row", ("pol", "col")), P(None, "row"), P("row", None), P(), P("row"))
    out_specs = (P(), P(), P(None, "row"))
    return jax.shard_map(
        functools.partial(lanczos, sizes), mesh=mesh, in_specs=in_specs, out_specs=out_specs, check_vma=False
    )
```
